32 devices in a mesh: batch: 8 (over z, y), expert: 4 (over x, core).
Axes of the slice: x: 2, y: 2, z: 4, core: 2. Of those that a mesh axis runs over, the one named last changes fastest.
Arguments:
- tokens: bfloat16 [32768, 768], P(('batch', 'expert')), may hold values from -6 to 6
- condition: bfloat16 [128, 768], P(('batch', 'expert')), may hold values from -6 to 6
- lengths: int32 [128], P(('batch', 'expert')), may hold values from 32 to 256, as said below
- routes: int32 [32768, 2], P(('batch', 'expert')), may hold values from 0 to 7, all different within a row
- cotangent: bfloat16 [32768, 768], P(('batch', 'expert')), may hold values from -6 to 6
- ada_weight: bfloat16 [768, 4608], replicated, may hold values from -0.21875 to 0.21875
- qkv_weight: bfloat16 [768, 2304], replicated, may hold values from -0.21875 to 0.21875
- out_weight: bfloat16 [768, 768], replicated, may hold values from -0.875 to 0.875
- router_weight: bfloat16 [768, 8], replicated, may hold values from -0.15625 to 0.15625
- shared_in: bfloat16 [768, 3072], replicated, may hold values from -0.21875 to 0.21875
- shared_out: bfloat16 [3072, 768], replicated, may hold values from -0.109375 to 0.109375
- expert_in: bfloat16 [8, 768, 3072], P('expert'), may hold values from -0.21875 to 0.21875
- expert_out: bfloat16 [8, 3072, 768], P('expert'), may hold values from -0.109375 to 0.109375
Outputs:
- out: bfloat16 [32768, 768], P(('batch', 'expert'))
- grad_tokens: float32 [32768, 768], P(('batch', 'expert'))
- grad_ada: float32 [768, 4608], P('batch', 'expert')
- grad_qkv: float32 [768, 2304], P('batch', 'expert')
- grad_out_proj: float32 [768, 768], P('batch', 'expert')
- grad_router: float32 [768, 8], P('batch', 'expert')
- grad_shared_in: float32 [768, 3072], P('batch', 'expert')
- grad_shared_out: float32 [3072, 768], P('batch', 'expert')
- grad_expert_in: float32 [8, 768, 3072], P('expert', 'batch')
- grad_expert_out: float32 [8, 3072, 768], P('expert', 'batch')
The draws below stay inside these ranges and needn't reach their ends.
Inputs may be any that keep to these rules, and one draw needn't show every extreme that they name: `lengths`: the live patches of an item come first, the rest are padding. Item 0 is full.
All inputs are finite; a program needn't handle non-finite values.
Results may differ from the reference program's by a relative error of at most 0.014.
The reference program's roundings to bfloat16 on the way count: a program that leaves them out, or rounds other values in their place, can miss the bound.
Values may be sent and summed in bfloat16 or wider, within the bound.
A program may use at most 320 MiB of HBM per device.

```python
import math
import jax
import jax.numpy as jnp
from jax import lax

D = 768
HEADS = 12
HEAD_DIM = 64
FF = 3072
EXPERTS = 8
SEQ = 256
TOK_DEV = 1024
CAP = 256
ITEMS = 128
TOKENS = 32768
DEVICES = 32


def draw_lengths(key, part):
    picked = jax.random.randint(key, (ITEMS,), SEQ // 8, SEQ + 1, dtype=jnp.int32)
    return picked.at[0].set(SEQ)


def levels(stream_key, dims, cuts, smallest, top_value):
    level = 1.0
    for dim, blocks in cuts:
        draws = jax.random.uniform(jax.random.fold_in(jax.random.fold_in(stream_key, 6), dim), (blocks,), jnp.float32, smallest / len(cuts), top_value / len(cuts))
        level = level * jnp.repeat(jnp.exp(draws), dims[dim] // blocks).reshape((-1,) + (1,) * (len(dims) - 1 - dim))
    return level


def choose_distinct(stream_key, rows, number_of, top, lift):
    sequence = jax.random.permutation(jax.random.fold_in(stream_key, 1), number_of)
    boost = sequence
    for power in range(3):
        boost = boost * boost // number_of
    boost = boost * lift // number_of
    tickets = jax.random.randint(jax.random.fold_in(stream_key, 2), (rows, number_of), 0, 4096) + boost
    sure = jax.random.permutation(jax.random.fold_in(stream_key, 3), rows)[jnp.arange(number_of) % rows]
    tickets = jnp.where(jnp.arange(rows)[:, None] == sure[None, :], 1 << 14, tickets)
    priority = tickets * number_of + jnp.arange(number_of)
    return lax.top_k(priority.astype(jnp.int32), top)[1].astype(jnp.int32)


def gaussian(key, extent, deviation, reach, pieces=(), held_as=jnp.bfloat16):
    loudness = levels(key, extent, pieces, -0.22, 0.18) if pieces else 1.0
    values = jax.random.normal(key, extent, jnp.float32) * deviation * loudness
    return jnp.minimum(jnp.maximum(values, -reach), reach).astype(held_as)


def setup_inputs(seed: int = 0) -> dict:
    splits = jax.random.split(jax.random.key(seed), 14)
    return {
        "tokens": gaussian(splits[0], (TOKENS, D), 1.0, 6.0, ((0, 32),)),
        "condition": gaussian(splits[1], (ITEMS, D), 1.0, 6.0, ((0, 32),)),
        "lengths": draw_lengths(jax.random.fold_in(splits[13], 71), 0),
        "routes": choose_distinct(splits[3], TOKENS, EXPERTS, 2, 2048),
        "cotangent": gaussian(splits[4], (TOKENS, D), 1.0, 6.0, ((0, 32),)),
        "ada_weight": gaussian(splits[5], (D, 6 * D), D ** -0.5, 0.21875),
        "qkv_weight": gaussian(splits[6], (D, 3 * D), D ** -0.5, 0.21875),
        "out_weight": gaussian(splits[7], (D, D), (D // 16) ** -0.5, 0.875),
        "router_weight": gaussian(splits[8], (D, EXPERTS), 0.025, 0.15625),
        "shared_in": gaussian(splits[9], (D, FF), D ** -0.5, 0.21875),
        "shared_out": gaussian(splits[10], (FF, D), FF ** -0.5, 0.109375),
        "expert_in": gaussian(splits[11], (EXPERTS, D, FF), D ** -0.5, 0.21875, ((0, 4),)),
        "expert_out": gaussian(splits[12], (EXPERTS, FF, D), FF ** -0.5, 0.109375, ((0, 4),)),
    }


GELU_C = 0.7978845608028654
GELU_A = 0.044715
EPSILON = 1e-06
MASKED = -1000000000.0

@jax.custom_vjp
def low(v):
    return lax.optimization_barrier(v.astype(jnp.bfloat16)).astype(jnp.float32)

@jax.custom_vjp
def low_back(v):
    return v

def low_keep(v):
    return (low(v), None)

def low_pass(kept, grad):
    return (grad,)

def back_keep(v):
    return (v, None)

def back_low(kept, grad):
    return (low(grad),)
low.defvjp(low_keep, low_pass)
low_back.defvjp(back_keep, back_low)

def gelu_tanh(values):
    inside_arg = GELU_C * (values + GELU_A * values * values * values)
    return 0.5 * values * (1.0 + jnp.tanh(inside_arg))

def normalize_rows(values):
    centre = values - lax.optimization_barrier(jnp.mean(values, -1, keepdims=True))
    return centre * lax.rsqrt(lax.optimization_barrier(jnp.mean(centre * centre, -1, keepdims=True)) + EPSILON)

def attend_block(operands):
    qkv_block, live_block = operands
    raw_scores = jnp.einsum('gqhd,gkhd->ghqk', qkv_block[:, :, 0], qkv_block[:, :, 1], precision=lax.Precision.HIGHEST) * HEAD_DIM ** (-0.5)
    scored = jnp.where(live_block[:, None, None, :], low_back(raw_scores), MASKED)
    weights_low = low(jax.nn.softmax(scored, -1))
    return jnp.einsum('ghqk,gkhd->gqhd', weights_low, qkv_block[:, :, 2], precision=lax.Precision.HIGHEST)

def expert_block(operands):
    rows_in, first_mat, second_mat = operands
    expert_pre = low_back(jnp.dot(rows_in, first_mat, precision=lax.Precision.HIGHEST))
    return low(low_back(jnp.dot(low(gelu_tanh(expert_pre)), second_mat, precision=lax.Precision.HIGHEST)))

def reference(tokens, condition, lengths, routes, cotangent, ada_weight, qkv_weight, out_weight, router_weight, shared_in, shared_out, expert_in, expert_out):
    live_mask = jnp.arange(SEQ)[None, :] < lengths[:, None]
    live_flat = live_mask.reshape(TOKENS)
    cond_act = low(jax.nn.silu(condition.astype(jnp.float32)))
    expert_ids = jnp.arange(EXPERTS)
    route_float = (routes[:, :, None] == expert_ids).astype(jnp.float32)
    route_hot = (routes[:, :, None] == expert_ids).astype(jnp.int32) * live_flat[:, None, None].astype(jnp.int32)
    per_device = route_hot.reshape(DEVICES, TOK_DEV * 2, EXPERTS)
    earlier = jnp.cumsum(per_device, axis=1) - per_device
    position = lax.optimization_barrier(jnp.sum(earlier * per_device, -1)).reshape(TOKENS, 2)
    kept_pair = live_flat[:, None] & (position < CAP)
    device_of = (jnp.arange(TOKENS, dtype=jnp.int32) // TOK_DEV)[:, None]
    slot_index = (routes * DEVICES + device_of) * CAP + position
    slot_total = EXPERTS * DEVICES * CAP
    target = jnp.where(kept_pair, slot_index, slot_total).reshape(TOKENS * 2).astype(jnp.int32)
    slot_pair = jnp.zeros(slot_total, jnp.int32).at[target].set(jnp.arange(TOKENS * 2, dtype=jnp.int32), mode='drop')
    filled = jnp.zeros(slot_total, jnp.float32).at[target].set(1.0, mode='drop')
    slot_token = slot_pair // 2
    safe_slot = jnp.where(kept_pair, slot_index, 0).astype(jnp.int32)
    kept_float = kept_pair.astype(jnp.float32)
    group_size = math.gcd(ITEMS, max(1, 4096 // SEQ))
    live_blocks = live_mask.reshape(ITEMS // group_size, group_size, SEQ)

    def forward(block_input, ada_mat, qkv_mat, out_mat, router_mat, first_mat, second_mat, expert_first, expert_second):
        modulation = jnp.dot(cond_act, ada_mat, precision=lax.Precision.HIGHEST).reshape(ITEMS, 6, 1, D)
        shift_attn, scale_attn, gate_attn, shift_mlp, scale_mlp, gate_mlp = [modulation[:, index_col] for index_col in range(6)]
        input_items = block_input.reshape(ITEMS, SEQ, D)
        h_attn = low(normalize_rows(input_items) * (1.0 + scale_attn) + shift_attn).reshape(TOKENS, D)
        qkv_all = low(low_back(jnp.dot(h_attn, qkv_mat, precision=lax.Precision.HIGHEST)))
        qkv_blocks = qkv_all.reshape(ITEMS // group_size, group_size, SEQ, 3, HEADS, HEAD_DIM)
        heads_out = lax.map(jax.checkpoint(attend_block), (qkv_blocks, live_blocks))
        heads_low = low(low_back(heads_out.reshape(TOKENS, D)))
        attn_out = low_back(jnp.dot(heads_low, out_mat, precision=lax.Precision.HIGHEST)).reshape(ITEMS, SEQ, D)
        x_mid = input_items + gate_attn * attn_out
        h_mlp = low(normalize_rows(x_mid) * (1.0 + scale_mlp) + shift_mlp).reshape(TOKENS, D)
        shared_pre = low_back(jnp.dot(h_mlp, first_mat, precision=lax.Precision.HIGHEST))
        shared_res = low_back(jnp.dot(low(gelu_tanh(shared_pre)), second_mat, precision=lax.Precision.HIGHEST))
        logits = jnp.dot(h_mlp, router_mat, precision=lax.Precision.HIGHEST)
        gate_weights = jax.nn.softmax(lax.optimization_barrier(jnp.sum(route_float * logits[:, None, :], -1)), -1)
        send_rows = (low_back(h_mlp[slot_token]) * filled[:, None]).reshape(EXPERTS, DEVICES * CAP, D)
        expert_rows = lax.map(jax.checkpoint(expert_block), (send_rows, expert_first, expert_second)).reshape(slot_total, D)
        pair_rows = expert_rows[safe_slot] * kept_float[:, :, None]
        moe_out = lax.optimization_barrier(jnp.sum(gate_weights[:, :, None] * pair_rows, 1))
        mlp_out = (shared_res + moe_out).reshape(ITEMS, SEQ, D)
        return (x_mid + gate_mlp * mlp_out).reshape(TOKENS, D)
    result, pullback = jax.vjp(forward, tokens.astype(jnp.float32), ada_weight.astype(jnp.float32), qkv_weight.astype(jnp.float32), out_weight.astype(jnp.float32), router_weight.astype(jnp.float32), shared_in.astype(jnp.float32), shared_out.astype(jnp.float32), expert_in.astype(jnp.float32), expert_out.astype(jnp.float32))
    gradients = pullback(cotangent.astype(jnp.float32))
    return (result.astype(jnp.bfloat16), gradients[0], gradients[1], gradients[2], gradients[3], gradients[4], gradients[5], gradients[6], gradients[7], gradients[8])
```

```python
import jax
import jax.numpy as jnp
from jax import lax
from jax.sharding import PartitionSpec as P

D = 768
HEADS = 12
HEAD_DIM = 64
EXPERTS = 8
SEQ = 256
CAP = 256


GELU_C = 0.7978845608028654
GELU_A = 0.044715
EPSILON = 1e-06
MASKED = -1000000000.0


def gelu_tanh(values):
    inside_arg = GELU_C * (values + GELU_A * values * values * values)
    return 0.5 * values * (1.0 + jnp.tanh(inside_arg))


def gelu_slope(values):
    tangent = jnp.tanh(GELU_C * (values + GELU_A * values * values * values))
    return 0.5 * (1.0 + tangent) + 0.5 * values * (1.0 - tangent * tangent) * GELU_C * (
        1.0 + 3.0 * GELU_A * values * values
    )


def normalize(values):
    centre = values - jnp.mean(values, -1, keepdims=True)
    factor = lax.rsqrt(jnp.mean(centre * centre, -1, keepdims=True) + EPSILON)
    return (centre * factor, factor)


def norm_back(grad_norm, normed, factor):
    return factor * (
        grad_norm
        - jnp.mean(grad_norm, -1, keepdims=True)
        - normed * jnp.mean(grad_norm * normed, -1, keepdims=True)
    )


def attention_scores(queries, keys_all, key_mask, scale_qk):
    raw_scores = (
        jnp.einsum("iqhd,ikhd->ihqk", queries, keys_all, preferred_element_type=jnp.float32)
        * scale_qk
    )
    return jnp.where(key_mask, raw_scores, MASKED)


def axis_split(size):
    inner = 2 if size <= 8 else 8
    return (size // inner, inner)


def group_sum(blocks, axis, groups):
    width = len(groups[0])
    if width == 1:
        return blocks[0].astype(jnp.float32)
    low = blocks.astype(jnp.bfloat16)
    if width == 2:
        pairs = [(g[0], g[1]) for g in groups] + [(g[1], g[0]) for g in groups]
        place = jnp.zeros((), jnp.int32)
        index = lax.axis_index(axis)
        for g in groups:
            place = jnp.where(index == g[1], 1, place)
        sent = lax.dynamic_index_in_dim(low, 1 - place, 0, keepdims=False)
        kept = lax.dynamic_index_in_dim(low, place, 0, keepdims=False)
        got = lax.ppermute(sent, axis, pairs)
        return kept.astype(jnp.float32) + got.astype(jnp.float32)
    got = lax.all_to_all(low, axis, 0, 0, tiled=True, axis_index_groups=groups)
    return jnp.sum(got.astype(jnp.float32), 0)


def inner_groups(outer, inner):
    return [[o * inner + i for i in range(inner)] for o in range(outer)]


def outer_groups(outer, inner):
    return [[o * inner + i for o in range(outer)] for i in range(inner)]


def reduce_batch(blocks):
    size = lax.axis_size("batch")
    outer, inner = axis_split(size)
    rest = blocks.shape[1:]
    v = jnp.moveaxis(blocks.reshape((outer, inner) + rest), 1, 0)
    v = group_sum(v, "batch", inner_groups(outer, inner))
    return group_sum(v, "batch", outer_groups(outer, inner))


def reduce_expert(blocks):
    size = lax.axis_size("expert")
    outer, inner = size // 2, 2
    rest = blocks.shape[1:]
    v = jnp.moveaxis(blocks.reshape((outer, inner) + rest), 1, 0)
    v = group_sum(v, "expert", inner_groups(outer, inner))
    return group_sum(v, "expert", outer_groups(outer, inner))


def reduce_dense(grad):
    nb, ne = lax.axis_size("batch"), lax.axis_size("expert")
    r, c = grad.shape
    v = jnp.transpose(grad.astype(jnp.bfloat16).reshape(r, ne, c // ne), (1, 0, 2))
    v = reduce_expert(v)
    return reduce_batch(v.reshape(nb, r // nb, c // ne))


def reduce_local(grad):
    nb = lax.axis_size("batch")
    n, r, c = grad.shape
    v = jnp.transpose(grad.astype(jnp.bfloat16).reshape(n, nb, r // nb, c), (1, 0, 2, 3))
    return reduce_batch(v)


def per_device(
    tokens,
    condition,
    lengths,
    routes,
    cotangent,
    ada_weight,
    qkv_weight,
    out_weight,
    router_weight,
    shared_in,
    shared_out,
    expert_in,
    expert_out,
):
    groups = lax.axis_size("expert")
    local_experts = expert_in.shape[0]
    item_count = lengths.shape[0]
    token_count = tokens.shape[0]
    scale_qk = HEAD_DIM ** (-0.5)
    live_mask = jnp.arange(SEQ)[None, :] < lengths[:, None]
    live_flat = live_mask.reshape(token_count)
    key_mask = live_mask[:, None, None, :]
    cond_act = jax.nn.silu(condition.astype(jnp.float32)).astype(jnp.bfloat16)
    modulation = jnp.dot(cond_act, ada_weight, preferred_element_type=jnp.float32).reshape(
        item_count, 6, 1, D
    )
    shift_attn, scale_attn, gate_attn, shift_mlp, scale_mlp, gate_mlp = [
        modulation[:, index_col] for index_col in range(6)
    ]
    expert_ids = jnp.arange(EXPERTS)
    route_float = (routes[:, :, None] == expert_ids).astype(jnp.float32)
    route_hot = (routes[:, :, None] == expert_ids).astype(jnp.int32) * live_flat[
        :, None, None
    ].astype(jnp.int32)
    flat_hot = route_hot.reshape(token_count * 2, EXPERTS)
    earlier = jnp.cumsum(flat_hot, axis=0) - flat_hot
    position = jnp.sum(earlier * flat_hot, -1).reshape(token_count, 2)
    kept_pair = live_flat[:, None] & (position < CAP)
    slot_index = routes * CAP + position
    slot_total = EXPERTS * CAP
    target = jnp.where(kept_pair, slot_index, slot_total).reshape(token_count * 2)
    slot_pair = (
        jnp.zeros(slot_total, jnp.int32)
        .at[target]
        .set(jnp.arange(token_count * 2, dtype=jnp.int32), mode="drop")
    )
    filled_low = (
        jnp.zeros(slot_total, jnp.float32)
        .at[target]
        .set(1.0, mode="drop")
        .astype(jnp.bfloat16)[:, None]
    )
    slot_token = slot_pair // 2
    safe_slot = jnp.where(kept_pair, slot_index, 0)
    kept_float = kept_pair.astype(jnp.float32)
    input_items = tokens.astype(jnp.float32).reshape(item_count, SEQ, D)
    normed_attn, factor_attn = normalize(input_items)
    h_attn = (
        (normed_attn * (1.0 + scale_attn) + shift_attn).astype(jnp.bfloat16).reshape(token_count, D)
    )
    qkv_all = (
        jnp.dot(h_attn, qkv_weight, preferred_element_type=jnp.float32)
        .astype(jnp.bfloat16)
        .reshape(item_count, SEQ, 3, HEADS, HEAD_DIM)
    )
    queries = qkv_all[:, :, 0]
    keys_all = qkv_all[:, :, 1]
    values_all = qkv_all[:, :, 2]
    scores = attention_scores(queries, keys_all, key_mask, scale_qk)
    peak = jnp.max(scores, -1, keepdims=True)
    log_total = peak + jnp.log(jnp.sum(jnp.exp(scores - peak), -1, keepdims=True))
    probabilities = jnp.exp(scores - log_total)
    heads_out = jnp.einsum(
        "ihqk,ikhd->iqhd",
        probabilities.astype(jnp.bfloat16),
        values_all,
        preferred_element_type=jnp.float32,
    )
    heads_low = heads_out.astype(jnp.bfloat16).reshape(token_count, D)
    attn_out = jnp.dot(heads_low, out_weight, preferred_element_type=jnp.float32).reshape(
        item_count, SEQ, D
    )
    x_mid = input_items + gate_attn * attn_out
    normed_mlp, factor_mlp = normalize(x_mid)
    h_mlp = (
        (normed_mlp * (1.0 + scale_mlp) + shift_mlp).astype(jnp.bfloat16).reshape(token_count, D)
    )
    shared_pre = jnp.dot(h_mlp, shared_in, preferred_element_type=jnp.float32)
    shared_act = gelu_tanh(shared_pre).astype(jnp.bfloat16)
    shared_res = jnp.dot(shared_act, shared_out, preferred_element_type=jnp.float32)
    logits = jnp.dot(h_mlp, router_weight, preferred_element_type=jnp.float32)
    gate_weights = jax.nn.softmax(jnp.sum(route_float * logits[:, None, :], -1), -1)
    send_rows = (h_mlp[slot_token] * filled_low).reshape(groups, local_experts, CAP, D)
    received = lax.all_to_all(send_rows, "expert", split_axis=0, concat_axis=0, tiled=True)
    expert_pre = jnp.einsum(
        "sjcd,jdf->sjcf", received, expert_in, preferred_element_type=jnp.float32
    )
    expert_act = gelu_tanh(expert_pre).astype(jnp.bfloat16)
    expert_rows = jnp.einsum(
        "sjcf,jfd->sjcd", expert_act, expert_out, preferred_element_type=jnp.float32
    ).astype(jnp.bfloat16)
    outputs = (expert_rows, expert_pre, received)
    expert_rows = outputs[0]
    rows_in = outputs[-1]
    returned = lax.all_to_all(
        expert_rows, "expert", split_axis=0, concat_axis=0, tiled=True
    ).reshape(slot_total, D)
    pair_rows = returned[safe_slot].astype(jnp.float32) * kept_float[:, :, None]
    moe_out = jnp.sum(gate_weights[:, :, None] * pair_rows, 1)
    mlp_out = (shared_res + moe_out).reshape(item_count, SEQ, D)
    result = (x_mid + gate_mlp * mlp_out).reshape(token_count, D).astype(jnp.bfloat16)
    grad_y = cotangent.astype(jnp.float32).reshape(item_count, SEQ, D)
    grad_gate_mlp = jnp.sum(grad_y * mlp_out, 1)
    grad_mlp = (gate_mlp * grad_y).reshape(token_count, D)
    g_shared = grad_mlp.astype(jnp.bfloat16)
    grad_w_sh2 = jnp.einsum("tf,td->fd", shared_act, g_shared, preferred_element_type=jnp.float32)
    g_pre = (
        jnp.einsum("td,fd->tf", g_shared, shared_out, preferred_element_type=jnp.float32)
        * gelu_slope(shared_pre)
    ).astype(jnp.bfloat16)
    grad_w_sh1 = jnp.einsum("td,tf->df", h_mlp, g_pre, preferred_element_type=jnp.float32)
    grad_h = jnp.einsum("tf,df->td", g_pre, shared_in, preferred_element_type=jnp.float32)
    g_gate = jnp.sum(grad_mlp[:, None, :] * pair_rows, -1)
    g_row = (
        (gate_weights[:, :, None] * kept_float[:, :, None] * grad_mlp[:, None, :])
        .astype(jnp.bfloat16)
        .reshape(token_count * 2, D)
    )
    send_grad = (g_row[slot_pair] * filled_low).reshape(groups, local_experts, CAP, D)
    grad_rows = lax.all_to_all(send_grad, "expert", split_axis=0, concat_axis=0, tiled=True)
    expert_pre = outputs[1]
    expert_act = gelu_tanh(expert_pre).astype(jnp.bfloat16)
    grad_w_e2 = jnp.einsum(
        "sjcf,sjcd->jfd", expert_act, grad_rows, preferred_element_type=jnp.float32
    )
    g_epre = (
        jnp.einsum("sjcd,jfd->sjcf", grad_rows, expert_out, preferred_element_type=jnp.float32)
        * gelu_slope(expert_pre)
    ).astype(jnp.bfloat16)
    grad_w_e1 = jnp.einsum("sjcd,sjcf->jdf", rows_in, g_epre, preferred_element_type=jnp.float32)
    g_in = jnp.einsum(
        "sjcf,jdf->sjcd", g_epre, expert_in, preferred_element_type=jnp.float32
    ).astype(jnp.bfloat16)
    grad_back = lax.all_to_all(g_in, "expert", split_axis=0, concat_axis=0, tiled=True).reshape(
        slot_total, D
    )
    grad_h = grad_h + jnp.sum(grad_back[safe_slot].astype(jnp.float32) * kept_float[:, :, None], 1)
    weighted = jnp.sum(gate_weights * g_gate, -1, keepdims=True)
    g_sel = gate_weights * (g_gate - weighted)
    grad_logits = jnp.sum(route_float * g_sel[:, :, None], 1)
    grad_w_router = jnp.dot(
        h_mlp.astype(jnp.float32).T, grad_logits, precision=lax.Precision.HIGHEST
    )
    grad_h = grad_h + jnp.dot(
        grad_logits, router_weight.astype(jnp.float32).T, precision=lax.Precision.HIGHEST
    )
    grad_h_items = grad_h.reshape(item_count, SEQ, D)
    grad_shift_mlp = jnp.sum(grad_h_items, 1)
    grad_scale_mlp = jnp.sum(grad_h_items * normed_mlp, 1)
    grad_mid = grad_y + norm_back(grad_h_items * (1.0 + scale_mlp), normed_mlp, factor_mlp)
    grad_gate_attn = jnp.sum(grad_mid * attn_out, 1)
    g_attn = (gate_attn * grad_mid).astype(jnp.bfloat16).reshape(token_count, D)
    grad_w_out = jnp.einsum("td,te->de", heads_low, g_attn, preferred_element_type=jnp.float32)
    g_heads = (
        jnp.einsum("te,de->td", g_attn, out_weight, preferred_element_type=jnp.float32)
        .astype(jnp.bfloat16)
        .reshape(item_count, SEQ, HEADS, HEAD_DIM)
    )
    scores_again = attention_scores(queries, keys_all, key_mask, scale_qk)
    probs_again = jnp.exp(scores_again - log_total)
    grad_values = jnp.einsum(
        "ihqk,iqhd->ikhd",
        probs_again.astype(jnp.bfloat16),
        g_heads,
        preferred_element_type=jnp.float32,
    )
    g_probs = jnp.einsum("iqhd,ikhd->ihqk", g_heads, values_all, preferred_element_type=jnp.float32)
    g_scores = (probs_again * (g_probs - jnp.sum(probs_again * g_probs, -1, keepdims=True))).astype(
        jnp.bfloat16
    )
    grad_queries = (
        jnp.einsum("ihqk,ikhd->iqhd", g_scores, keys_all, preferred_element_type=jnp.float32)
        * scale_qk
    )
    grad_keys = (
        jnp.einsum("ihqk,iqhd->ikhd", g_scores, queries, preferred_element_type=jnp.float32)
        * scale_qk
    )
    g_qkv = (
        jnp.stack([grad_queries, grad_keys, grad_values], 2)
        .astype(jnp.bfloat16)
        .reshape(token_count, 3 * D)
    )
    grad_w_qkv = jnp.einsum("td,te->de", h_attn, g_qkv, preferred_element_type=jnp.float32)
    g_h_attn = jnp.einsum(
        "te,de->td", g_qkv, qkv_weight, preferred_element_type=jnp.float32
    ).reshape(item_count, SEQ, D)
    grad_shift_attn = jnp.sum(g_h_attn, 1)
    grad_scale_attn = jnp.sum(g_h_attn * normed_attn, 1)
    grad_input = grad_mid + norm_back(g_h_attn * (1.0 + scale_attn), normed_attn, factor_attn)
    grad_mod = jnp.stack(
        [
            grad_shift_attn,
            grad_scale_attn,
            grad_gate_attn,
            grad_shift_mlp,
            grad_scale_mlp,
            grad_gate_mlp,
        ],
        1,
    ).reshape(item_count, 6 * D)
    nb = lax.axis_size("batch")
    ada_cols = grad_mod.shape[1] // groups
    mod_parts = jnp.transpose(grad_mod.reshape(item_count, groups, ada_cols), (1, 0, 2))
    mod_mine = lax.all_to_all(mod_parts, "expert", 0, 0, tiled=True).reshape(
        groups * item_count, ada_cols
    )
    mod_all = lax.all_gather(mod_mine, "batch", axis=0, tiled=True)
    act_all = lax.all_gather(cond_act, ("batch", "expert"), axis=0, tiled=True)
    ada_rows = D // nb
    act_mine = lax.dynamic_slice_in_dim(act_all, lax.axis_index("batch") * ada_rows, ada_rows, 1)
    grad_ada = jnp.dot(
        act_mine.astype(jnp.float32).T, mod_all, precision=lax.Precision.HIGHEST
    )
    reduced = (
        grad_ada,
        reduce_dense(grad_w_qkv),
        reduce_dense(grad_w_out),
        lax.psum_scatter(
            lax.psum_scatter(grad_w_router, "batch", scatter_dimension=0, tiled=True),
            "expert",
            scatter_dimension=1,
            tiled=True,
        ),
        reduce_dense(grad_w_sh1),
        reduce_dense(grad_w_sh2),
    )
    expert_sums = (reduce_local(grad_w_e1), reduce_local(grad_w_e2))
    return (
        result,
        grad_input.reshape(token_count, D),
        reduced[0],
        reduced[1],
        reduced[2],
        reduced[3],
        reduced[4],
        reduced[5],
        expert_sums[0],
        expert_sums[1],
    )


def solution(mesh):
    placed = (
        P(("batch", "expert"), None),
        P(("batch", "expert"), None),
        P(("batch", "expert")),
        P(("batch", "expert"), None),
        P(("batch", "expert"), None),
        P(),
        P(),
        P(),
        P(),
        P(),
        P(),
        P("expert", None, None),
        P("expert", None, None),
    )
    return jax.shard_map(
        per_device,
        mesh=mesh,
        in_specs=placed,
        out_specs=(
            P(("batch", "expert"), None),
            P(("batch", "expert"), None),
            P("batch", "expert"),
            P("batch", "expert"),
            P("batch", "expert"),
            P("batch", "expert"),
            P("batch", "expert"),
            P("batch", "expert"),
            P("expert", "batch", None),
            P("expert", "batch", None),
        ),
        check_vma=False,
    )
```

```python
import functools
import math

import jax
import jax.numpy as jnp
from jax import lax
from jax.experimental import pallas as pl
from jax.experimental.pallas import tpu as pltpu
from jax.sharding import PartitionSpec as P

D = 768
HEADS = 12
HEAD_DIM = 64
FF = 3072
EXPERTS = 8
SEQ = 256
CAP = 256
LANES = 128
PAIRS = HEADS // 2
H_MLP, G_SHARED, H_ATTN, HEADS_OUT = range(4)

GELU_C = 0.7978845608028654
GELU_A = 0.044715
EPSILON = 1e-06
MASKED = -1000000000.0
LOG2E = math.log2(math.e)
SCALE = HEAD_DIM ** (-0.5)

F32 = jnp.float32
BF16 = jnp.bfloat16
VMEM_LIMIT = 60 * 1024 * 1024
COST = 0.5


def dot_nn(a, b):
    return jnp.dot(a, b, preferred_element_type=F32)


def dot_nt(a, b):
    return lax.dot_general(a, b, (((1,), (1,)), ((), ())), preferred_element_type=F32)


def dot_tn(a, b):
    return lax.dot_general(a, b, (((0,), (0,)), ((), ())), preferred_element_type=F32)


def normalize(values):
    centre = values - jnp.mean(values, -1, keepdims=True)
    factor = lax.rsqrt(jnp.mean(centre * centre, -1, keepdims=True) + EPSILON)
    return (centre * factor, factor)


def norm_back(grad_norm, normed, factor):
    return factor * (
        grad_norm
        - jnp.mean(grad_norm, -1, keepdims=True)
        - normed * jnp.mean(grad_norm * normed, -1, keepdims=True)
    )


def half_masks():
    lane = lax.broadcasted_iota(jnp.int32, (1, LANES), 1)
    low = jnp.where(lane < HEAD_DIM, 1.0, 0.0).astype(BF16)
    return (low, (1.0 - low).astype(BF16))


def whole(shape):
    return pl.BlockSpec(shape, lambda *_: (0,) * len(shape))


def kind_of(which, t):
    return pl.BlockSpec((1, t, D), lambda *_: (which, 0, 0), pipeline_mode=pl.Buffered(1))


def once(shape):
    return pl.BlockSpec(shape, lambda *_: (0,) * len(shape), pipeline_mode=pl.Buffered(1))


def cost(flops, moved):
    return pl.CostEstimate(
        flops=int(COST * flops), bytes_accessed=int(COST * moved), transcendentals=0
    )


def params(**more):
    return pltpu.CompilerParams(vmem_limit_bytes=VMEM_LIMIT, **more)


def attn_forward_kernel(
    len_ref, tok_ref, cot_ref, mod_ref, wqkv_ref, wout_ref,
    qkv_ref, lse_ref, attn_ref, rows_ref,
):
    item = pl.program_id(0)
    mod = mod_ref[0]
    x = tok_ref[...].astype(F32)
    normed, _ = normalize(x)
    h = (normed * (1.0 + mod[1:2]) + mod[0:1]).astype(BF16)
    rows_ref[H_ATTN] = h
    qkv_ref[...] = dot_nn(h, wqkv_ref[...]).astype(BF16)
    key_live = lax.broadcasted_iota(jnp.int32, (1, SEQ), 1) < len_ref[item]
    masks = half_masks()
    lane = lax.broadcasted_iota(jnp.int32, (SEQ, LANES), 1)
    lse_all = jnp.zeros((SEQ, LANES), F32)
    for pair in range(PAIRS):
        at = LANES * pair
        q2 = qkv_ref[:, at : at + LANES]
        k2 = qkv_ref[:, D + at : D + at + LANES]
        v2 = qkv_ref[:, 2 * D + at : 2 * D + at + LANES]
        outs = []
        for half in range(2):
            s = dot_nt(q2 * masks[half], k2) * (SCALE * LOG2E)
            s = jnp.where(key_live, s, MASKED * LOG2E)
            peak = jnp.max(s, -1, keepdims=True)
            e = jnp.exp2(s - peak)
            total = jnp.sum(e, -1, keepdims=True)
            probs = (e * (1.0 / total)).astype(BF16)
            outs.append(dot_nn(probs, v2))
            lse = peak + jnp.log(total) * LOG2E
            lse_all = jnp.where(lane == 2 * pair + half, lse, lse_all)
        rows_ref[HEADS_OUT, :, at : at + LANES] = jnp.where(
            lane < HEAD_DIM, outs[0], outs[1]
        ).astype(BF16)
    lse_ref[...] = lse_all
    attn = dot_nn(rows_ref[HEADS_OUT], wout_ref[...])
    attn_ref[...] = attn
    x_mid = x + mod[2:3] * attn
    normed_mlp, _ = normalize(x_mid)
    rows_ref[H_MLP] = (normed_mlp * (1.0 + mod[4:5]) + mod[3:4]).astype(BF16)
    rows_ref[G_SHARED] = (mod[5:6] * cot_ref[...].astype(F32)).astype(BF16)


def attn_forward(lengths, tokens, cot, mod, wqkv, wout):
    t = tokens.shape[0]
    items = t // SEQ
    row = lambda w: pl.BlockSpec((SEQ, w), lambda i, _: (i, 0))
    return pl.pallas_call(
        attn_forward_kernel,
        name="attn_forward",
        grid_spec=pltpu.PrefetchScalarGridSpec(
            num_scalar_prefetch=1,
            grid=(items,),
            in_specs=[
                row(D), row(D), pl.BlockSpec((1, 6, D), lambda i, _: (i, 0, 0)),
                once((D, 3 * D)), once((D, D)),
            ],
            out_specs=[
                row(3 * D), row(LANES), row(D), pl.BlockSpec((4, SEQ, D), lambda i, _: (0, i, 0)),
            ],
        ),
        out_shape=[
            jax.ShapeDtypeStruct((t, 3 * D), BF16),
            jax.ShapeDtypeStruct((t, LANES), F32),
            jax.ShapeDtypeStruct((t, D), F32),
            jax.ShapeDtypeStruct((4, t, D), BF16),
        ],
        compiler_params=params(),
        cost_estimate=cost(int(8.1e9), int(24e6)),
    )(lengths, tokens, cot, mod, wqkv, wout)


def live_of(len_ref, items, shape, dim):
    tok = lax.broadcasted_iota(jnp.int32, shape, dim)
    limit = jnp.zeros(shape, jnp.int32)
    for i in range(items):
        limit = jnp.where(tok >= i * SEQ, i * SEQ + len_ref[i], limit)
    return tok < limit


def route_kernel(len_ref, h_ref, rw_ref, rcol_ref, rrow_ref, info_ref, pos_ref):
    t = h_ref.shape[1]
    items = t // SEQ
    lane = lax.broadcasted_iota(jnp.int32, (t, LANES), 1)
    r0 = rcol_ref[:, 0:1]
    r1 = rcol_ref[:, 1:2]
    live = live_of(len_ref, items, (t, 1), 0)
    is0 = lane == r0
    is1 = lane == r1
    hot = jnp.where((is0 | is1) & live, 1.0, 0.0)
    before = (
        lax.broadcasted_iota(jnp.int32, (t, t), 1) < lax.broadcasted_iota(jnp.int32, (t, t), 0)
    )
    tri = jnp.where(before, 1.0, 0.0).astype(BF16)
    count = dot_nn(tri, hot.astype(BF16))
    p0 = jnp.sum(jnp.where(is0, count, 0.0), -1, keepdims=True)
    p1 = jnp.sum(jnp.where(is1, count, 0.0), -1, keepdims=True)
    slot0 = jnp.where(live & (p0 < CAP), r0.astype(F32) * CAP + p0, -1.0)
    slot1 = jnp.where(live & (p1 < CAP), r1.astype(F32) * CAP + p1, -1.0)
    logits = dot_nn(h_ref[0], rw_ref[...])
    l0 = jnp.sum(jnp.where(is0, logits, 0.0), -1, keepdims=True)
    l1 = jnp.sum(jnp.where(is1, logits, 0.0), -1, keepdims=True)
    top = jnp.maximum(l0, l1)
    e0 = jnp.exp(l0 - top)
    e1 = jnp.exp(l1 - top)
    total = e0 + e1
    info = jnp.zeros((t, LANES), F32)
    for k, column in enumerate(
        (e0 / total, e1 / total, slot0, slot1, r0.astype(F32), r1.astype(F32))
    ):
        info = jnp.where(lane == k, column, info)
    info_ref[...] = info
    expert = lax.broadcasted_iota(jnp.int32, (EXPERTS, t), 0)
    live_row = live_of(len_ref, items, (1, t), 1)
    hot_row = ((expert == rrow_ref[0:1, :]) | (expert == rrow_ref[1:2, :])) & live_row
    count_row = dot_nt(jnp.where(hot_row, 1.0, 0.0).astype(BF16), tri)
    pos_ref[...] = jnp.where(hot_row, count_row, -1.0)


def route(lengths, rows, rw_pad, routes, routes_t):
    t = rows.shape[1]
    return pl.pallas_call(
        route_kernel,
        name="route",
        grid=(1,),
        in_specs=[
            pl.BlockSpec(memory_space=pltpu.SMEM), kind_of(H_MLP, t), whole(rw_pad.shape),
            whole(routes.shape), whole(routes_t.shape),
        ],
        out_specs=[whole((t, LANES)), whole((EXPERTS, t))],
        out_shape=[
            jax.ShapeDtypeStruct((t, LANES), F32),
            jax.ShapeDtypeStruct((EXPERTS, t), F32),
        ],
        compiler_params=params(),
        cost_estimate=cost(int(1e9), int(3e6)),
    )(lengths, rows, rw_pad, routes, routes_t)


def dispatch_kernel(local, first, h_ref, cot_ref, mod_ref, info_ref, pos_ref, out_ref, grad_scr):
    group = pl.program_id(0)
    t = h_ref.shape[1]
    items = t // SEQ
    expert = group * local + first

    @pl.when(group == 0)
    def _():
        for i in range(items):
            rows = slice(i * SEQ, (i + 1) * SEQ)
            grad_scr[rows] = mod_ref[i, 5:6, :] * cot_ref[rows].astype(F32)

    pos = pos_ref[pl.ds(expert, 1), :]
    slot = lax.broadcasted_iota(jnp.int32, (CAP, t), 0).astype(F32)
    hot = jnp.where(slot == pos, 1.0, 0.0).astype(BF16)
    out_ref[0, 0] = dot_nn(hot, h_ref[0]).astype(BF16)
    name = expert.astype(F32)
    weight = jnp.where(
        info_ref[:, 4:5] == name, info_ref[:, 0:1],
        jnp.where(info_ref[:, 5:6] == name, info_ref[:, 1:2], 0.0),
    )
    rows = (weight * grad_scr[...]).astype(BF16)
    out_ref[0, 1] = dot_nn(hot, rows).astype(BF16)


def dispatch(first, local, rows, cot, mod, info, pos):
    t = rows.shape[1]
    groups = EXPERTS // local
    return pl.pallas_call(
        functools.partial(dispatch_kernel, local, first),
        name="dispatch",
        grid=(groups,),
        in_specs=[
            kind_of(H_MLP, t), once((t, D)), once(mod.shape), once((t, LANES)), once((EXPERTS, t)),
        ],
        out_specs=pl.BlockSpec((1, 2, CAP, D), lambda g: (g, 0, 0, 0)),
        out_shape=jax.ShapeDtypeStruct((groups, 2, CAP, D), BF16),
        scratch_shapes=[pltpu.VMEM((t, D), F32)],
        compiler_params=params(),
        cost_estimate=cost(int(3.3e9), int(8e6)),
    )(rows, cot, mod, info, pos)


def gelu_pair(v):
    square = v * v
    gate = 0.5 * jnp.tanh(v * (GELU_C * GELU_A * square + GELU_C)) + 0.5
    act = v * gate
    slope = gate + act * (1.0 - gate) * (6.0 * GELU_C * GELU_A * square + 2.0 * GELU_C)
    return act, slope


def ffn_main_kernel(where_ref, x_ref, g_ref, w1_ref, w2_ref, *rest, paired, halved):
    if paired:
        out_ref, act_ref, gpre_ref = rest
        x, g = x_ref[0, 0], x_ref[0, 1]
    else:
        y_ref, gx_ref, act_ref, *gpre_refs, gpre_ref = rest
        x, g = x_ref[0], g_ref[0]
    for f in range(4):
        cols = slice(f * (FF // 4), (f + 1) * (FF // 4))
        act, slope = gelu_pair(dot_nn(x, w1_ref[0, :, cols]))
        act_ref[:, cols] = act.astype(BF16)
        gpre_ref[:, cols] = (dot_nt(g, w2_ref[0, cols, :]) * slope).astype(BF16)
    y = dot_nn(act_ref[...], w2_ref[0])
    gx = dot_nt(gpre_ref[...], w1_ref[0])
    if paired:
        out_ref[0, 0] = y.astype(BF16)
        out_ref[0, 1] = gx.astype(BF16)
    else:
        y_ref[...] = y
        gx_ref[...] = gx
    if halved:
        first = where_ref[0] == 0
        width = FF // 4
        for x_at in range(2):
            low = gpre_ref[:, 2 * x_at * width : (2 * x_at + 1) * width]
            high = gpre_ref[:, (2 * x_at + 1) * width : (2 * x_at + 2) * width]
            cols = slice(x_at * width, (x_at + 1) * width)
            gpre_refs[0][:, cols] = jnp.where(first, low, high)
            gpre_refs[1][:, cols] = jnp.where(first, high, low)


def ffn_main(x, w1, w2, which, where=None):
    paired = x.ndim == 4
    halved = where is not None
    rows = x.shape[0] * CAP if paired else x.shape[1]
    chunk = lambda w: pl.BlockSpec((CAP, w), lambda s, *_: (s, 0))
    scratch = []
    if paired:
        first = [pl.BlockSpec((1, 2, CAP, D), lambda s, *_: (s, 0, 0, 0)), once((8, D))]
        args = (x, jnp.zeros((8, D), BF16))
        outs, out_specs = [jax.ShapeDtypeStruct(x.shape, BF16)], first[:1]
    else:
        kind = lambda k: pl.BlockSpec((1, CAP, D), lambda s, *_: (k, s, 0))
        first = [kind(H_MLP), kind(G_SHARED)]
        args = (x, x)
        outs, out_specs = [jax.ShapeDtypeStruct((rows, D), F32)] * 2, [chunk(D)] * 2
    outs = outs + [jax.ShapeDtypeStruct((rows, FF), BF16)]
    out_specs = out_specs + [chunk(FF)]
    if halved:
        outs = outs + [jax.ShapeDtypeStruct((rows, FF // 2), BF16)] * 2
        out_specs = out_specs + [chunk(FF // 2)] * 2
        scratch = [pltpu.VMEM((CAP, FF), BF16)]
    else:
        where = jnp.zeros((1,), jnp.int32)
        outs = outs + [jax.ShapeDtypeStruct((rows, FF), BF16)]
        out_specs = out_specs + [chunk(FF)]
    weight = lambda r, c: pl.BlockSpec(
        (1, r, c), lambda s, *_: (which, 0, 0), pipeline_mode=pl.Buffered(1)
    )
    return pl.pallas_call(
        functools.partial(ffn_main_kernel, paired=paired, halved=halved),
        name="ffn_main_pairs" if paired else "ffn_main_shared",
        grid_spec=pltpu.PrefetchScalarGridSpec(
            num_scalar_prefetch=1,
            grid=(rows // CAP,),
            in_specs=first + [weight(D, FF), weight(FF, D)],
            out_specs=out_specs,
            scratch_shapes=scratch,
        ),
        out_shape=outs,
        compiler_params=params(),
        cost_estimate=cost(8 * rows * D * FF, int(30e6)),
    )(where, *args, w1, w2)


def weight_grad_kernel(mode, where_ref, a_ref, b_ref, *outs):
    a = a_ref[...].reshape(-1, D)
    part = dot_tn(a, b_ref[...]).astype(BF16)
    if mode == "plain":
        outs[0][...] = part
        return
    first = where_ref[0] == 0
    keep_ref, send_ref = outs
    if mode == "in":
        for z in range(4):
            low = part[192 * z : 192 * z + 96]
            high = part[192 * z + 96 : 192 * z + 192]
            at = (z % 2) ^ where_ref[1], (z // 2) ^ where_ref[2]
            keep_ref[at] = jnp.where(first, low, high)
            send_ref[at] = jnp.where(first, high, low)
    else:
        low, high = part[:, :384], part[:, 384:]
        mine = jnp.where(first, low, high)
        other = jnp.where(first, high, low)
        for k in range(8):
            cols = slice(k * 384, k * 384 + 384)
            keep_ref[0, 0, :, cols] = mine[k * 96 : k * 96 + 96]
            send_ref[0, 0, :, cols] = other[k * 96 : k * 96 + 96]


def weight_grad(mode, mine, a, kind, b):
    rows = b.shape[0]
    tile = FF // 4
    tile_of = lambda s, m: s
    if mode == "out":
        tile_of = lambda s, m: ((s % 2) ^ m[2]) * 2 + ((s // 2) ^ m[1])
    if a.ndim == 3:
        a_spec = kind_of(kind, rows)
    else:
        a_spec = pl.BlockSpec(
            (a.shape[0], 1, CAP, D), lambda s, m: (0, kind, 0, 0), pipeline_mode=pl.Buffered(1)
        )
    if mode == "plain":
        outs = [jax.ShapeDtypeStruct((D, FF), BF16)]
        specs = [pl.BlockSpec((D, tile), lambda s, m: (0, s))]
    else:
        outs = [jax.ShapeDtypeStruct((2, 2, 96, FF), BF16)] * 2
        if mode == "in":
            specs = [pl.BlockSpec((2, 2, 96, tile), lambda s, m: (0, 0, 0, s))] * 2
        else:
            specs = [pl.BlockSpec((1, 1, 96, FF), lambda s, m: (s // 2, s % 2, 0, 0))] * 2
    return pl.pallas_call(
        functools.partial(weight_grad_kernel, mode),
        name="weight_grad_" + mode,
        grid_spec=pltpu.PrefetchScalarGridSpec(
            num_scalar_prefetch=1,
            grid=(FF // tile,),
            in_specs=[a_spec, pl.BlockSpec((rows, tile), lambda s, m: (0, tile_of(s, m)))],
            out_specs=specs,
        ),
        out_shape=outs,
        compiler_params=params(),
        cost_estimate=cost(2 * rows * D * FF, int(13e6)),
    )(mine, a, b)


def batch_at(where_ref, b, y_last):
    z = b // 2
    y = (b % 2) ^ where_ref[2]
    near, far = (z % 2) ^ where_ref[3], (z // 2) ^ where_ref[4]
    return (near, far, y) if y_last else (y, near, far)


def own_columns(where_ref, v, width):
    low = jnp.concatenate([v[:, :width], v[:, 2 * width : 3 * width]], 1)
    high = jnp.concatenate([v[:, width : 2 * width], v[:, 3 * width :]], 1)
    return jnp.where(where_ref[0] == 0, low, high)


def shared_grad_kernel(
    where_ref, mine_ref, peer_ref, gpre_ref, gpre_peer_ref, act_ref, act_peer_ref,
    keep_ref, send_ref, g_scr,
):
    step = pl.program_id(0)
    side = step // 2
    rows = act_ref.shape[0]

    @pl.when(step == 0)
    def _():
        g_scr[:rows] = own_columns(where_ref, mine_ref[G_SHARED], D // 4)
        g_scr[rows:] = own_columns(where_ref, peer_ref[G_SHARED], D // 4)

    part = (
        dot_tn(mine_ref[H_MLP], gpre_ref[...]) + dot_tn(peer_ref[H_MLP], gpre_peer_ref[...])
    ).astype(BF16)
    for half in range(2):
        for s, ref in ((0, keep_ref), (1, send_ref)):
            @pl.when((step % 2 == half) & (side == s))
            def _():
                for b in range(8):
                    ref[(*batch_at(where_ref, b, False), 0, slice(None), slice(half * 384, half * 384 + 384))] = part[b * 96 : b * 96 + 96]

    both = (dot_tn(g_scr[:rows], act_ref[...]) + dot_tn(g_scr[rows:], act_peer_ref[...])).astype(BF16)
    first = where_ref[1] == 0
    low, high = both[:192], both[192:]
    for ref, v in ((keep_ref, jnp.where(first, low, high)), (send_ref, jnp.where(first, high, low))):
        for h in range(2):
            for y in range(2):
                at = batch_at(where_ref, 2 * step + y, False)
                ref[(*at, 1, slice(None), slice(h * 384, h * 384 + 384))] = v[
                    h * 96 : h * 96 + 96, y * 384 : y * 384 + 384
                ]


def shared_grad(where, mine, peer, gpre, gpre_peer, act, act_peer):
    rows = act.shape[0]
    gpre_spec = pl.BlockSpec((rows, FF // 8), lambda s, m: (0, ((s // 2) ^ m[1]) * 2 + s % 2))
    act_spec = pl.BlockSpec((rows, FF // 4), lambda s, m: (0, s))
    stack = pl.BlockSpec((2, rows, D), lambda s, m: (0, 0, 0), pipeline_mode=pl.Buffered(1))
    shape = (2, 2, 2, 2, 96, D)
    return pl.pallas_call(
        shared_grad_kernel,
        name="shared_grad",
        grid_spec=pltpu.PrefetchScalarGridSpec(
            num_scalar_prefetch=1,
            grid=(4,),
            in_specs=[stack, stack, gpre_spec, gpre_spec, act_spec, act_spec],
            out_specs=[once(shape)] * 2,
            scratch_shapes=[pltpu.VMEM((2 * rows, D // 2), BF16)],
        ),
        out_shape=[jax.ShapeDtypeStruct(shape, BF16)] * 2,
        compiler_params=params(),
        cost_estimate=cost(4 * rows * D * FF, int(25e6)),
    )(where, mine, peer, gpre, gpre_peer, act, act_peer)


def backward_kernel(
    local, fast, first_item, len_ref, where_ref, tok_ref, cot_ref, mod_ref, attn_ref, qkv_ref, lse_ref,
    sres_ref, gsh_ref, info_ref, wqkv_ref, wout_ref, rwt_ref, *rest,
):
    back = rest[:local]
    if fast:
        out_ref, gtok_ref, gmod_ref, own_ref, other_ref, gq_ref, yr_ref, gr_ref = rest[-8:]
    else:
        out_ref, gtok_ref, gmod_ref, own_ref, gq_ref, yr_ref, gr_ref = rest[-7:]
    item = pl.program_id(0) + first_item
    slots = yr_ref.shape[0]

    @pl.when(pl.program_id(0) == 0)
    def _():
        for j in range(local):
            for g in range(EXPERTS // local):
                rows = slice((g * local + j) * CAP, (g * local + j + 1) * CAP)
                yr_ref[rows] = back[j][g, 0]
                gr_ref[rows] = back[j][g, 1]

    mod = mod_ref[0]
    x = tok_ref[...].astype(F32)
    cot = cot_ref[...].astype(F32)
    attn = attn_ref[...]
    x_mid = x + mod[2:3] * attn
    normed_mlp, factor_mlp = normalize(x_mid)
    gw0, gw1 = info_ref[:, 0:1], info_ref[:, 1:2]
    slot = lax.broadcasted_iota(jnp.int32, (SEQ, slots), 1).astype(F32)
    hot0 = jnp.where(slot == info_ref[:, 2:3], 1.0, 0.0).astype(BF16)
    hot1 = jnp.where(slot == info_ref[:, 3:4], 1.0, 0.0).astype(BF16)
    row0 = dot_nn(hot0, yr_ref[...])
    row1 = dot_nn(hot1, yr_ref[...])
    mlp_out = sres_ref[...] + (gw0 * row0 + gw1 * row1)
    out_ref[...] = (x_mid + mod[5:6] * mlp_out).astype(BF16)
    gmod_ref[0, 5:6, :] = jnp.sum(cot * mlp_out, 0, keepdims=True)
    grad_mlp = mod[5:6] * cot
    gate0 = jnp.sum(grad_mlp * row0, -1, keepdims=True)
    gate1 = jnp.sum(grad_mlp * row1, -1, keepdims=True)
    weighted = gw0 * gate0 + gw1 * gate1
    sel0 = gw0 * (gate0 - weighted)
    sel1 = gw1 * (gate1 - weighted)
    high0 = sel0.astype(BF16).astype(F32)
    high1 = sel1.astype(BF16).astype(F32)
    lane = lax.broadcasted_iota(jnp.int32, (SEQ, LANES), 1)
    lane_f = lane.astype(F32)
    r0, r1 = info_ref[:, 4:5], info_ref[:, 5:6]
    g_logits = (
        jnp.where(lane_f == r0, high0, 0.0)
        + jnp.where(lane_f == r1, high1, 0.0)
        + jnp.where(lane_f == r0 + EXPERTS, sel0 - high0, 0.0)
        + jnp.where(lane_f == r1 + EXPERTS, sel1 - high1, 0.0)
    ).astype(BF16)
    grad_h = gsh_ref[...] + dot_nn(hot0 + hot1, gr_ref[...]) + dot_nn(g_logits, rwt_ref[...])
    gmod_ref[0, 3:4, :] = jnp.sum(grad_h, 0, keepdims=True)
    gmod_ref[0, 4:5, :] = jnp.sum(grad_h * normed_mlp, 0, keepdims=True)
    grad_mid = cot + norm_back(grad_h * (1.0 + mod[4:5]), normed_mlp, factor_mlp)
    gmod_ref[0, 2:3, :] = jnp.sum(grad_mid * attn, 0, keepdims=True)
    g_attn = (mod[2:3] * grad_mid).astype(BF16)
    g_heads = dot_nt(g_attn, wout_ref[...]).astype(BF16)
    key_live = lax.broadcasted_iota(jnp.int32, (1, SEQ), 1) < len_ref[item]
    masks = half_masks()
    low_half = lane < HEAD_DIM
    for pair in range(PAIRS):
        at = LANES * pair
        q2 = qkv_ref[:, at : at + LANES]
        k2 = qkv_ref[:, D + at : D + at + LANES]
        v2 = qkv_ref[:, 2 * D + at : 2 * D + at + LANES]
        gh2 = g_heads[:, at : at + LANES]
        dq, dk, dv = [], [], []
        for half in range(2):
            head = 2 * pair + half
            s = dot_nt(q2 * masks[half], k2) * (SCALE * LOG2E)
            s = jnp.where(key_live, s, MASKED * LOG2E)
            probs = jnp.exp2(s - lse_ref[:, head : head + 1])
            g_probs = dot_nt(gh2 * masks[half], v2)
            spread = jnp.sum(probs * g_probs, -1, keepdims=True)
            g_scores = (probs * (g_probs - spread)).astype(BF16)
            dq.append(dot_nn(g_scores, k2))
            dk.append(dot_tn(g_scores, q2))
            dv.append(dot_tn(probs.astype(BF16), gh2))
        gq_ref[:, at : at + LANES] = (jnp.where(low_half, dq[0], dq[1]) * SCALE).astype(BF16)
        gq_ref[:, D + at : D + at + LANES] = (
            jnp.where(low_half, dk[0], dk[1]) * SCALE
        ).astype(BF16)
        gq_ref[:, 2 * D + at : 2 * D + at + LANES] = jnp.where(low_half, dv[0], dv[1]).astype(BF16)
    g_qkv = gq_ref[...]
    g_h = dot_nt(g_qkv, wqkv_ref[...])
    normed, factor = normalize(x)
    gmod_ref[0, 0:1, :] = jnp.sum(g_h, 0, keepdims=True)
    gmod_ref[0, 1:2, :] = jnp.sum(g_h * normed, 0, keepdims=True)
    gmod_ref[0, 6:8, :] = jnp.zeros((2, D), F32)
    gtok_ref[...] = grad_mid + norm_back(g_h * (1.0 + mod[1:2]), normed, factor)
    if fast:
        sides = [
            jnp.concatenate(
                [
                    g_qkv[:, 576 * c : 576 * c + 576],
                    g_qkv[:, 1152 + 576 * c : 1728 + 576 * c],
                    g_attn[:, 192 * c : 192 * c + 192],
                    g_attn[:, 384 + 192 * c : 576 + 192 * c],
                ], 1
            )
            for c in range(2)
        ]
        first = where_ref[0] == 0
        own_ref[:, : 2 * D] = jnp.where(first, sides[0], sides[1])
        own_ref[:, 2 * D :] = g_logits
        other_ref[:, : 2 * D] = jnp.where(first, sides[1], sides[0])
        other_ref[:, 2 * D :] = g_logits
    else:
        own_ref[:, : 3 * D] = g_qkv
        own_ref[:, 3 * D : 4 * D] = g_attn
        own_ref[:, 4 * D :] = g_logits


def backward(
    fast, where, first_item, count, so_far, lengths, tokens, cot, mod, attn, qkv, lse, sres, gsh,
    info, back, wqkv, wout, rwt,
):
    t = tokens.shape[0]
    row = lambda w: pl.BlockSpec((SEQ, w), lambda i, *_: (i + first_item, 0))
    new = lambda w: pl.BlockSpec((SEQ, w), lambda i, *_: (i, 0))
    local = len(back)
    item_block = lambda r: pl.BlockSpec((1, r, D), lambda i, *_: (i + first_item, 0, 0))
    known = 14 + local
    widths = [2 * D + LANES] * 2 if fast else [4 * D + LANES]
    outs = pl.pallas_call(
        functools.partial(backward_kernel, local, fast, first_item),
        name="backward",
        grid_spec=pltpu.PrefetchScalarGridSpec(
            num_scalar_prefetch=2,
            grid=(count,),
            in_specs=[
                row(D), row(D), item_block(6),
                row(D), row(3 * D), row(LANES), row(D), row(D), row(LANES),
                once((D, 3 * D)), once((D, D)), once((LANES, D)),
            ] + [once(b.shape) for b in back]
            + [pl.BlockSpec(memory_space=pl.ANY)] * len(so_far),
            out_specs=[row(D), row(D), item_block(8)] + [new(w) for w in widths],
            scratch_shapes=[
                pltpu.VMEM((SEQ, 3 * D), BF16),
                pltpu.VMEM((EXPERTS * CAP, D), BF16),
                pltpu.VMEM((EXPERTS * CAP, D), BF16),
            ],
        ),
        out_shape=[
            jax.ShapeDtypeStruct((t, D), BF16),
            jax.ShapeDtypeStruct((t, D), F32),
            jax.ShapeDtypeStruct((t // SEQ, 8, D), F32),
        ] + [jax.ShapeDtypeStruct((count * SEQ, w), BF16) for w in widths],
        input_output_aliases={known + i: i for i in range(len(so_far))},
        compiler_params=params(),
        cost_estimate=cost(int(5e9) * count, int(7e6) * count),
    )(
        lengths, where, tokens, cot, mod, attn, qkv, lse, sres, gsh, info, wqkv, wout, rwt,
        *back, *so_far,
    )
    return (outs[:3], *outs[3:])


def tail_grad_kernel(fast, many, where_ref, *refs):
    stacks, grads, outs = refs[:many], refs[many:-2 if fast else -3], refs[-2 if fast else -3:]
    width = 3 * D // 2 if fast else 3 * D
    part = grads[0].shape[0]
    each = len(grads) // many

    def total(kind, start, size):
        value = None
        for i, g in enumerate(grads):
            at = (i % each) * part
            term = dot_tn(stacks[i // each][kind, at : at + part], g[:, start : start + size])
            value = term if value is None else value + term
        return value

    d_qkv = total(H_ATTN, 0, width).astype(BF16)
    d_out = total(HEADS_OUT, width, width // 3).astype(BF16)
    d_router = total(H_MLP, width + width // 3, LANES)
    d_router = (d_router + pltpu.roll(d_router, LANES - EXPERTS, 1)).astype(BF16)
    if not fast:
        outs[0][...], outs[1][...], outs[2][...] = d_qkv, d_out, d_router
        return
    first = where_ref[1] == 0
    low, high = [
        jnp.concatenate(
            [d_qkv[:, 576 * x : 576 * x + 576], d_out[:, 192 * x : 192 * x + 192], d_router], 1
        )
        for x in range(2)
    ]
    for ref, v in ((outs[0], jnp.where(first, low, high)), (outs[1], jnp.where(first, high, low))):
        for b in range(8):
            ref[batch_at(where_ref, b, True)] = v[b * 96 : b * 96 + 96]


def tail_grad(fast, where, stacks, grads):
    if fast:
        outs = [jax.ShapeDtypeStruct((2, 2, 2, 96, D + LANES), BF16)] * 2
    else:
        outs = [
            jax.ShapeDtypeStruct((D, 3 * D), BF16),
            jax.ShapeDtypeStruct((D, D), BF16),
            jax.ShapeDtypeStruct((D, LANES), BF16),
        ]
    vmem = pl.BlockSpec(memory_space=pltpu.VMEM)
    return pl.pallas_call(
        functools.partial(tail_grad_kernel, fast, len(stacks)),
        name="tail_grad",
        in_specs=[pl.BlockSpec(memory_space=pltpu.SMEM)] + [vmem] * (len(stacks) + len(grads)),
        out_specs=[vmem] * len(outs),
        out_shape=outs,
        compiler_params=params(),
        cost_estimate=cost(int(5e9), int(20e6)),
    )(where, *stacks, *grads)


def after(value, *others):
    if not others:
        return value
    return lax.optimization_barrier((value,) + tuple(others))[0]


def group_sum(blocks, axis, groups):
    width = len(groups[0])
    if width == 1:
        return blocks[0].astype(F32)
    low = blocks.astype(BF16)
    if width == 2:
        place = jnp.zeros((), jnp.int32)
        index = lax.axis_index(axis)
        for g in groups:
            place = jnp.where(index == g[1], 1, place)
        sent = lax.dynamic_index_in_dim(low, 1 - place, 0, keepdims=False)
        kept = lax.dynamic_index_in_dim(low, place, 0, keepdims=False)
        return pair_sum(kept, sent, axis, groups)
    got = lax.all_to_all(low, axis, 0, 0, tiled=True, axis_index_groups=groups)
    return jnp.sum(got.astype(F32), 0)


def pair_sum(kept, sent, axis, groups):
    pairs = [(g[0], g[1]) for g in groups] + [(g[1], g[0]) for g in groups]
    got = lax.ppermute(sent, axis, pairs)
    return kept.astype(F32) + got.astype(F32)


def swap(value, axis, bit):
    size = lax.axis_size(axis)
    return lax.ppermute(value.astype(BF16), axis, [(i, i ^ bit) for i in range(size)])


class Chain:
    def __init__(self, keep, send, stages):
        self.terms, self.send, self.stages = [keep], send, list(stages)

    def total(self):
        value = self.terms[0].astype(F32)
        for term in self.terms[1:]:
            value = value + term.astype(F32)
        return value

    def step(self, send_after=(), take_after=()):
        axis, bit = self.stages.pop(0)
        got = swap(after(self.send, *send_after), axis, bit)
        self.terms.append(after(got, *take_after))
        if self.stages:
            terms = self.terms
            self.terms = [v[1] for v in terms]
            self.send = self.total().astype(BF16)
            self.terms = [v[0] for v in terms]
        else:
            self.send = None
        return self


def inner_groups(outer, inner):
    return [[o * inner + i for i in range(inner)] for o in range(outer)]


def outer_groups(outer, inner):
    return [[o * inner + i for o in range(outer)] for i in range(inner)]


def batch_split(size):
    inner = 2 if size <= 8 else 8
    return (size // inner, inner)


def reduce_batch(blocks):
    outer, inner = batch_split(lax.axis_size("batch"))
    v = jnp.moveaxis(blocks.reshape((outer, inner) + blocks.shape[1:]), 1, 0)
    v = group_sum(v, "batch", inner_groups(outer, inner))
    return group_sum(v, "batch", outer_groups(outer, inner))


def reduce_expert(blocks):
    outer, inner = lax.axis_size("expert") // 2, 2
    v = jnp.moveaxis(blocks.reshape((outer, inner) + blocks.shape[1:]), 1, 0)
    v = group_sum(v, "expert", inner_groups(outer, inner))
    return group_sum(v, "expert", outer_groups(outer, inner))


def reduce_dense(grad):
    nb, ne = lax.axis_size("batch"), lax.axis_size("expert")
    r, c = grad.shape
    v = jnp.transpose(grad.reshape(r, ne, c // ne), (1, 0, 2))
    v = reduce_expert(v)
    return reduce_batch(v.reshape(nb, r // nb, c // ne))


def reduce_local(grad):
    nb = lax.axis_size("batch")
    r, c = grad.shape
    return reduce_batch(grad.reshape(nb, r // nb, c))


def all_pairs(parts):
    nb, ne = parts.shape[:2]
    return lax.all_to_all(
        parts.reshape((nb * ne,) + parts.shape[2:]), ("batch", "expert"), 0, 0, tiled=True
    )


def per_device(
    tokens, condition, lengths, routes, cotangent, ada_weight, qkv_weight, out_weight,
    router_weight, shared_in, shared_out, expert_in, expert_out,
):
    nb, ne = lax.axis_size("batch"), lax.axis_size("expert")
    local = expert_in.shape[0]
    items = lengths.shape[0]
    t = tokens.shape[0]
    fast = nb == 8 and ne == 4 and local == 2
    batch, expert = lax.axis_index("batch"), lax.axis_index("expert")
    z_at = batch // 2
    where = jnp.stack([expert % 2, expert // 2, batch % 2, z_at % 2, z_at // 2]).astype(jnp.int32)
    y_at = jnp.stack([batch % 2, z_at % 2, z_at // 2]).astype(jnp.int32)

    act = jax.nn.silu(condition.astype(F32)).astype(BF16)
    mod = dot_nn(act, ada_weight).reshape(items, 6, D)
    rw_pad = jnp.pad(router_weight, ((0, 0), (0, LANES - EXPERTS)))
    rw_t = router_weight.T
    rwt_pad = jnp.pad(jnp.concatenate([rw_t, rw_t], 0), ((0, LANES - 2 * EXPERTS), (0, 0)))

    qkv, lse, attn, rows = attn_forward(lengths, tokens, cotangent, mod, qkv_weight, out_weight)
    if fast:
        peer_rows = swap(rows, "expert", 1)
    info, pos = route(lengths, rows, rw_pad, routes, routes.T)
    sent, received = [], []
    rows_now = rows
    for j in range(local):
        sent.append(dispatch(j, local, rows_now, cotangent, mod, info, pos))
        rows_now = after(rows, sent[j])
    sres, gsh, s_act, *s_gpre = ffn_main(
        rows_now, shared_in[None], shared_out[None], 0, where if fast else None
    )
    if fast:
        peer_act = swap(s_act, "expert", 1)
        peer_gpre = swap(s_gpre[1], "expert", 1)
    for j in range(local):
        part = after(sent[j], sres) if j else sent[j]
        received.append(lax.all_to_all(part, "expert", 0, 0, tiled=True))
    back, expert_grads = [], []
    last = sres
    for j in range(local):
        rows_in = after(received[j], last)
        y, act_e, gpre_e = ffn_main(rows_in, expert_in, expert_out, j)
        back.append(lax.all_to_all(y, "expert", 0, 0, tiled=True))
        grad_rows = after(rows_in, back[j - 1]) if j else rows_in
        d2 = weight_grad("out" if fast else "plain", y_at, grad_rows, 1, act_e)
        d1 = weight_grad("in" if fast else "plain", y_at, after(rows_in, d2[0]), 0, gpre_e)
        last = d1[0]
        expert_grads.append((d1, d2))
    rows_now = after(rows, last)
    if fast:
        expert_stages = [("batch", 1), ("batch", 2), ("batch", 4)]
        shared_stages = [("expert", 2), ("batch", 1), ("batch", 2), ("batch", 4)]
        tail_stages = [("expert", 2), ("batch", 2), ("batch", 4), ("batch", 1)]
        in0, out0 = [Chain(*g, expert_stages) for g in expert_grads[0]]
        in1, out1 = [Chain(*g, expert_stages) for g in expert_grads[1]]
        out0.step()
        rows_now = after(rows_now, out0.send)
        shared_grads = shared_grad(where, rows_now, peer_rows, s_gpre[0], peer_gpre, s_act, peer_act)
        shared_sum = Chain(*shared_grads, shared_stages)
    else:
        shared_grads = (
            weight_grad("plain", y_at, rows_now, H_MLP, s_gpre[0])[0],
            weight_grad("plain", y_at, rows_now, G_SHARED, s_act)[0],
        )
    pieces = items if fast else 2
    per = items // pieces
    tok = after(tokens, shared_grads[0])
    outs, own, other = [], [], []
    for piece in range(pieces):
        outs, first, *second = backward(
            fast, where, piece * per, per, outs, lengths, tok, cotangent, mod, attn, qkv, lse,
            sres, gsh, info, back, qkv_weight, out_weight, rwt_pad,
        )
        own.append(first)
        now = (outs[0],)
        tok = after(tokens, *now)
        if fast:
            other.append(swap(second[0], "expert", 1))
            if piece == 0:
                in0.step(take_after=now)
                out0.step(take_after=now)
                tok = after(tok, in0.send, out0.send)
            elif piece == 2:
                in0.step(take_after=now)
                out0.step(take_after=now)
                tok = after(tok, in0.send, out0.terms[-1])
            elif piece == 3:
                out1.step(take_after=now)
                in0.step(take_after=now)
                shared_sum.step(take_after=now)
                where_now = after(where, out1.send, shared_sum.send, in0.terms[-1])
    result, grad_tokens, grad_mod = outs
    stacks = [rows, peer_rows] if fast else [rows]
    if not fast:
        where_now = where
    tail = tail_grad(fast, where_now, stacks, own + other)

    cols, ada_rows = 6 * D // ne, D // nb
    mod_parts = jnp.transpose(grad_mod[:, :6].reshape(items, ne, cols), (1, 0, 2))
    act_parts = jnp.transpose(act.astype(F32).reshape(items, nb, ada_rows), (1, 0, 2))
    act_parts = jnp.pad(act_parts, ((0, 0), (0, 0), (0, -ada_rows % LANES)))
    width = act_parts.shape[-1]
    parts = jnp.concatenate(
        [
            jnp.broadcast_to(mod_parts[None], (nb, ne, items, cols)),
            jnp.broadcast_to(act_parts[:, None], (nb, ne, items, width)),
        ],
        -1,
    )
    got = all_pairs(parts)

    if fast:
        def unfold(v):
            return v.reshape(96, 8, 384).transpose(2, 1, 0).reshape(384, D)

        tail_sum = Chain(*tail, tail_stages)
        token = tail[0]
        order = (
            in1, out1, tail_sum, in1, out1, shared_sum, in1,
            tail_sum, shared_sum, tail_sum, shared_sum, tail_sum,
        )
        for chain in order:
            chain.step(take_after=(token,))
            token = chain.send if chain.stages else token
        got = after(got, token)
        assert not any(c.stages for c in (in0, in1, out0, out1, shared_sum, tail_sum))
        sh, tl = shared_sum.total(), tail_sum.total()
        g_sh1 = sh[0]
        g_sh2 = sh[1].reshape(96, 2, 384).transpose(2, 1, 0).reshape(384, 192)
        g_e1 = jnp.stack([in0.total(), in1.total()])
        g_e2 = jnp.stack([unfold(out0.total()), unfold(out1.total())])
        g_qkv = tl[:, :576]
        g_out = tl[:, 576:768]
        g_rt = lax.dynamic_slice_in_dim(tl[:, 768:776], 2 * expert, 2, 1)
    else:
        def flipped(grad):
            r, c = grad.shape
            return jnp.transpose(reduce_dense_t(grad))

        def reduce_dense_t(grad):
            r, c = grad.shape
            v = reduce_expert(grad.reshape(ne, r // ne, c))
            v = jnp.transpose(v.reshape(r // ne, nb, c // nb), (1, 0, 2))
            return reduce_batch(v)

        g_sh1 = reduce_dense(shared_grads[0])
        g_sh2 = flipped(shared_grads[1])
        g_e1 = jnp.stack([reduce_local(g[0][0]) for g in expert_grads])
        g_e2 = jnp.stack([
            jnp.transpose(reduce_batch(jnp.transpose(g[1][0].reshape(D, nb, FF // nb), (1, 0, 2))))
            for g in expert_grads
        ])
        g_qkv = reduce_dense(tail[0])
        g_out = reduce_dense(tail[1])
        g_rt = reduce_dense(tail[2][:, :EXPERTS])
    got = got.reshape(nb * ne * items, cols + width)
    grad_ada = jnp.dot(
        got[:, cols : cols + ada_rows].T, got[:, :cols], precision=lax.Precision.HIGHEST
    )
    return (
        result, grad_tokens, grad_ada, g_qkv, g_out, g_rt, g_sh1, g_sh2, g_e1, g_e2
    )


def solution(mesh):
    placed = (
        P(("batch", "expert"), None),
        P(("batch", "expert"), None),
        P(("batch", "expert")),
        P(("batch", "expert"), None),
        P(("batch", "expert"), None),
        P(),
        P(),
        P(),
        P(),
        P(),
        P(),
        P("expert", None, None),
        P("expert", None, None),
    )
    return jax.shard_map(
        per_device,
        mesh=mesh,
        in_specs=placed,
        out_specs=(
            P(("batch", "expert"), None),
            P(("batch", "expert"), None),
            P("batch", "expert"),
            P("batch", "expert"),
            P("batch", "expert"),
            P("batch", "expert"),
            P("batch", "expert"),
            P("batch", "expert"),
            P("expert", "batch", None),
            P("expert", "batch", None),
        ),
        check_vma=False,
    )
```

```python
import functools
import math

import jax
import jax.numpy as jnp
from jax import lax
from jax.experimental import pallas as pl
from jax.experimental.pallas import tpu as pltpu
from jax.sharding import PartitionSpec as P

D = 768
HEADS = 12
HEAD_DIM = 64
FF = 3072
EXPERTS = 8
SEQ = 256
CAP = 256
LANES = 128
PAIRS = HEADS // 2
H_MLP, G_SHARED, H_ATTN, HEADS_OUT = range(4)

GELU_C = 0.7978845608028654
GELU_A = 0.044715
EPSILON = 1e-06
MASKED = -1000000000.0
LOG2E = math.log2(math.e)
SCALE = HEAD_DIM ** (-0.5)

F32 = jnp.float32
BF16 = jnp.bfloat16
VMEM_LIMIT = 60 * 1024 * 1024
COST = 0.5


def dot_nn(a, b):
    return jnp.dot(a, b, preferred_element_type=F32)


def dot_nt(a, b):
    return lax.dot_general(a, b, (((1,), (1,)), ((), ())), preferred_element_type=F32)


def dot_tn(a, b):
    return lax.dot_general(a, b, (((0,), (0,)), ((), ())), preferred_element_type=F32)


def normalize(values):
    centre = values - jnp.mean(values, -1, keepdims=True)
    factor = lax.rsqrt(jnp.mean(centre * centre, -1, keepdims=True) + EPSILON)
    return (centre * factor, factor)


def norm_back(grad_norm, normed, factor):
    return factor * (
        grad_norm
        - jnp.mean(grad_norm, -1, keepdims=True)
        - normed * jnp.mean(grad_norm * normed, -1, keepdims=True)
    )


def half_masks():
    lane = lax.broadcasted_iota(jnp.int32, (1, LANES), 1)
    low = jnp.where(lane < HEAD_DIM, 1.0, 0.0).astype(BF16)
    return (low, (1.0 - low).astype(BF16))


def whole(shape):
    return pl.BlockSpec(shape, lambda *_: (0,) * len(shape))


def kind_of(which, t):
    return pl.BlockSpec((1, t, D), lambda *_: (which, 0, 0), pipeline_mode=pl.Buffered(1))


def once(shape):
    return pl.BlockSpec(shape, lambda *_: (0,) * len(shape), pipeline_mode=pl.Buffered(1))


ANY = pl.BlockSpec(memory_space=pl.ANY)


class Fetch:
    def __init__(self, pairs, sems):
        self.step = pl.program_id(0)
        self.copies = [
            pltpu.make_async_copy(src, dst, sems.at[i]) for i, (src, dst) in enumerate(pairs)
        ]

        @pl.when(self.step == 0)
        def _():
            for copy in self.copies:
                copy.start()

    def need(self, *which):
        @pl.when(self.step == 0)
        def _():
            for i in which:
                self.copies[i].wait()


def cost(flops, moved):
    return pl.CostEstimate(
        flops=int(COST * flops), bytes_accessed=int(COST * moved), transcendentals=0
    )


def params(**more):
    return pltpu.CompilerParams(vmem_limit_bytes=VMEM_LIMIT, **more)


def attn_forward_kernel(
    len_ref, tok_ref, cot_ref, mod_ref, wqkv_ref, wout_ref,
    qkv_ref, lse_ref, attn_ref, rows_ref,
):
    item = pl.program_id(0)
    mod = mod_ref[0]
    x = tok_ref[...].astype(F32)
    normed, _ = normalize(x)
    h = (normed * (1.0 + mod[1:2]) + mod[0:1]).astype(BF16)
    rows_ref[H_ATTN] = h
    qkv_ref[...] = dot_nn(h, wqkv_ref[...]).astype(BF16)
    key_live = lax.broadcasted_iota(jnp.int32, (1, SEQ), 1) < len_ref[item]
    masks = half_masks()
    lane = lax.broadcasted_iota(jnp.int32, (SEQ, LANES), 1)
    lse_all = jnp.zeros((SEQ, LANES), F32)
    for pair in range(PAIRS):
        at = LANES * pair
        q2 = qkv_ref[:, at : at + LANES]
        k2 = qkv_ref[:, D + at : D + at + LANES]
        v2 = qkv_ref[:, 2 * D + at : 2 * D + at + LANES]
        outs = []
        for half in range(2):
            s = dot_nt(q2 * masks[half], k2) * (SCALE * LOG2E)
            s = jnp.where(key_live, s, MASKED * LOG2E)
            peak = jnp.max(s, -1, keepdims=True)
            e = jnp.exp2(s - peak)
            total = jnp.sum(e, -1, keepdims=True)
            probs = (e * (1.0 / total)).astype(BF16)
            outs.append(dot_nn(probs, v2))
            lse = peak + jnp.log(total) * LOG2E
            lse_all = jnp.where(lane == 2 * pair + half, lse, lse_all)
        rows_ref[HEADS_OUT, :, at : at + LANES] = jnp.where(
            lane < HEAD_DIM, outs[0], outs[1]
        ).astype(BF16)
    lse_ref[...] = lse_all
    attn = dot_nn(rows_ref[HEADS_OUT], wout_ref[...])
    attn_ref[...] = attn
    x_mid = x + mod[2:3] * attn
    normed_mlp, _ = normalize(x_mid)
    rows_ref[H_MLP] = (normed_mlp * (1.0 + mod[4:5]) + mod[3:4]).astype(BF16)
    rows_ref[G_SHARED] = (mod[5:6] * cot_ref[...].astype(F32)).astype(BF16)


def attn_forward(lengths, tokens, cot, mod, wqkv, wout):
    t = tokens.shape[0]
    items = t // SEQ
    row = lambda w: pl.BlockSpec((SEQ, w), lambda i, _: (i, 0))
    return pl.pallas_call(
        attn_forward_kernel,
        name="attn_forward",
        grid_spec=pltpu.PrefetchScalarGridSpec(
            num_scalar_prefetch=1,
            grid=(items,),
            in_specs=[
                row(D), row(D), pl.BlockSpec((1, 6, D), lambda i, _: (i, 0, 0)),
                once((D, 3 * D)), once((D, D)),
            ],
            out_specs=[
                row(3 * D), row(LANES), row(D), pl.BlockSpec((4, SEQ, D), lambda i, _: (0, i, 0)),
            ],
        ),
        out_shape=[
            jax.ShapeDtypeStruct((t, 3 * D), BF16),
            jax.ShapeDtypeStruct((t, LANES), F32),
            jax.ShapeDtypeStruct((t, D), F32),
            jax.ShapeDtypeStruct((4, t, D), BF16),
        ],
        compiler_params=params(),
        cost_estimate=cost(int(8.1e9), int(24e6)),
    )(lengths, tokens, cot, mod, wqkv, wout)


def live_of(len_ref, items, shape, dim):
    tok = lax.broadcasted_iota(jnp.int32, shape, dim)
    limit = jnp.zeros(shape, jnp.int32)
    for i in range(items):
        limit = jnp.where(tok >= i * SEQ, i * SEQ + len_ref[i], limit)
    return tok < limit


def route_kernel(local, len_ref, h_ref, rw_ref, rcol_ref, rrow_ref, info_ref, pos_ref):
    t = h_ref.shape[1]
    items = t // SEQ
    lane = lax.broadcasted_iota(jnp.int32, (t, LANES), 1)
    r0 = rcol_ref[:, 0:1]
    r1 = rcol_ref[:, 1:2]
    live = live_of(len_ref, items, (t, 1), 0)
    is0 = lane == r0
    is1 = lane == r1
    hot = jnp.where((is0 | is1) & live, 1.0, 0.0)
    before = (
        lax.broadcasted_iota(jnp.int32, (t, t), 1) < lax.broadcasted_iota(jnp.int32, (t, t), 0)
    )
    tri = jnp.where(before, 1.0, 0.0).astype(BF16)
    count = dot_nn(tri, hot.astype(BF16))
    p0 = jnp.sum(jnp.where(is0, count, 0.0), -1, keepdims=True)
    p1 = jnp.sum(jnp.where(is1, count, 0.0), -1, keepdims=True)
    groups = EXPERTS // local
    block0 = (r0 % local) * groups + r0 // local
    block1 = (r1 % local) * groups + r1 // local
    slot0 = jnp.where(live & (p0 < CAP), block0.astype(F32) * CAP + p0, -1.0)
    slot1 = jnp.where(live & (p1 < CAP), block1.astype(F32) * CAP + p1, -1.0)
    logits = dot_nn(h_ref[0], rw_ref[...])
    l0 = jnp.sum(jnp.where(is0, logits, 0.0), -1, keepdims=True)
    l1 = jnp.sum(jnp.where(is1, logits, 0.0), -1, keepdims=True)
    top = jnp.maximum(l0, l1)
    e0 = jnp.exp(l0 - top)
    e1 = jnp.exp(l1 - top)
    total = e0 + e1
    info = jnp.zeros((t, LANES), F32)
    for k, column in enumerate(
        (e0 / total, e1 / total, slot0, slot1, r0.astype(F32), r1.astype(F32))
    ):
        info = jnp.where(lane == k, column, info)
    info_ref[...] = info
    expert = lax.broadcasted_iota(jnp.int32, (EXPERTS, t), 0)
    live_row = live_of(len_ref, items, (1, t), 1)
    hot_row = ((expert == rrow_ref[0:1, :]) | (expert == rrow_ref[1:2, :])) & live_row
    count_row = dot_nt(jnp.where(hot_row, 1.0, 0.0).astype(BF16), tri)
    pos_ref[...] = jnp.where(hot_row, count_row, -1.0)


def route(local, lengths, rows, rw_pad, routes, routes_t):
    t = rows.shape[1]
    return pl.pallas_call(
        functools.partial(route_kernel, local),
        name="route",
        grid=(1,),
        in_specs=[
            pl.BlockSpec(memory_space=pltpu.SMEM), kind_of(H_MLP, t), whole(rw_pad.shape),
            whole(routes.shape), whole(routes_t.shape),
        ],
        out_specs=[whole((t, LANES)), whole((EXPERTS, t))],
        out_shape=[
            jax.ShapeDtypeStruct((t, LANES), F32),
            jax.ShapeDtypeStruct((EXPERTS, t), F32),
        ],
        compiler_params=params(),
        cost_estimate=cost(int(1e9), int(3e6)),
    )(lengths, rows, rw_pad, routes, routes_t)


def dispatch_kernel(local, first, h_ref, cot_ref, mod_ref, info_ref, pos_ref, out_ref, grad_scr):
    group = pl.program_id(0)
    t = h_ref.shape[1]
    items = t // SEQ
    expert = group * local + first

    @pl.when(group == 0)
    def _():
        for i in range(items):
            rows = slice(i * SEQ, (i + 1) * SEQ)
            grad_scr[rows] = mod_ref[i, 5:6, :] * cot_ref[rows].astype(F32)

    pos = pos_ref[pl.ds(expert, 1), :]
    slot = lax.broadcasted_iota(jnp.int32, (CAP, t), 0).astype(F32)
    hot = jnp.where(slot == pos, 1.0, 0.0).astype(BF16)
    out_ref[0, 0] = dot_nn(hot, h_ref[0]).astype(BF16)
    name = expert.astype(F32)
    weight = jnp.where(
        info_ref[:, 4:5] == name, info_ref[:, 0:1],
        jnp.where(info_ref[:, 5:6] == name, info_ref[:, 1:2], 0.0),
    )
    rows = (weight * grad_scr[...]).astype(BF16)
    out_ref[0, 1] = dot_nn(hot, rows).astype(BF16)


def dispatch(first, local, rows, cot, mod, info, pos):
    t = rows.shape[1]
    groups = EXPERTS // local
    return pl.pallas_call(
        functools.partial(dispatch_kernel, local, first),
        name="dispatch",
        grid=(groups,),
        in_specs=[
            kind_of(H_MLP, t), once((t, D)), once(mod.shape), once((t, LANES)), once((EXPERTS, t)),
        ],
        out_specs=pl.BlockSpec((1, 2, CAP, D), lambda g: (g, 0, 0, 0)),
        out_shape=jax.ShapeDtypeStruct((groups, 2, CAP, D), BF16),
        scratch_shapes=[pltpu.VMEM((t, D), F32)],
        compiler_params=params(),
        cost_estimate=cost(int(3.3e9), int(8e6)),
    )(rows, cot, mod, info, pos)


def gelu_pair(v):
    square = v * v
    gate = 0.5 * jnp.tanh(v * (GELU_C * GELU_A * square + GELU_C)) + 0.5
    act = v * gate
    slope = gate + act * (1.0 - gate) * (6.0 * GELU_C * GELU_A * square + 2.0 * GELU_C)
    return act, slope


def shared_main_kernel(halved, where_ref, x_ref, g_ref, w1_ref, w2_ref, *rest):
    y_ref, gx_ref, act_ref, *gpre_refs, gpre_ref = rest
    x, g = x_ref[0], g_ref[0]
    for f in range(4):
        cols = slice(f * (FF // 4), (f + 1) * (FF // 4))
        act, slope = gelu_pair(dot_nn(x, w1_ref[:, cols]))
        act_ref[:, cols] = act.astype(BF16)
        gpre_ref[:, cols] = (dot_nt(g, w2_ref[cols, :]) * slope).astype(BF16)
    y_ref[...] = dot_nn(act_ref[...], w2_ref[...])
    gx_ref[...] = dot_nt(gpre_ref[...], w1_ref[...])
    if halved:
        first = where_ref[0] == 0
        width = FF // 4
        for x_at in range(2):
            low = gpre_ref[:, 2 * x_at * width : (2 * x_at + 1) * width]
            high = gpre_ref[:, (2 * x_at + 1) * width : (2 * x_at + 2) * width]
            cols = slice(x_at * width, (x_at + 1) * width)
            gpre_refs[0][:, cols] = jnp.where(first, low, high)
            gpre_refs[1][:, cols] = jnp.where(first, high, low)


def shared_main(halved, where, rows, w1, w2):
    t = rows.shape[1]
    chunk = lambda w: pl.BlockSpec((SEQ, w), lambda s, m: (s, 0))
    kind = lambda k: pl.BlockSpec((1, SEQ, D), lambda s, m: (k, s, 0))
    widths = [FF // 2] * 2 if halved else [FF]
    return pl.pallas_call(
        functools.partial(shared_main_kernel, halved),
        name="shared_main",
        grid_spec=pltpu.PrefetchScalarGridSpec(
            num_scalar_prefetch=1,
            grid=(t // SEQ,),
            in_specs=[kind(H_MLP), kind(G_SHARED), once((D, FF)), once((FF, D))],
            out_specs=[chunk(D), chunk(D), chunk(FF)] + [chunk(w) for w in widths],
            scratch_shapes=[pltpu.VMEM((SEQ, FF), BF16)] if halved else [],
        ),
        out_shape=[jax.ShapeDtypeStruct((t, D), F32)] * 2
        + [jax.ShapeDtypeStruct((t, FF), BF16)]
        + [jax.ShapeDtypeStruct((t, w), BF16) for w in widths],
        compiler_params=params(),
        cost_estimate=cost(8 * t * D * FF, int(30e6)),
    )(where, rows, rows, w1, w2)


def store_out_grad(where_ref, part, keep_ref, send_ref):
    first = where_ref[0] == 0
    low, high = part[:, :384], part[:, 384:]
    mine = jnp.where(first, low, high)
    other = jnp.where(first, high, low)
    for k in range(8):
        cols = slice(k * 384, k * 384 + 384)
        keep_ref[0, 0, :, cols] = mine[k * 96 : k * 96 + 96]
        send_ref[0, 0, :, cols] = other[k * 96 : k * 96 + 96]


def expert_first_kernel(fast, where_ref, rows_ref, w1_ref, act_ref, slope_ref, *outs):
    x = rows_ref[:, 0].reshape(-1, D)
    g = rows_ref[:, 1].reshape(-1, D)
    act, slope = gelu_pair(dot_nn(x, w1_ref[0]))
    act = act.astype(BF16)
    act_ref[...] = act
    slope_ref[...] = slope
    part = dot_tn(g, act).astype(BF16)
    if fast:
        store_out_grad(where_ref, part, *outs)
    else:
        outs[0][...] = part


def expert_first(fast, where, rows, w1, which):
    count = rows.shape[0] * CAP
    tile = FF // 4 if fast else FF // 8
    tile_of = lambda s, m: ((s % 2) ^ m[2]) * 2 + ((s // 2) ^ m[1]) if fast else s
    col = pl.BlockSpec((count, tile), lambda s, m: (0, tile_of(s, m)))
    if fast:
        grads = [jax.ShapeDtypeStruct((2, 2, 96, FF), BF16)] * 2
        specs = [pl.BlockSpec((1, 1, 96, FF), lambda s, m: (s // 2, s % 2, 0, 0))] * 2
    else:
        grads = [jax.ShapeDtypeStruct((D, FF), BF16)]
        specs = [pl.BlockSpec((D, tile), lambda s, m: (0, s))]
    act, slope, *grads = pl.pallas_call(
        functools.partial(expert_first_kernel, fast),
        name="expert_first",
        grid_spec=pltpu.PrefetchScalarGridSpec(
            num_scalar_prefetch=1,
            grid=(FF // tile,),
            in_specs=[
                once(rows.shape), pl.BlockSpec((1, D, tile), lambda s, m: (which, 0, tile_of(s, m))),
            ],
            out_specs=[col, col] + specs,
        ),
        out_shape=[
            jax.ShapeDtypeStruct((count, FF), BF16), jax.ShapeDtypeStruct((count, FF), F32),
        ] + grads,
        compiler_params=params(),
        cost_estimate=cost(4 * count * D * FF, int(30e6)),
    )(where, rows, w1)
    return act, slope, grads


def expert_second_kernel(rows_ref, act_ref, slope_ref, w1_ref, w2_ref, out_ref, gpre_ref):
    g = rows_ref[0, 1]
    for f in range(4):
        cols = slice(f * (FF // 4), (f + 1) * (FF // 4))
        gpre_ref[:, cols] = (dot_nt(g, w2_ref[0, cols, :]) * slope_ref[:, cols]).astype(BF16)
    out_ref[0, 0] = dot_nn(act_ref[...], w2_ref[0]).astype(BF16)
    out_ref[0, 1] = dot_nt(gpre_ref[...], w1_ref[0]).astype(BF16)


def expert_second(rows, act, slope, w1, w2, which):
    count = rows.shape[0] * CAP
    chunk = lambda w: pl.BlockSpec((CAP, w), lambda s: (s, 0))
    pair = pl.BlockSpec((1, 2, CAP, D), lambda s: (s, 0, 0, 0))
    weight = lambda r, c: pl.BlockSpec(
        (1, r, c), lambda s: (which, 0, 0), pipeline_mode=pl.Buffered(1)
    )
    return pl.pallas_call(
        expert_second_kernel,
        name="expert_second",
        grid=(rows.shape[0],),
        in_specs=[pair, chunk(FF), chunk(FF), weight(D, FF), weight(FF, D)],
        out_specs=[pair, chunk(FF)],
        out_shape=[
            jax.ShapeDtypeStruct(rows.shape, BF16), jax.ShapeDtypeStruct((count, FF), BF16),
        ],
        compiler_params=params(),
        cost_estimate=cost(6 * count * D * FF, int(40e6)),
    )(rows, act, slope, w1, w2)


def weight_grad_kernel(fast, where_ref, a_ref, b_ref, *outs):
    part = dot_tn(a_ref[...].reshape(-1, D), b_ref[...]).astype(BF16)
    if not fast:
        outs[0][...] = part
        return
    first = where_ref[0] == 0
    keep_ref, send_ref = outs
    for z in range(4):
        low = part[192 * z : 192 * z + 96]
        high = part[192 * z + 96 : 192 * z + 192]
        at = (z % 2) ^ where_ref[1], (z // 2) ^ where_ref[2]
        keep_ref[at] = jnp.where(first, low, high)
        send_ref[at] = jnp.where(first, high, low)


def weight_grad(fast, where, a, kind, b):
    rows = b.shape[0]
    tile = FF // 4
    if a.ndim == 3:
        a_spec = kind_of(kind, rows)
    else:
        a_spec = pl.BlockSpec(
            (a.shape[0], 1, CAP, D), lambda s, m: (0, kind, 0, 0), pipeline_mode=pl.Buffered(1)
        )
    if fast:
        outs = [jax.ShapeDtypeStruct((2, 2, 96, FF), BF16)] * 2
        specs = [pl.BlockSpec((2, 2, 96, tile), lambda s, m: (0, 0, 0, s))] * 2
    else:
        outs = [jax.ShapeDtypeStruct((D, FF), BF16)]
        specs = [pl.BlockSpec((D, tile), lambda s, m: (0, s))]
    return pl.pallas_call(
        functools.partial(weight_grad_kernel, fast),
        name="weight_grad",
        grid_spec=pltpu.PrefetchScalarGridSpec(
            num_scalar_prefetch=1,
            grid=(FF // tile,),
            in_specs=[a_spec, pl.BlockSpec((rows, tile), lambda s, m: (0, s))],
            out_specs=specs,
        ),
        out_shape=outs,
        compiler_params=params(),
        cost_estimate=cost(2 * rows * D * FF, int(13e6)),
    )(where, a, b)


def batch_at(where_ref, b):
    z = b // 2
    return (b % 2) ^ where_ref[2], (z % 2) ^ where_ref[3], (z // 2) ^ where_ref[4]


def own_columns(where_ref, v, width):
    low = jnp.concatenate([v[:, :width], v[:, 2 * width : 3 * width]], 1)
    high = jnp.concatenate([v[:, width : 2 * width], v[:, 3 * width :]], 1)
    return jnp.where(where_ref[0] == 0, low, high)


def shared_grad_kernel(
    where_ref, mine_ref, peer_ref, gpre_ref, gpre_peer_ref, act_ref, act_peer_ref,
    keep_ref, send_ref, g_scr, part_scr,
):
    step = pl.program_id(0)
    side = step // 2
    rows = act_ref.shape[0]

    @pl.when(step == 0)
    def _():
        g_scr[:rows] = own_columns(where_ref, mine_ref[G_SHARED], D // 4)
        g_scr[rows:] = own_columns(where_ref, peer_ref[G_SHARED], D // 4)

    @pl.when(step % 2 == 0)
    def _():
        part = (
            dot_tn(mine_ref[H_MLP], gpre_ref[...]) + dot_tn(peer_ref[H_MLP], gpre_peer_ref[...])
        ).astype(BF16)
        for b in range(8):
            part_scr[batch_at(where_ref, b)] = part[b * 96 : b * 96 + 96]
        for s, ref in ((0, keep_ref), (1, send_ref)):
            @pl.when(side == s)
            def _():
                ref[:, :, :, 0] = part_scr[...]

    both = (dot_tn(g_scr[:rows], act_ref[...]) + dot_tn(g_scr[rows:], act_peer_ref[...])).astype(BF16)
    first = where_ref[1] == 0
    low, high = both[:192], both[192:]
    for ref, v in ((keep_ref, jnp.where(first, low, high)), (send_ref, jnp.where(first, high, low))):
        for h in range(2):
            for y in range(2):
                at = batch_at(where_ref, 2 * step + y)
                ref[(*at, 1, slice(None), slice(h * 384, h * 384 + 384))] = v[
                    h * 96 : h * 96 + 96, y * 384 : y * 384 + 384
                ]


def shared_grad(where, mine, peer, gpre, gpre_peer, act, act_peer):
    rows = act.shape[0]
    gpre_spec = pl.BlockSpec((rows, FF // 4), lambda s, m: (0, (s // 2) ^ m[1]))
    act_spec = pl.BlockSpec((rows, FF // 4), lambda s, m: (0, s))
    stack = pl.BlockSpec((2, rows, D), lambda s, m: (0, 0, 0), pipeline_mode=pl.Buffered(1))
    shape = (2, 2, 2, 2, 96, D)
    return pl.pallas_call(
        shared_grad_kernel,
        name="shared_grad",
        grid_spec=pltpu.PrefetchScalarGridSpec(
            num_scalar_prefetch=1,
            grid=(4,),
            in_specs=[stack, stack, gpre_spec, gpre_spec, act_spec, act_spec],
            out_specs=[once(shape)] * 2,
            scratch_shapes=[
                pltpu.VMEM((2 * rows, D // 2), BF16), pltpu.VMEM((2, 2, 2, 96, D), BF16),
            ],
        ),
        out_shape=[jax.ShapeDtypeStruct(shape, BF16)] * 2,
        compiler_params=params(),
        cost_estimate=cost(4 * rows * D * FF, int(25e6)),
    )(where, mine, peer, gpre, gpre_peer, act, act_peer)


def backward_kernel(
    local, fast, first_item, len_ref, where_ref, tok_ref, cot_ref, mod_ref, attn_ref, qkv_ref, lse_ref,
    sres_ref, gsh_ref, info_ref, wqkv_ref, wout_ref, rwt_ref, *rest,
):
    back = rest[:local]
    if fast:
        out_ref, gtok_ref, gmod_ref, own_ref, other_ref, gq_ref = rest[-6:]
    else:
        out_ref, gtok_ref, gmod_ref, own_ref, gq_ref = rest[-5:]
    item = pl.program_id(0) + first_item
    slots = EXPERTS * CAP
    each = slots // local

    def pick(hot, kind):
        value = None
        for j in range(local):
            rows = back[j][:, kind].reshape(each, D)
            term = dot_nn(hot[:, j * each : (j + 1) * each], rows)
            value = term if value is None else value + term
        return value

    mod = mod_ref[0]
    x = tok_ref[...].astype(F32)
    cot = cot_ref[...].astype(F32)
    attn = attn_ref[...]
    x_mid = x + mod[2:3] * attn
    normed_mlp, factor_mlp = normalize(x_mid)
    gw0, gw1 = info_ref[:, 0:1], info_ref[:, 1:2]
    slot = lax.broadcasted_iota(jnp.int32, (SEQ, slots), 1).astype(F32)
    hot0 = jnp.where(slot == info_ref[:, 2:3], 1.0, 0.0).astype(BF16)
    hot1 = jnp.where(slot == info_ref[:, 3:4], 1.0, 0.0).astype(BF16)
    row0 = pick(hot0, 0)
    row1 = pick(hot1, 0)
    mlp_out = sres_ref[...] + (gw0 * row0 + gw1 * row1)
    out_ref[...] = (x_mid + mod[5:6] * mlp_out).astype(BF16)
    gmod_ref[0, 5:6, :] = jnp.sum(cot * mlp_out, 0, keepdims=True)
    grad_mlp = mod[5:6] * cot
    gate0 = jnp.sum(grad_mlp * row0, -1, keepdims=True)
    gate1 = jnp.sum(grad_mlp * row1, -1, keepdims=True)
    weighted = gw0 * gate0 + gw1 * gate1
    sel0 = gw0 * (gate0 - weighted)
    sel1 = gw1 * (gate1 - weighted)
    high0 = sel0.astype(BF16).astype(F32)
    high1 = sel1.astype(BF16).astype(F32)
    lane = lax.broadcasted_iota(jnp.int32, (SEQ, LANES), 1)
    lane_f = lane.astype(F32)
    r0, r1 = info_ref[:, 4:5], info_ref[:, 5:6]
    g_logits = (
        jnp.where(lane_f == r0, high0, 0.0)
        + jnp.where(lane_f == r1, high1, 0.0)
        + jnp.where(lane_f == r0 + EXPERTS, sel0 - high0, 0.0)
        + jnp.where(lane_f == r1 + EXPERTS, sel1 - high1, 0.0)
    ).astype(BF16)
    grad_h = gsh_ref[...] + pick(hot0 + hot1, 1) + dot_nn(g_logits, rwt_ref[...])
    gmod_ref[0, 3:4, :] = jnp.sum(grad_h, 0, keepdims=True)
    gmod_ref[0, 4:5, :] = jnp.sum(grad_h * normed_mlp, 0, keepdims=True)
    grad_mid = cot + norm_back(grad_h * (1.0 + mod[4:5]), normed_mlp, factor_mlp)
    gmod_ref[0, 2:3, :] = jnp.sum(grad_mid * attn, 0, keepdims=True)
    g_attn = (mod[2:3] * grad_mid).astype(BF16)
    g_heads = dot_nt(g_attn, wout_ref[...]).astype(BF16)
    key_live = lax.broadcasted_iota(jnp.int32, (1, SEQ), 1) < len_ref[item]
    masks = half_masks()
    low_half = lane < HEAD_DIM
    for pair in range(PAIRS):
        at = LANES * pair
        q2 = qkv_ref[:, at : at + LANES]
        k2 = qkv_ref[:, D + at : D + at + LANES]
        v2 = qkv_ref[:, 2 * D + at : 2 * D + at + LANES]
        gh2 = g_heads[:, at : at + LANES]
        dq, dk, dv = [], [], []
        for half in range(2):
            head = 2 * pair + half
            s = dot_nt(q2 * masks[half], k2) * (SCALE * LOG2E)
            s = jnp.where(key_live, s, MASKED * LOG2E)
            probs = jnp.exp2(s - lse_ref[:, head : head + 1])
            g_probs = dot_nt(gh2 * masks[half], v2)
            spread = jnp.sum(probs * g_probs, -1, keepdims=True)
            g_scores = (probs * (g_probs - spread)).astype(BF16)
            dq.append(dot_nn(g_scores, k2))
            dk.append(dot_tn(g_scores, q2))
            dv.append(dot_tn(probs.astype(BF16), gh2))
        gq_ref[:, at : at + LANES] = (jnp.where(low_half, dq[0], dq[1]) * SCALE).astype(BF16)
        gq_ref[:, D + at : D + at + LANES] = (
            jnp.where(low_half, dk[0], dk[1]) * SCALE
        ).astype(BF16)
        gq_ref[:, 2 * D + at : 2 * D + at + LANES] = jnp.where(low_half, dv[0], dv[1]).astype(BF16)
    g_qkv = gq_ref[...]
    g_h = dot_nt(g_qkv, wqkv_ref[...])
    normed, factor = normalize(x)
    gmod_ref[0, 0:1, :] = jnp.sum(g_h, 0, keepdims=True)
    gmod_ref[0, 1:2, :] = jnp.sum(g_h * normed, 0, keepdims=True)
    gmod_ref[0, 6:8, :] = jnp.zeros((2, D), F32)
    gtok_ref[...] = grad_mid + norm_back(g_h * (1.0 + mod[1:2]), normed, factor)
    if fast:
        sides = [
            jnp.concatenate(
                [
                    g_qkv[:, 576 * c : 576 * c + 576],
                    g_qkv[:, 1152 + 576 * c : 1728 + 576 * c],
                    g_attn[:, 192 * c : 192 * c + 192],
                    g_attn[:, 384 + 192 * c : 576 + 192 * c],
                ], 1
            )
            for c in range(2)
        ]
        first = where_ref[0] == 0
        own_ref[:, : 2 * D] = jnp.where(first, sides[0], sides[1])
        own_ref[:, 2 * D :] = g_logits
        other_ref[:, : 2 * D] = jnp.where(first, sides[1], sides[0])
        other_ref[:, 2 * D :] = g_logits
    else:
        own_ref[:, : 3 * D] = g_qkv
        own_ref[:, 3 * D : 4 * D] = g_attn
        own_ref[:, 4 * D :] = g_logits


def backward(
    fast, where, first_item, count, so_far, lengths, tokens, cot, mod, attn, qkv, lse, sres, gsh,
    info, back, wqkv, wout, rwt,
):
    t = tokens.shape[0]
    row = lambda w: pl.BlockSpec((SEQ, w), lambda i, *_: (i + first_item, 0))
    new = lambda w: pl.BlockSpec((SEQ, w), lambda i, *_: (i, 0))
    local = len(back)
    item_block = lambda r: pl.BlockSpec((1, r, D), lambda i, *_: (i + first_item, 0, 0))
    known = 14 + local
    widths = [2 * D + LANES] * 2 if fast else [4 * D + LANES]
    outs = pl.pallas_call(
        functools.partial(backward_kernel, local, fast, first_item),
        name="backward",
        grid_spec=pltpu.PrefetchScalarGridSpec(
            num_scalar_prefetch=2,
            grid=(count,),
            in_specs=[
                row(D), row(D), item_block(6),
                row(D), row(3 * D), row(LANES), row(D), row(D), row(LANES),
                once((D, 3 * D)), once((D, D)), once((LANES, D)),
            ] + [once(b.shape) for b in back]
            + [pl.BlockSpec(memory_space=pl.ANY)] * len(so_far),
            out_specs=[row(D), row(D), item_block(8)] + [new(w) for w in widths],
            scratch_shapes=[
                pltpu.VMEM((SEQ, 3 * D), BF16),
            ],
        ),
        out_shape=[
            jax.ShapeDtypeStruct((t, D), BF16),
            jax.ShapeDtypeStruct((t, D), F32),
            jax.ShapeDtypeStruct((t // SEQ, 8, D), F32),
        ] + [jax.ShapeDtypeStruct((count * SEQ, w), BF16) for w in widths],
        input_output_aliases={known + i: i for i in range(len(so_far))},
        compiler_params=params(),
        cost_estimate=cost(int(5e9) * count, int(7e6) * count),
    )(
        lengths, where, tokens, cot, mod, attn, qkv, lse, sres, gsh, info, wqkv, wout, rwt,
        *back, *so_far,
    )
    return (outs[:3], *outs[3:])


def tail_grad_kernel(fast, many, where_ref, *refs):
    count = 2 if fast else 3
    *refs, stack_ref, grad_ref, sems = refs
    stacks, grads, outs = refs[:many], refs[many:-count], refs[-count:]
    width = 3 * D // 2 if fast else 3 * D
    each = len(grads) // many
    t = stacks[0].shape[1]
    pairs = []
    for i, stack in enumerate(stacks):
        start = i * t
        pairs.append((stack.at[G_SHARED + 1 :], stack_ref.at[i, : 4 - G_SHARED - 1]))
        pairs.append((stack.at[H_MLP], stack_ref.at[i, 2]))
        for g in grads[i * each : (i + 1) * each]:
            pairs.append((g, grad_ref.at[pl.ds(start, g.shape[0])]))
            start += g.shape[0]
    fetch = Fetch(pairs, sems)
    d_qkv = d_out = d_router = None
    for i in range(many):
        fetch.need(*range((2 + each) * i, (2 + each) * (i + 1)))
        rows = slice(i * t, (i + 1) * t)
        terms = (
            dot_tn(stack_ref[i, 0], grad_ref[rows, :width]),
            dot_tn(stack_ref[i, 1], grad_ref[rows, width : width + width // 3]),
            dot_tn(stack_ref[i, 2], grad_ref[rows, width + width // 3 :]),
        )
        if i:
            terms = (d_qkv + terms[0], d_out + terms[1], d_router + terms[2])
        d_qkv, d_out, d_router = terms
    d_qkv, d_out = d_qkv.astype(BF16), d_out.astype(BF16)
    d_router = (d_router + pltpu.roll(d_router, LANES - EXPERTS, 1)).astype(BF16)
    if not fast:
        outs[0][...], outs[1][...], outs[2][...] = d_qkv, d_out, d_router
        return
    first = where_ref[1] == 0
    low, high = [
        jnp.concatenate(
            [d_qkv[:, 576 * x : 576 * x + 576], d_out[:, 192 * x : 192 * x + 192], d_router], 1
        )
        for x in range(2)
    ]
    for ref, v in ((outs[0], jnp.where(first, low, high)), (outs[1], jnp.where(first, high, low))):
        for b in range(8):
            ref[batch_at(where_ref, b)] = v[b * 96 : b * 96 + 96]


def tail_grad(fast, where, stacks, grads):
    if fast:
        outs = [jax.ShapeDtypeStruct((2, 2, 2, 96, D + LANES), BF16)] * 2
    else:
        outs = [
            jax.ShapeDtypeStruct((D, 3 * D), BF16),
            jax.ShapeDtypeStruct((D, D), BF16),
            jax.ShapeDtypeStruct((D, LANES), BF16),
        ]
    t, wide = stacks[0].shape[1], grads[0].shape[1]
    many = len(stacks)
    return pl.pallas_call(
        functools.partial(tail_grad_kernel, fast, len(stacks)),
        name="tail_grad",
        grid_spec=pltpu.PrefetchScalarGridSpec(
            num_scalar_prefetch=1,
            grid=(1,),
            in_specs=[ANY] * (len(stacks) + len(grads)),
            out_specs=[once(o.shape) for o in outs],
            scratch_shapes=[
                pltpu.VMEM((many, 3, t, D), BF16),
                pltpu.VMEM((many * t, wide), BF16),
                pltpu.SemaphoreType.DMA((2 * many + len(grads),)),
            ],
        ),
        out_shape=outs,
        compiler_params=params(),
        cost_estimate=cost(int(5e9), int(20e6)),
    )(where, *stacks, *grads)


def after(value, *others):
    if not others:
        return value
    return lax.optimization_barrier((value,) + tuple(others))[0]


def group_sum(blocks, axis, groups):
    width = len(groups[0])
    if width == 1:
        return blocks[0].astype(F32)
    low = blocks.astype(BF16)
    if width == 2:
        place = jnp.zeros((), jnp.int32)
        index = lax.axis_index(axis)
        for g in groups:
            place = jnp.where(index == g[1], 1, place)
        sent = lax.dynamic_index_in_dim(low, 1 - place, 0, keepdims=False)
        kept = lax.dynamic_index_in_dim(low, place, 0, keepdims=False)
        return pair_sum(kept, sent, axis, groups)
    got = lax.all_to_all(low, axis, 0, 0, tiled=True, axis_index_groups=groups)
    return jnp.sum(got.astype(F32), 0)


def pair_sum(kept, sent, axis, groups):
    pairs = [(g[0], g[1]) for g in groups] + [(g[1], g[0]) for g in groups]
    got = lax.ppermute(sent, axis, pairs)
    return kept.astype(F32) + got.astype(F32)


def swap(value, axis, bit):
    size = lax.axis_size(axis)
    return lax.ppermute(value.astype(BF16), axis, [(i, i ^ bit) for i in range(size)])


class Chain:
    def __init__(self, keep, send, stages):
        self.terms, self.send, self.stages = [keep], send, list(stages)

    def total(self):
        value = self.terms[0].astype(F32)
        for term in self.terms[1:]:
            value = value + term.astype(F32)
        return value

    def step(self, send_after=(), take_after=()):
        axis, bit = self.stages.pop(0)
        got = swap(after(self.send, *send_after), axis, bit)
        self.terms.append(after(got, *take_after))
        if self.stages:
            terms = self.terms
            self.terms = [v[1] for v in terms]
            self.send = self.total().astype(BF16)
            self.terms = [v[0] for v in terms]
        else:
            self.send = None
        return self


def inner_groups(outer, inner):
    return [[o * inner + i for i in range(inner)] for o in range(outer)]


def outer_groups(outer, inner):
    return [[o * inner + i for o in range(outer)] for i in range(inner)]


def batch_split(size):
    inner = 2 if size <= 8 else 8
    return (size // inner, inner)


def reduce_batch(blocks):
    outer, inner = batch_split(lax.axis_size("batch"))
    v = jnp.moveaxis(blocks.reshape((outer, inner) + blocks.shape[1:]), 1, 0)
    v = group_sum(v, "batch", inner_groups(outer, inner))
    return group_sum(v, "batch", outer_groups(outer, inner))


def reduce_expert(blocks):
    outer, inner = lax.axis_size("expert") // 2, 2
    v = jnp.moveaxis(blocks.reshape((outer, inner) + blocks.shape[1:]), 1, 0)
    v = group_sum(v, "expert", inner_groups(outer, inner))
    return group_sum(v, "expert", outer_groups(outer, inner))


def reduce_dense(grad):
    nb, ne = lax.axis_size("batch"), lax.axis_size("expert")
    r, c = grad.shape
    v = jnp.transpose(grad.reshape(r, ne, c // ne), (1, 0, 2))
    v = reduce_expert(v)
    return reduce_batch(v.reshape(nb, r // nb, c // ne))


def reduce_local(grad):
    nb = lax.axis_size("batch")
    r, c = grad.shape
    return reduce_batch(grad.reshape(nb, r // nb, c))


def all_pairs(parts):
    nb, ne = parts.shape[:2]
    return lax.all_to_all(
        parts.reshape((nb * ne,) + parts.shape[2:]), ("batch", "expert"), 0, 0, tiled=True
    )


def per_device(
    tokens, condition, lengths, routes, cotangent, ada_weight, qkv_weight, out_weight,
    router_weight, shared_in, shared_out, expert_in, expert_out,
):
    nb, ne = lax.axis_size("batch"), lax.axis_size("expert")
    local = expert_in.shape[0]
    items = lengths.shape[0]
    t = tokens.shape[0]
    fast = nb == 8 and ne == 4 and local == 2
    batch, expert = lax.axis_index("batch"), lax.axis_index("expert")
    z_at = batch // 2
    where = jnp.stack([expert % 2, expert // 2, batch % 2, z_at % 2, z_at // 2]).astype(jnp.int32)
    y_at = jnp.stack([batch % 2, z_at % 2, z_at // 2]).astype(jnp.int32)

    act = jax.nn.silu(condition.astype(F32)).astype(BF16)
    mod = dot_nn(act, ada_weight).reshape(items, 6, D)
    rw_pad = jnp.pad(router_weight, ((0, 0), (0, LANES - EXPERTS)))
    rw_t = router_weight.T
    rwt_pad = jnp.pad(jnp.concatenate([rw_t, rw_t], 0), ((0, LANES - 2 * EXPERTS), (0, 0)))

    qkv, lse, attn, rows = attn_forward(lengths, tokens, cotangent, mod, qkv_weight, out_weight)
    if fast:
        peer_rows = swap(rows, "expert", 1)
    info, pos = route(local, lengths, rows, rw_pad, routes, routes.T)
    sent, received = [], []
    rows_now = rows
    for j in range(local):
        sent.append(dispatch(j, local, rows_now, cotangent, mod, info, pos))
        rows_now = after(rows, sent[j])
    sres, gsh, s_act, *s_gpre = shared_main(fast, where, rows_now, shared_in, shared_out)
    if fast:
        peer_act = swap(s_act, "expert", 1)
        peer_gpre = swap(s_gpre[1], "expert", 1)
    for j in range(local):
        part = after(sent[j], sres) if j else sent[j]
        received.append(lax.all_to_all(part, "expert", 0, 0, tiled=True))
    expert_stages = [("batch", 1), ("batch", 2), ("batch", 4)]
    dense_stages = [("expert", 2), ("batch", 1), ("batch", 2), ("batch", 4)]
    back, expert_grads, chains = [], [], []
    last = (sres,)
    for j in range(local):
        rows_in = after(received[j], *last)
        act_e, slope_e, d2 = expert_first(fast, y_at, rows_in, expert_in, j)
        waits = [d2[0], *back]
        if fast:
            chains.append(Chain(*d2, expert_stages))
            if j == 1:
                chains[0].step(take_after=d2[:1])
                waits.append(chains[0].send)
        rows_in = after(rows_in, *waits)
        y, gpre_e = expert_second(rows_in, act_e, slope_e, expert_in, expert_out, j)
        back.append(lax.all_to_all(y, "expert", 0, 0, tiled=True))
        d1 = weight_grad(fast, y_at, after(rows_in, y), 0, gpre_e)
        last = (d1[0],)
        if fast:
            chains.append(Chain(*d1, expert_stages))
        expert_grads.append((d1, d2))
    if fast:
        out0, in0, out1, in1 = chains
        now = last
        out0.step(take_after=now)
        in0.step(take_after=now)
        rows_now = after(rows, *last, out0.send, in0.send)
        shared_grads = shared_grad(where, rows_now, peer_rows, s_gpre[0], peer_gpre, s_act, peer_act)
        shared_sum = Chain(*shared_grads, dense_stages)
    else:
        rows_now = after(rows, *last)
        shared_grads = (
            weight_grad(fast, y_at, rows_now, H_MLP, s_gpre[0])[0],
            weight_grad(fast, y_at, rows_now, G_SHARED, s_act)[0],
        )
    pieces = [items // 2, items - items // 2]
    tok = after(tokens, shared_grads[0])
    outs, own, other = [], [], []
    done = 0
    for piece, per in enumerate(pieces):
        outs, first, *second = backward(
            fast, where, done, per, outs, lengths, tok, cotangent, mod, attn, qkv, lse,
            sres, gsh, info, back, qkv_weight, out_weight, rwt_pad,
        )
        done += per
        own.append(first)
        now = (outs[0],)
        tok = after(tokens, *now)
        if fast:
            other.append(swap(second[0], "expert", 1))
            if piece == 0:
                out0.step(take_after=now)
                in0.step(take_after=now)
                out1.step(take_after=now)
                tok = after(tok, out0.terms[-1], in0.send, out1.send)
            else:
                in1.step(take_after=now)
                in0.step(take_after=now)
                out1.step(take_after=now)
                where_now = after(where, in0.terms[-1], out1.send, in1.send)
    result, grad_tokens, grad_mod = outs
    stacks = [rows, peer_rows] if fast else [rows]
    if not fast:
        where_now = where
    tail = tail_grad(fast, where_now, stacks, own + other)

    cols, ada_rows = 6 * D // ne, D // nb
    mod_parts = grad_mod[:, :6].reshape(items, ne, cols).astype(BF16)
    mod_parts = jnp.transpose(mod_parts, (1, 0, 2))
    act_parts = jnp.transpose(act.reshape(items, nb, ada_rows), (1, 0, 2))
    act_parts = jnp.pad(act_parts, ((0, 0), (0, 0), (0, -ada_rows % LANES)))
    width = act_parts.shape[-1]
    parts = jnp.concatenate(
        [
            jnp.broadcast_to(mod_parts[None], (nb, ne, items, cols)),
            jnp.broadcast_to(act_parts[:, None], (nb, ne, items, width)),
        ],
        -1,
    )
    got = all_pairs(after(parts, tail[0]))

    if fast:
        def unfold(v):
            return v.reshape(96, 8, 384).transpose(2, 1, 0).reshape(384, D)

        tail_sum = Chain(*tail, dense_stages)
        token = tail[0]
        for chain in (
            shared_sum, out1, in1, shared_sum, tail_sum, in1, shared_sum, tail_sum, shared_sum,
            tail_sum, tail_sum,
        ):
            chain.step(take_after=(token,))
            token = chain.send if chain.stages else chain.terms[-1]
        tl = tail_sum.total()
        got = after(got, token)
        assert not any(c.stages for c in (in0, in1, out0, out1, shared_sum, tail_sum))
        sh = shared_sum.total()
        g_sh1 = sh[0]
        g_sh2 = sh[1].reshape(96, 2, 384).transpose(2, 1, 0).reshape(384, 192)
        g_e1 = jnp.stack([in0.total(), in1.total()])
        g_e2 = jnp.stack([unfold(out0.total()), unfold(out1.total())])
        g_qkv = tl[:, :576]
        g_out = tl[:, 576:768]
        g_rt = lax.dynamic_slice_in_dim(tl[:, 768:776], 2 * expert, 2, 1)
    else:
        def flipped(grad):
            r, c = grad.shape
            return jnp.transpose(reduce_dense_t(grad))

        def reduce_dense_t(grad):
            r, c = grad.shape
            v = reduce_expert(grad.reshape(ne, r // ne, c))
            v = jnp.transpose(v.reshape(r // ne, nb, c // nb), (1, 0, 2))
            return reduce_batch(v)

        g_sh1 = reduce_dense(shared_grads[0])
        g_sh2 = flipped(shared_grads[1])
        g_e1 = jnp.stack([reduce_local(g[0][0]) for g in expert_grads])
        g_e2 = jnp.stack([
            jnp.transpose(reduce_batch(jnp.transpose(g[1][0].reshape(D, nb, FF // nb), (1, 0, 2))))
            for g in expert_grads
        ])
        g_qkv = reduce_dense(tail[0])
        g_out = reduce_dense(tail[1])
        g_rt = reduce_dense(tail[2][:, :EXPERTS])
    got = got.reshape(nb * ne * items, cols + width).astype(F32)
    grad_ada = jnp.dot(
        got[:, cols : cols + ada_rows].T, got[:, :cols], precision=lax.Precision.HIGHEST
    )
    return (
        result, grad_tokens, grad_ada, g_qkv, g_out, g_rt, g_sh1, g_sh2, g_e1, g_e2
    )


def solution(mesh):
    placed = (
        P(("batch", "expert"), None),
        P(("batch", "expert"), None),
        P(("batch", "expert")),
        P(("batch", "expert"), None),
        P(("batch", "expert"), None),
        P(),
        P(),
        P(),
        P(),
        P(),
        P(),
        P("expert", None, None),
        P("expert", None, None),
    )
    return jax.shard_map(
        per_device,
        mesh=mesh,
        in_specs=placed,
        out_specs=(
            P(("batch", "expert"), None),
            P(("batch", "expert"), None),
            P("batch", "expert"),
            P("batch", "expert"),
            P("batch", "expert"),
            P("batch", "expert"),
            P("batch", "expert"),
            P("batch", "expert"),
            P("expert", "batch", None),
            P("expert", "batch", None),
        ),
        check_vma=False,
    )
```

```python
import functools
import math

import jax
import jax.numpy as jnp
from jax import lax
from jax.experimental import pallas as pl
from jax.experimental.pallas import tpu as pltpu
from jax.sharding import PartitionSpec as P

D = 768
HEADS = 12
HEAD_DIM = 64
FF = 3072
EXPERTS = 8
SEQ = 256
CAP = 256
LANES = 128
PAIRS = HEADS // 2
H_MLP, G_SHARED, H_ATTN, HEADS_OUT = range(4)

GELU_C = 0.7978845608028654
GELU_A = 0.044715
EPSILON = 1e-06
MASKED = -1000000000.0
LOG2E = math.log2(math.e)
SCALE = HEAD_DIM ** (-0.5)

F32 = jnp.float32
BF16 = jnp.bfloat16
VMEM_LIMIT = 60 * 1024 * 1024
COST = 0.5


def dot_nn(a, b):
    return jnp.dot(a, b, preferred_element_type=F32)


def dot_nt(a, b):
    return lax.dot_general(a, b, (((1,), (1,)), ((), ())), preferred_element_type=F32)


def dot_tn(a, b):
    return lax.dot_general(a, b, (((0,), (0,)), ((), ())), preferred_element_type=F32)


def normalize(values):
    centre = values - jnp.mean(values, -1, keepdims=True)
    factor = lax.rsqrt(jnp.mean(centre * centre, -1, keepdims=True) + EPSILON)
    return (centre * factor, factor)


def norm_back(grad_norm, normed, factor):
    return factor * (
        grad_norm
        - jnp.mean(grad_norm, -1, keepdims=True)
        - normed * jnp.mean(grad_norm * normed, -1, keepdims=True)
    )


def half_masks():
    lane = lax.broadcasted_iota(jnp.int32, (1, LANES), 1)
    low = jnp.where(lane < HEAD_DIM, 1.0, 0.0).astype(BF16)
    return (low, (1.0 - low).astype(BF16))


def whole(shape):
    return pl.BlockSpec(shape, lambda *_: (0,) * len(shape))


def kind_of(which, t):
    return pl.BlockSpec((1, t, D), lambda *_: (which, 0, 0), pipeline_mode=pl.Buffered(1))


def once(shape):
    return pl.BlockSpec(shape, lambda *_: (0,) * len(shape), pipeline_mode=pl.Buffered(1))


ANY = pl.BlockSpec(memory_space=pl.ANY)


class Fetch:
    def __init__(self, pairs, sems):
        self.step = pl.program_id(0)
        self.copies = [
            pltpu.make_async_copy(src, dst, sems.at[i]) for i, (src, dst) in enumerate(pairs)
        ]

        @pl.when(self.step == 0)
        def _():
            for copy in self.copies:
                copy.start()

    def need(self, *which):
        @pl.when(self.step == 0)
        def _():
            for i in which:
                self.copies[i].wait()


def cost(flops, moved):
    return pl.CostEstimate(
        flops=int(COST * flops), bytes_accessed=int(COST * moved), transcendentals=0
    )


def params(**more):
    return pltpu.CompilerParams(vmem_limit_bytes=VMEM_LIMIT, **more)


def attn_forward_kernel(
    len_ref, tok_ref, cot_ref, mod_ref, wqkv_ref, wout_ref,
    qkv_ref, lse_ref, attn_ref, rows_ref,
):
    item = pl.program_id(0)
    mod = mod_ref[0]
    x = tok_ref[...].astype(F32)
    normed, _ = normalize(x)
    h = (normed * (1.0 + mod[1:2]) + mod[0:1]).astype(BF16)
    rows_ref[H_ATTN] = h
    qkv_ref[...] = dot_nn(h, wqkv_ref[...]).astype(BF16)
    key_live = lax.broadcasted_iota(jnp.int32, (1, SEQ), 1) < len_ref[item]
    masks = half_masks()
    lane = lax.broadcasted_iota(jnp.int32, (SEQ, LANES), 1)
    lse_all = jnp.zeros((SEQ, LANES), F32)
    for pair in range(PAIRS):
        at = LANES * pair
        q2 = qkv_ref[:, at : at + LANES]
        k2 = qkv_ref[:, D + at : D + at + LANES]
        v2 = qkv_ref[:, 2 * D + at : 2 * D + at + LANES]
        outs = []
        for half in range(2):
            s = dot_nt(q2 * masks[half], k2) * (SCALE * LOG2E)
            s = jnp.where(key_live, s, MASKED * LOG2E)
            peak = jnp.max(s, -1, keepdims=True)
            e = jnp.exp2(s - peak)
            total = jnp.sum(e, -1, keepdims=True)
            probs = (e * (1.0 / total)).astype(BF16)
            outs.append(dot_nn(probs, v2))
            lse = peak + jnp.log(total) * LOG2E
            lse_all = jnp.where(lane == 2 * pair + half, lse, lse_all)
        rows_ref[HEADS_OUT, :, at : at + LANES] = jnp.where(
            lane < HEAD_DIM, outs[0], outs[1]
        ).astype(BF16)
    lse_ref[...] = lse_all
    attn = dot_nn(rows_ref[HEADS_OUT], wout_ref[...])
    attn_ref[...] = attn
    x_mid = x + mod[2:3] * attn
    normed_mlp, _ = normalize(x_mid)
    rows_ref[H_MLP] = (normed_mlp * (1.0 + mod[4:5]) + mod[3:4]).astype(BF16)
    rows_ref[G_SHARED] = (mod[5:6] * cot_ref[...].astype(F32)).astype(BF16)


def attn_forward(lengths, tokens, cot, mod, wqkv, wout):
    t = tokens.shape[0]
    items = t // SEQ
    row = lambda w: pl.BlockSpec((SEQ, w), lambda i, _: (i, 0))
    return pl.pallas_call(
        attn_forward_kernel,
        name="attn_forward",
        grid_spec=pltpu.PrefetchScalarGridSpec(
            num_scalar_prefetch=1,
            grid=(items,),
            in_specs=[
                row(D), row(D), pl.BlockSpec((1, 6, D), lambda i, _: (i, 0, 0)),
                once((D, 3 * D)), once((D, D)),
            ],
            out_specs=[
                row(3 * D), row(LANES), row(D), pl.BlockSpec((4, SEQ, D), lambda i, _: (0, i, 0)),
            ],
        ),
        out_shape=[
            jax.ShapeDtypeStruct((t, 3 * D), BF16),
            jax.ShapeDtypeStruct((t, LANES), F32),
            jax.ShapeDtypeStruct((t, D), F32),
            jax.ShapeDtypeStruct((4, t, D), BF16),
        ],
        compiler_params=params(),
        cost_estimate=cost(int(8.1e9), int(24e6)),
    )(lengths, tokens, cot, mod, wqkv, wout)


def live_of(len_ref, items, shape, dim):
    tok = lax.broadcasted_iota(jnp.int32, shape, dim)
    limit = jnp.zeros(shape, jnp.int32)
    for i in range(items):
        limit = jnp.where(tok >= i * SEQ, i * SEQ + len_ref[i], limit)
    return tok < limit


def route_kernel(local, len_ref, h_ref, rw_ref, routes_ref, info_ref, line_ref, pos_ref):
    t = h_ref.shape[1]
    items = t // SEQ
    r0, r1 = routes_ref[0:1, :], routes_ref[1:2, :]
    expert = lax.broadcasted_iota(jnp.int32, (EXPERTS, t), 0)
    is0, is1 = expert == r0, expert == r1
    live = live_of(len_ref, items, (1, t), 1)
    hot = (is0 | is1) & live
    before = (
        lax.broadcasted_iota(jnp.int32, (t, t), 1) < lax.broadcasted_iota(jnp.int32, (t, t), 0)
    )
    tri = jnp.where(before, 1.0, 0.0).astype(BF16)
    count = dot_nt(jnp.where(hot, 1.0, 0.0).astype(BF16), tri)
    pos_ref[...] = jnp.where(hot, count, -1.0)
    pick = lambda where, v: jnp.sum(jnp.where(where, v, 0.0), 0, keepdims=True)
    p0, p1 = pick(is0, count), pick(is1, count)
    groups = EXPERTS // local
    block0 = (r0 % local) * groups + r0 // local
    block1 = (r1 % local) * groups + r1 // local
    slot0 = jnp.where(live & (p0 < CAP), block0.astype(F32) * CAP + p0, -1.0)
    slot1 = jnp.where(live & (p1 < CAP), block1.astype(F32) * CAP + p1, -1.0)
    logits = dot_nt(rw_ref[...], h_ref[0])
    l0, l1 = pick(is0, logits), pick(is1, logits)
    top = jnp.maximum(l0, l1)
    e0 = jnp.exp(l0 - top)
    e1 = jnp.exp(l1 - top)
    total = e0 + e1
    line = jnp.zeros((8, t), F32)
    for k, value in enumerate(
        (e0 / total, e1 / total, slot0, slot1, r0.astype(F32), r1.astype(F32))
    ):
        line = jnp.where(expert == k, value, line)
    line_ref[...] = line
    info_ref[:, 0:8] = line.T


def route(local, lengths, rows, rw_t, routes_t):
    t = rows.shape[1]
    return pl.pallas_call(
        functools.partial(route_kernel, local),
        name="route",
        grid=(1,),
        in_specs=[
            pl.BlockSpec(memory_space=pltpu.SMEM), kind_of(H_MLP, t), whole(rw_t.shape),
            whole(routes_t.shape),
        ],
        out_specs=[whole((t, LANES)), whole((8, t)), whole((EXPERTS, t))],
        out_shape=[
            jax.ShapeDtypeStruct((t, LANES), F32),
            jax.ShapeDtypeStruct((8, t), F32),
            jax.ShapeDtypeStruct((EXPERTS, t), F32),
        ],
        compiler_params=params(),
        cost_estimate=cost(int(1e9), int(3e6)),
    )(lengths, rows, rw_t, routes_t)


def dispatch_kernel(local, first, h_ref, cot_ref, mod_ref, line_ref, pos_ref, out_ref):
    t = h_ref.shape[1]
    items = t // SEQ
    expert = pl.program_id(0) * local + first
    pos = pos_ref[pl.ds(expert, 1), :]
    slot = lax.broadcasted_iota(jnp.int32, (CAP, t), 0).astype(F32)
    hot = jnp.where(slot == pos, 1.0, 0.0).astype(BF16)
    out_ref[0, 0] = dot_nn(hot, h_ref[0]).astype(BF16)
    name = expert.astype(F32)
    weight = jnp.where(
        line_ref[4:5] == name, line_ref[0:1], jnp.where(line_ref[5:6] == name, line_ref[1:2], 0.0)
    )
    high = weight.astype(BF16).astype(F32)
    middle = (weight - high).astype(BF16).astype(F32)
    item = (lax.broadcasted_iota(jnp.int32, (1, t), 1) // SEQ).astype(F32)
    lane = lax.broadcasted_iota(jnp.int32, (8, t), 0)
    table = jnp.zeros((8, t), F32)
    for k, value in enumerate((high, middle, weight - high - middle, item)):
        table = jnp.where(lane == k, value, table)
    values = dot_nt(hot, table.astype(BF16))
    weight_col = values[:, 0:1] + values[:, 1:2] + values[:, 2:3]
    item_col = values[:, 3:4]
    gate = jnp.broadcast_to(mod_ref[0, 5:6, :], (CAP, D))
    for i in range(1, items):
        gate = jnp.where(item_col == i, mod_ref[i, 5:6, :], gate)
    grad = gate * dot_nn(hot, cot_ref[...])
    out_ref[0, 1] = (weight_col * grad).astype(BF16)


def dispatch(first, local, rows, cot, mod, line, pos):
    t = rows.shape[1]
    groups = EXPERTS // local
    return pl.pallas_call(
        functools.partial(dispatch_kernel, local, first),
        name="dispatch",
        grid=(groups,),
        in_specs=[
            kind_of(H_MLP, t), once((t, D)), once(mod.shape), once((8, t)), once((EXPERTS, t)),
        ],
        out_specs=pl.BlockSpec((1, 2, CAP, D), lambda g: (g, 0, 0, 0)),
        out_shape=jax.ShapeDtypeStruct((groups, 2, CAP, D), BF16),
        compiler_params=params(),
        cost_estimate=cost(int(3.3e9), int(8e6)),
    )(rows, cot, mod, line, pos)


def gelu_pair(v):
    square = v * v
    gate = 0.5 * jnp.tanh(v * (GELU_C * GELU_A * square + GELU_C)) + 0.5
    act = v * gate
    slope = gate + act * (1.0 - gate) * (6.0 * GELU_C * GELU_A * square + 2.0 * GELU_C)
    return act, slope


def shared_main_kernel(halved, where_ref, x_ref, g_ref, w1_ref, w2_ref, *rest):
    y_ref, gx_ref, act_ref, *gpre_refs, gpre_ref = rest
    x, g = x_ref[0], g_ref[0]
    for f in range(4):
        cols = slice(f * (FF // 4), (f + 1) * (FF // 4))
        act, slope = gelu_pair(dot_nn(x, w1_ref[:, cols]))
        act_ref[:, cols] = act.astype(BF16)
        gpre_ref[:, cols] = (dot_nt(g, w2_ref[cols, :]) * slope).astype(BF16)
    y_ref[...] = dot_nn(act_ref[...], w2_ref[...])
    gx_ref[...] = dot_nt(gpre_ref[...], w1_ref[...])
    if halved:
        first = where_ref[0] == 0
        width = FF // 4
        for x_at in range(2):
            low = gpre_ref[:, 2 * x_at * width : (2 * x_at + 1) * width]
            high = gpre_ref[:, (2 * x_at + 1) * width : (2 * x_at + 2) * width]
            cols = slice(x_at * width, (x_at + 1) * width)
            gpre_refs[0][:, cols] = jnp.where(first, low, high)
            gpre_refs[1][:, cols] = jnp.where(first, high, low)


def shared_main(halved, where, rows, w1, w2):
    t = rows.shape[1]
    chunk = lambda w: pl.BlockSpec((SEQ, w), lambda s, m: (s, 0))
    kind = lambda k: pl.BlockSpec((1, SEQ, D), lambda s, m: (k, s, 0))
    widths = [FF // 2] * 2 if halved else [FF]
    return pl.pallas_call(
        functools.partial(shared_main_kernel, halved),
        name="shared_main",
        grid_spec=pltpu.PrefetchScalarGridSpec(
            num_scalar_prefetch=1,
            grid=(t // SEQ,),
            in_specs=[kind(H_MLP), kind(G_SHARED), once((D, FF)), once((FF, D))],
            out_specs=[chunk(D), chunk(D), chunk(FF)] + [chunk(w) for w in widths],
            scratch_shapes=[pltpu.VMEM((SEQ, FF), BF16)] if halved else [],
        ),
        out_shape=[jax.ShapeDtypeStruct((t, D), F32)] * 2
        + [jax.ShapeDtypeStruct((t, FF), BF16)]
        + [jax.ShapeDtypeStruct((t, w), BF16) for w in widths],
        compiler_params=params(),
        cost_estimate=cost(8 * t * D * FF, int(30e6)),
    )(where, rows, rows, w1, w2)


def store_out_grad(where_ref, part, keep_ref, send_ref):
    first = where_ref[0] == 0
    low, high = part[:, :384], part[:, 384:]
    mine = jnp.where(first, low, high)
    other = jnp.where(first, high, low)
    for k in range(8):
        cols = slice(k * 384, k * 384 + 384)
        keep_ref[0, 0, :, cols] = mine[k * 96 : k * 96 + 96]
        send_ref[0, 0, :, cols] = other[k * 96 : k * 96 + 96]


def expert_first_kernel(fast, where_ref, rows_ref, w1_ref, act_ref, slope_ref, *outs):
    x = rows_ref[:, 0].reshape(-1, D)
    g = rows_ref[:, 1].reshape(-1, D)
    act, slope = gelu_pair(dot_nn(x, w1_ref[0]))
    act = act.astype(BF16)
    act_ref[...] = act
    slope_ref[...] = slope
    part = dot_tn(g, act).astype(BF16)
    if fast:
        store_out_grad(where_ref, part, *outs)
    else:
        outs[0][...] = part


def expert_first(fast, where, rows, w1, which):
    count = rows.shape[0] * CAP
    tile = FF // 4 if fast else FF // 8
    tile_of = lambda s, m: ((s % 2) ^ m[2]) * 2 + ((s // 2) ^ m[1]) if fast else s
    col = pl.BlockSpec((count, tile), lambda s, m: (0, tile_of(s, m)))
    if fast:
        grads = [jax.ShapeDtypeStruct((2, 2, 96, FF), BF16)] * 2
        specs = [pl.BlockSpec((1, 1, 96, FF), lambda s, m: (s // 2, s % 2, 0, 0))] * 2
    else:
        grads = [jax.ShapeDtypeStruct((D, FF), BF16)]
        specs = [pl.BlockSpec((D, tile), lambda s, m: (0, s))]
    act, slope, *grads = pl.pallas_call(
        functools.partial(expert_first_kernel, fast),
        name="expert_first",
        grid_spec=pltpu.PrefetchScalarGridSpec(
            num_scalar_prefetch=1,
            grid=(FF // tile,),
            in_specs=[
                once(rows.shape), pl.BlockSpec((1, D, tile), lambda s, m: (which, 0, tile_of(s, m))),
            ],
            out_specs=[col, col] + specs,
        ),
        out_shape=[
            jax.ShapeDtypeStruct((count, FF), BF16), jax.ShapeDtypeStruct((count, FF), F32),
        ] + grads,
        compiler_params=params(),
        cost_estimate=cost(4 * count * D * FF, int(30e6)),
    )(where, rows, w1)
    return act, slope, grads


def expert_second_kernel(rows_ref, act_ref, slope_ref, w1_ref, w2_ref, out_ref, gpre_ref):
    g = rows_ref[0, 1]
    for f in range(4):
        cols = slice(f * (FF // 4), (f + 1) * (FF // 4))
        gpre_ref[:, cols] = (dot_nt(g, w2_ref[0, cols, :]) * slope_ref[:, cols]).astype(BF16)
    out_ref[0, 0] = dot_nn(act_ref[...], w2_ref[0]).astype(BF16)
    out_ref[0, 1] = dot_nt(gpre_ref[...], w1_ref[0]).astype(BF16)


def expert_second(rows, act, slope, w1, w2, which):
    count = rows.shape[0] * CAP
    chunk = lambda w: pl.BlockSpec((CAP, w), lambda s: (s, 0))
    pair = pl.BlockSpec((1, 2, CAP, D), lambda s: (s, 0, 0, 0))
    weight = lambda r, c: pl.BlockSpec(
        (1, r, c), lambda s: (which, 0, 0), pipeline_mode=pl.Buffered(1)
    )
    return pl.pallas_call(
        expert_second_kernel,
        name="expert_second",
        grid=(rows.shape[0],),
        in_specs=[pair, chunk(FF), chunk(FF), weight(D, FF), weight(FF, D)],
        out_specs=[pair, chunk(FF)],
        out_shape=[
            jax.ShapeDtypeStruct(rows.shape, BF16), jax.ShapeDtypeStruct((count, FF), BF16),
        ],
        compiler_params=params(),
        cost_estimate=cost(6 * count * D * FF, int(40e6)),
    )(rows, act, slope, w1, w2)


def weight_grad_kernel(fast, where_ref, a_ref, b_ref, *outs):
    part = dot_tn(a_ref[...].reshape(-1, D), b_ref[...]).astype(BF16)
    if not fast:
        outs[0][...] = part
        return
    first = where_ref[0] == 0
    keep_ref, send_ref = outs
    for z in range(4):
        low = part[192 * z : 192 * z + 96]
        high = part[192 * z + 96 : 192 * z + 192]
        at = (z % 2) ^ where_ref[1], (z // 2) ^ where_ref[2]
        keep_ref[at] = jnp.where(first, low, high)
        send_ref[at] = jnp.where(first, high, low)


def weight_grad(fast, where, a, kind, b):
    rows = b.shape[0]
    tile = FF // 4
    if a.ndim == 3:
        a_spec = kind_of(kind, rows)
    else:
        a_spec = pl.BlockSpec(
            (a.shape[0], 1, CAP, D), lambda s, m: (0, kind, 0, 0), pipeline_mode=pl.Buffered(1)
        )
    if fast:
        outs = [jax.ShapeDtypeStruct((2, 2, 96, FF), BF16)] * 2
        specs = [pl.BlockSpec((2, 2, 96, tile), lambda s, m: (0, 0, 0, s))] * 2
    else:
        outs = [jax.ShapeDtypeStruct((D, FF), BF16)]
        specs = [pl.BlockSpec((D, tile), lambda s, m: (0, s))]
    return pl.pallas_call(
        functools.partial(weight_grad_kernel, fast),
        name="weight_grad",
        grid_spec=pltpu.PrefetchScalarGridSpec(
            num_scalar_prefetch=1,
            grid=(FF // tile,),
            in_specs=[a_spec, pl.BlockSpec((rows, tile), lambda s, m: (0, s))],
            out_specs=specs,
        ),
        out_shape=outs,
        compiler_params=params(),
        cost_estimate=cost(2 * rows * D * FF, int(13e6)),
    )(where, a, b)


def batch_at(where_ref, b):
    z = b // 2
    return (b % 2) ^ where_ref[2], (z % 2) ^ where_ref[3], (z // 2) ^ where_ref[4]


def own_columns(where_ref, v, width):
    low = jnp.concatenate([v[:, :width], v[:, 2 * width : 3 * width]], 1)
    high = jnp.concatenate([v[:, width : 2 * width], v[:, 3 * width :]], 1)
    return jnp.where(where_ref[0] == 0, low, high)


def shared_grad_kernel(
    where_ref, mine_ref, peer_ref, gpre_ref, gpre_peer_ref, act_ref, act_peer_ref,
    keep_ref, send_ref, g_scr, part_scr,
):
    step = pl.program_id(0)
    side = step // 2
    rows = act_ref.shape[0]

    @pl.when(step == 0)
    def _():
        g_scr[:rows] = own_columns(where_ref, mine_ref[G_SHARED], D // 4)
        g_scr[rows:] = own_columns(where_ref, peer_ref[G_SHARED], D // 4)

    @pl.when(step % 2 == 0)
    def _():
        part = (
            dot_tn(mine_ref[H_MLP], gpre_ref[...]) + dot_tn(peer_ref[H_MLP], gpre_peer_ref[...])
        ).astype(BF16)
        for b in range(8):
            part_scr[batch_at(where_ref, b)] = part[b * 96 : b * 96 + 96]
        for s, ref in ((0, keep_ref), (1, send_ref)):
            @pl.when(side == s)
            def _():
                ref[:, :, :, 0] = part_scr[...]

    both = (dot_tn(g_scr[:rows], act_ref[...]) + dot_tn(g_scr[rows:], act_peer_ref[...])).astype(BF16)
    first = where_ref[1] == 0
    low, high = both[:192], both[192:]
    for ref, v in ((keep_ref, jnp.where(first, low, high)), (send_ref, jnp.where(first, high, low))):
        for h in range(2):
            for y in range(2):
                at = batch_at(where_ref, 2 * step + y)
                ref[(*at, 1, slice(None), slice(h * 384, h * 384 + 384))] = v[
                    h * 96 : h * 96 + 96, y * 384 : y * 384 + 384
                ]


def shared_grad(where, mine, peer, gpre, gpre_peer, act, act_peer):
    rows = act.shape[0]
    gpre_spec = pl.BlockSpec((rows, FF // 4), lambda s, m: (0, (s // 2) ^ m[1]))
    act_spec = pl.BlockSpec((rows, FF // 4), lambda s, m: (0, s))
    stack = pl.BlockSpec((2, rows, D), lambda s, m: (0, 0, 0), pipeline_mode=pl.Buffered(1))
    shape = (2, 2, 2, 2, 96, D)
    return pl.pallas_call(
        shared_grad_kernel,
        name="shared_grad",
        grid_spec=pltpu.PrefetchScalarGridSpec(
            num_scalar_prefetch=1,
            grid=(4,),
            in_specs=[stack, stack, gpre_spec, gpre_spec, act_spec, act_spec],
            out_specs=[once(shape)] * 2,
            scratch_shapes=[
                pltpu.VMEM((2 * rows, D // 2), BF16), pltpu.VMEM((2, 2, 2, 96, D), BF16),
            ],
        ),
        out_shape=[jax.ShapeDtypeStruct(shape, BF16)] * 2,
        compiler_params=params(),
        cost_estimate=cost(4 * rows * D * FF, int(25e6)),
    )(where, mine, peer, gpre, gpre_peer, act, act_peer)


def backward_kernel(
    local, fast, first_item, len_ref, where_ref, tok_ref, cot_ref, mod_ref, attn_ref, qkv_ref, lse_ref,
    sres_ref, gsh_ref, info_ref, wqkv_ref, wout_ref, rwt_ref, *rest,
):
    back = rest[:local]
    if fast:
        out_ref, gtok_ref, gmod_ref, own_ref, other_ref, gq_ref = rest[-6:]
    else:
        out_ref, gtok_ref, gmod_ref, own_ref, gq_ref = rest[-5:]
    item = pl.program_id(0) + first_item
    slots = EXPERTS * CAP
    each = slots // local

    def pick(hot, kind):
        value = None
        for j in range(local):
            rows = back[j][:, kind].reshape(each, D)
            term = dot_nn(hot[:, j * each : (j + 1) * each], rows)
            value = term if value is None else value + term
        return value

    mod = mod_ref[0]
    x = tok_ref[...].astype(F32)
    cot = cot_ref[...].astype(F32)
    attn = attn_ref[...]
    x_mid = x + mod[2:3] * attn
    normed_mlp, factor_mlp = normalize(x_mid)
    gw0, gw1 = info_ref[:, 0:1], info_ref[:, 1:2]
    slot = lax.broadcasted_iota(jnp.int32, (SEQ, slots), 1).astype(F32)
    hot0 = jnp.where(slot == info_ref[:, 2:3], 1.0, 0.0).astype(BF16)
    hot1 = jnp.where(slot == info_ref[:, 3:4], 1.0, 0.0).astype(BF16)
    row0 = pick(hot0, 0)
    row1 = pick(hot1, 0)
    mlp_out = sres_ref[...] + (gw0 * row0 + gw1 * row1)
    out_ref[...] = (x_mid + mod[5:6] * mlp_out).astype(BF16)
    gmod_ref[0, 5:6, :] = jnp.sum(cot * mlp_out, 0, keepdims=True)
    grad_mlp = mod[5:6] * cot
    gate0 = jnp.sum(grad_mlp * row0, -1, keepdims=True)
    gate1 = jnp.sum(grad_mlp * row1, -1, keepdims=True)
    weighted = gw0 * gate0 + gw1 * gate1
    sel0 = gw0 * (gate0 - weighted)
    sel1 = gw1 * (gate1 - weighted)
    high0 = sel0.astype(BF16).astype(F32)
    high1 = sel1.astype(BF16).astype(F32)
    lane = lax.broadcasted_iota(jnp.int32, (SEQ, LANES), 1)
    lane_f = lane.astype(F32)
    r0, r1 = info_ref[:, 4:5], info_ref[:, 5:6]
    g_logits = (
        jnp.where(lane_f == r0, high0, 0.0)
        + jnp.where(lane_f == r1, high1, 0.0)
        + jnp.where(lane_f == r0 + EXPERTS, sel0 - high0, 0.0)
        + jnp.where(lane_f == r1 + EXPERTS, sel1 - high1, 0.0)
    ).astype(BF16)
    grad_h = gsh_ref[...] + pick(hot0 + hot1, 1) + dot_nn(g_logits, rwt_ref[...])
    gmod_ref[0, 3:4, :] = jnp.sum(grad_h, 0, keepdims=True)
    gmod_ref[0, 4:5, :] = jnp.sum(grad_h * normed_mlp, 0, keepdims=True)
    grad_mid = cot + norm_back(grad_h * (1.0 + mod[4:5]), normed_mlp, factor_mlp)
    gmod_ref[0, 2:3, :] = jnp.sum(grad_mid * attn, 0, keepdims=True)
    g_attn = (mod[2:3] * grad_mid).astype(BF16)
    g_heads = dot_nt(g_attn, wout_ref[...]).astype(BF16)
    key_live = lax.broadcasted_iota(jnp.int32, (1, SEQ), 1) < len_ref[item]
    masks = half_masks()
    low_half = lane < HEAD_DIM
    for pair in range(PAIRS):
        at = LANES * pair
        q2 = qkv_ref[:, at : at + LANES]
        k2 = qkv_ref[:, D + at : D + at + LANES]
        v2 = qkv_ref[:, 2 * D + at : 2 * D + at + LANES]
        gh2 = g_heads[:, at : at + LANES]
        dq, dk, dv = [], [], []
        for half in range(2):
            head = 2 * pair + half
            s = dot_nt(q2 * masks[half], k2) * (SCALE * LOG2E)
            s = jnp.where(key_live, s, MASKED * LOG2E)
            probs = jnp.exp2(s - lse_ref[:, head : head + 1])
            g_probs = dot_nt(gh2 * masks[half], v2)
            spread = jnp.sum(probs * g_probs, -1, keepdims=True)
            g_scores = (probs * (g_probs - spread)).astype(BF16)
            dq.append(dot_nn(g_scores, k2))
            dk.append(dot_tn(g_scores, q2))
            dv.append(dot_tn(probs.astype(BF16), gh2))
        gq_ref[:, at : at + LANES] = (jnp.where(low_half, dq[0], dq[1]) * SCALE).astype(BF16)
        gq_ref[:, D + at : D + at + LANES] = (
            jnp.where(low_half, dk[0], dk[1]) * SCALE
        ).astype(BF16)
        gq_ref[:, 2 * D + at : 2 * D + at + LANES] = jnp.where(low_half, dv[0], dv[1]).astype(BF16)
    g_qkv = gq_ref[...]
    g_h = dot_nt(g_qkv, wqkv_ref[...])
    normed, factor = normalize(x)
    gmod_ref[0, 0:1, :] = jnp.sum(g_h, 0, keepdims=True)
    gmod_ref[0, 1:2, :] = jnp.sum(g_h * normed, 0, keepdims=True)
    gmod_ref[0, 6:8, :] = jnp.zeros((2, D), F32)
    gtok_ref[...] = grad_mid + norm_back(g_h * (1.0 + mod[1:2]), normed, factor)
    if fast:
        sides = [
            jnp.concatenate(
                [
                    g_qkv[:, 576 * c : 576 * c + 576],
                    g_qkv[:, 1152 + 576 * c : 1728 + 576 * c],
                    g_attn[:, 192 * c : 192 * c + 192],
                    g_attn[:, 384 + 192 * c : 576 + 192 * c],
                ], 1
            )
            for c in range(2)
        ]
        first = where_ref[0] == 0
        own_ref[:, : 2 * D] = jnp.where(first, sides[0], sides[1])
        own_ref[:, 2 * D :] = g_logits
        other_ref[:, : 2 * D] = jnp.where(first, sides[1], sides[0])
        other_ref[:, 2 * D :] = g_logits
    else:
        own_ref[:, : 3 * D] = g_qkv
        own_ref[:, 3 * D : 4 * D] = g_attn
        own_ref[:, 4 * D :] = g_logits


def backward(
    fast, where, first_item, count, so_far, lengths, tokens, cot, mod, attn, qkv, lse, sres, gsh,
    info, back, wqkv, wout, rwt,
):
    t = tokens.shape[0]
    row = lambda w: pl.BlockSpec((SEQ, w), lambda i, *_: (i + first_item, 0))
    new = lambda w: pl.BlockSpec((SEQ, w), lambda i, *_: (i, 0))
    local = len(back)
    item_block = lambda r: pl.BlockSpec((1, r, D), lambda i, *_: (i + first_item, 0, 0))
    known = 14 + local
    widths = [2 * D + LANES] * 2 if fast else [4 * D + LANES]
    outs = pl.pallas_call(
        functools.partial(backward_kernel, local, fast, first_item),
        name="backward",
        grid_spec=pltpu.PrefetchScalarGridSpec(
            num_scalar_prefetch=2,
            grid=(count,),
            in_specs=[
                row(D), row(D), item_block(6),
                row(D), row(3 * D), row(LANES), row(D), row(D), row(LANES),
                once((D, 3 * D)), once((D, D)), once((LANES, D)),
            ] + [once(b.shape) for b in back]
            + [pl.BlockSpec(memory_space=pl.ANY)] * len(so_far),
            out_specs=[row(D), row(D), item_block(8)] + [new(w) for w in widths],
            scratch_shapes=[
                pltpu.VMEM((SEQ, 3 * D), BF16),
            ],
        ),
        out_shape=[
            jax.ShapeDtypeStruct((t, D), BF16),
            jax.ShapeDtypeStruct((t, D), F32),
            jax.ShapeDtypeStruct((t // SEQ, 8, D), F32),
        ] + [jax.ShapeDtypeStruct((count * SEQ, w), BF16) for w in widths],
        input_output_aliases={known + i: i for i in range(len(so_far))},
        compiler_params=params(),
        cost_estimate=cost(int(5e9) * count, int(7e6) * count),
    )(
        lengths, where, tokens, cot, mod, attn, qkv, lse, sres, gsh, info, wqkv, wout, rwt,
        *back, *so_far,
    )
    return (outs[:3], *outs[3:])


def tail_grad_kernel(fast, many, where_ref, *refs):
    count = 2 if fast else 3
    *refs, stack_ref, grad_ref, sems = refs
    stacks, grads, outs = refs[:many], refs[many:-count], refs[-count:]
    width = 3 * D // 2 if fast else 3 * D
    each = len(grads) // many
    t = stacks[0].shape[1]
    pairs = []
    for i, stack in enumerate(stacks):
        start = i * t
        pairs.append((stack.at[G_SHARED + 1 :], stack_ref.at[i, : 4 - G_SHARED - 1]))
        pairs.append((stack.at[H_MLP], stack_ref.at[i, 2]))
        for g in grads[i * each : (i + 1) * each]:
            pairs.append((g, grad_ref.at[pl.ds(start, g.shape[0])]))
            start += g.shape[0]
    fetch = Fetch(pairs, sems)
    d_qkv = d_out = d_router = None
    for i in range(many):
        fetch.need(*range((2 + each) * i, (2 + each) * (i + 1)))
        rows = slice(i * t, (i + 1) * t)
        terms = (
            dot_tn(stack_ref[i, 0], grad_ref[rows, :width]),
            dot_tn(stack_ref[i, 1], grad_ref[rows, width : width + width // 3]),
            dot_tn(stack_ref[i, 2], grad_ref[rows, width + width // 3 :]),
        )
        if i:
            terms = (d_qkv + terms[0], d_out + terms[1], d_router + terms[2])
        d_qkv, d_out, d_router = terms
    d_qkv, d_out = d_qkv.astype(BF16), d_out.astype(BF16)
    d_router = (d_router + pltpu.roll(d_router, LANES - EXPERTS, 1)).astype(BF16)
    if not fast:
        outs[0][...], outs[1][...], outs[2][...] = d_qkv, d_out, d_router
        return
    first = where_ref[1] == 0
    low, high = [
        jnp.concatenate(
            [d_qkv[:, 576 * x : 576 * x + 576], d_out[:, 192 * x : 192 * x + 192], d_router], 1
        )
        for x in range(2)
    ]
    for ref, v in ((outs[0], jnp.where(first, low, high)), (outs[1], jnp.where(first, high, low))):
        for b in range(8):
            ref[batch_at(where_ref, b)] = v[b * 96 : b * 96 + 96]


def tail_grad(fast, where, stacks, grads):
    if fast:
        outs = [jax.ShapeDtypeStruct((2, 2, 2, 96, D + LANES), BF16)] * 2
    else:
        outs = [
            jax.ShapeDtypeStruct((D, 3 * D), BF16),
            jax.ShapeDtypeStruct((D, D), BF16),
            jax.ShapeDtypeStruct((D, LANES), BF16),
        ]
    t, wide = stacks[0].shape[1], grads[0].shape[1]
    many = len(stacks)
    return pl.pallas_call(
        functools.partial(tail_grad_kernel, fast, len(stacks)),
        name="tail_grad",
        grid_spec=pltpu.PrefetchScalarGridSpec(
            num_scalar_prefetch=1,
            grid=(1,),
            in_specs=[ANY] * (len(stacks) + len(grads)),
            out_specs=[once(o.shape) for o in outs],
            scratch_shapes=[
                pltpu.VMEM((many, 3, t, D), BF16),
                pltpu.VMEM((many * t, wide), BF16),
                pltpu.SemaphoreType.DMA((2 * many + len(grads),)),
            ],
        ),
        out_shape=outs,
        compiler_params=params(),
        cost_estimate=cost(int(5e9), int(20e6)),
    )(where, *stacks, *grads)


def after(value, *others):
    if not others:
        return value
    return lax.optimization_barrier((value,) + tuple(others))[0]


def group_sum(blocks, axis, groups):
    width = len(groups[0])
    if width == 1:
        return blocks[0].astype(F32)
    low = blocks.astype(BF16)
    if width == 2:
        place = jnp.zeros((), jnp.int32)
        index = lax.axis_index(axis)
        for g in groups:
            place = jnp.where(index == g[1], 1, place)
        sent = lax.dynamic_index_in_dim(low, 1 - place, 0, keepdims=False)
        kept = lax.dynamic_index_in_dim(low, place, 0, keepdims=False)
        return pair_sum(kept, sent, axis, groups)
    got = lax.all_to_all(low, axis, 0, 0, tiled=True, axis_index_groups=groups)
    return jnp.sum(got.astype(F32), 0)


def pair_sum(kept, sent, axis, groups):
    pairs = [(g[0], g[1]) for g in groups] + [(g[1], g[0]) for g in groups]
    got = lax.ppermute(sent, axis, pairs)
    return kept.astype(F32) + got.astype(F32)


def swap(value, axis, bit):
    size = lax.axis_size(axis)
    return lax.ppermute(value.astype(BF16), axis, [(i, i ^ bit) for i in range(size)])


class Chain:
    def __init__(self, keep, send, stages):
        self.terms, self.send, self.stages = [keep], send, list(stages)

    def total(self):
        value = self.terms[0].astype(F32)
        for term in self.terms[1:]:
            value = value + term.astype(F32)
        return value

    def step(self, send_after=(), take_after=()):
        axis, bit = self.stages.pop(0)
        got = swap(after(self.send, *send_after), axis, bit)
        self.got = after(got, *take_after)
        self.terms.append(self.got)
        if self.stages:
            terms = self.terms
            self.terms = [v[1] for v in terms]
            self.send = self.total().astype(BF16)
            self.terms = [v[0] for v in terms]
        else:
            self.send = None
        return self


def inner_groups(outer, inner):
    return [[o * inner + i for i in range(inner)] for o in range(outer)]


def outer_groups(outer, inner):
    return [[o * inner + i for o in range(outer)] for i in range(inner)]


def batch_split(size):
    inner = 2 if size <= 8 else 8
    return (size // inner, inner)


def reduce_batch(blocks):
    outer, inner = batch_split(lax.axis_size("batch"))
    v = jnp.moveaxis(blocks.reshape((outer, inner) + blocks.shape[1:]), 1, 0)
    v = group_sum(v, "batch", inner_groups(outer, inner))
    return group_sum(v, "batch", outer_groups(outer, inner))


def reduce_expert(blocks):
    outer, inner = lax.axis_size("expert") // 2, 2
    v = jnp.moveaxis(blocks.reshape((outer, inner) + blocks.shape[1:]), 1, 0)
    v = group_sum(v, "expert", inner_groups(outer, inner))
    return group_sum(v, "expert", outer_groups(outer, inner))


def reduce_dense(grad):
    nb, ne = lax.axis_size("batch"), lax.axis_size("expert")
    r, c = grad.shape
    v = jnp.transpose(grad.reshape(r, ne, c // ne), (1, 0, 2))
    v = reduce_expert(v)
    return reduce_batch(v.reshape(nb, r // nb, c // ne))


def reduce_local(grad):
    nb = lax.axis_size("batch")
    r, c = grad.shape
    return reduce_batch(grad.reshape(nb, r // nb, c))


def all_pairs(parts):
    nb, ne = parts.shape[:2]
    return lax.all_to_all(
        parts.reshape((nb * ne,) + parts.shape[2:]), ("batch", "expert"), 0, 0, tiled=True
    )


def per_device(
    tokens, condition, lengths, routes, cotangent, ada_weight, qkv_weight, out_weight,
    router_weight, shared_in, shared_out, expert_in, expert_out,
):
    nb, ne = lax.axis_size("batch"), lax.axis_size("expert")
    local = expert_in.shape[0]
    items = lengths.shape[0]
    t = tokens.shape[0]
    fast = nb == 8 and ne == 4 and local == 2
    batch, expert = lax.axis_index("batch"), lax.axis_index("expert")
    z_at = batch // 2
    where = jnp.stack([expert % 2, expert // 2, batch % 2, z_at % 2, z_at // 2]).astype(jnp.int32)
    y_at = jnp.stack([batch % 2, z_at % 2, z_at // 2]).astype(jnp.int32)

    act = jax.nn.silu(condition.astype(F32)).astype(BF16)
    mod = dot_nn(act, ada_weight).reshape(items, 6, D)
    rw_t = router_weight.T
    rwt_pad = jnp.pad(jnp.concatenate([rw_t, rw_t], 0), ((0, LANES - 2 * EXPERTS), (0, 0)))

    qkv, lse, attn, rows = attn_forward(lengths, tokens, cotangent, mod, qkv_weight, out_weight)
    if fast:
        peer_rows = swap(rows, "expert", 1)
    info, line, pos = route(local, lengths, rows, rw_t, routes.T)
    sent, received = [], []
    rows_now = rows
    for j in range(local):
        sent.append(dispatch(j, local, rows_now, cotangent, mod, line, pos))
        rows_now = after(rows, sent[j])
    sres, gsh, s_act, *s_gpre = shared_main(fast, where, rows_now, shared_in, shared_out)
    if fast:
        peer_act = swap(s_act, "expert", 1)
        peer_gpre = swap(s_gpre[1], "expert", 1)
    for j in range(local):
        part = after(sent[j], sres) if j else sent[j]
        received.append(lax.all_to_all(part, "expert", 0, 0, tiled=True))
    expert_stages = [("batch", 1), ("batch", 2), ("batch", 4)]
    dense_stages = [("expert", 2), ("batch", 1), ("batch", 2), ("batch", 4)]
    back, expert_grads, chains = [], [], []
    last = (sres,)
    for j in range(local):
        rows_in = after(received[j], *last)
        act_e, slope_e, d2 = expert_first(fast, y_at, rows_in, expert_in, j)
        waits = [d2[0], *back]
        if fast:
            chains.append(Chain(*d2, expert_stages))
            if j == 1:
                chains[0].step(take_after=d2[:1])
                waits.append(chains[0].send)
        rows_in = after(rows_in, *waits)
        y, gpre_e = expert_second(rows_in, act_e, slope_e, expert_in, expert_out, j)
        back.append(lax.all_to_all(y, "expert", 0, 0, tiled=True))
        d1 = weight_grad(fast, y_at, after(rows_in, y), 0, gpre_e)
        last = (d1[0],)
        if fast:
            chains.append(Chain(*d1, expert_stages))
        expert_grads.append((d1, d2))
    if fast:
        out0, in0, out1, in1 = chains
        now = last
        out0.step(take_after=now)
        in0.step(take_after=now)
        rows_now = after(rows, *last, out0.send, in0.send)
        shared_grads = shared_grad(where, rows_now, peer_rows, s_gpre[0], peer_gpre, s_act, peer_act)
        shared_sum = Chain(*shared_grads, dense_stages)
    else:
        rows_now = after(rows, *last)
        shared_grads = (
            weight_grad(fast, y_at, rows_now, H_MLP, s_gpre[0])[0],
            weight_grad(fast, y_at, rows_now, G_SHARED, s_act)[0],
        )
    pieces = [items // 2, items - items // 2]
    tok = after(tokens, shared_grads[0])
    outs, own, other = [], [], []
    done = 0
    for piece, per in enumerate(pieces):
        outs, first, *second = backward(
            fast, where, done, per, outs, lengths, tok, cotangent, mod, attn, qkv, lse,
            sres, gsh, info, back, qkv_weight, out_weight, rwt_pad,
        )
        done += per
        own.append(first)
        now = (outs[0],)
        tok = after(tokens, *now)
        if fast:
            other.append(swap(second[0], "expert", 1))
            if piece == 0:
                out0.step(take_after=now)
                in0.step(take_after=now)
                out1.step(take_after=now)
                tok = after(tok, out0.terms[-1], in0.send, out1.send)
            else:
                in1.step(take_after=now)
                in0.step(take_after=now)
                out1.step(take_after=now)
                shared_sum.step(take_after=now)
                where_now = after(where, in0.got, out1.got, in1.send, shared_sum.got)
    result, grad_tokens, grad_mod = outs
    stacks = [rows, peer_rows] if fast else [rows]
    if not fast:
        where_now = where
    tail = tail_grad(fast, where_now, stacks, own + other)

    cols, ada_rows = 6 * D // ne, D // nb
    mod_parts = grad_mod[:, :6].reshape(items, ne, cols).astype(BF16)
    mod_parts = jnp.transpose(mod_parts, (1, 0, 2))
    act_parts = jnp.transpose(act.reshape(items, nb, ada_rows), (1, 0, 2))
    act_parts = jnp.pad(act_parts, ((0, 0), (0, 0), (0, -ada_rows % LANES)))
    width = act_parts.shape[-1]
    parts = jnp.concatenate(
        [
            jnp.broadcast_to(mod_parts[None], (nb, ne, items, cols)),
            jnp.broadcast_to(act_parts[:, None], (nb, ne, items, width)),
        ],
        -1,
    )
    got = all_pairs(after(parts, tail[0]))

    if fast:
        def unfold(v):
            return v.reshape(96, 8, 384).transpose(2, 1, 0).reshape(384, D)

        tail_sum = Chain(*tail, dense_stages)
        token = tail[0]
        for chain in (
            out1, in1, shared_sum, tail_sum, in1, shared_sum, tail_sum, shared_sum, tail_sum,
            tail_sum,
        ):
            chain.step(take_after=(token,))
            token = chain.send if chain.stages else chain.terms[-1]
        tl = tail_sum.total()
        got = after(got, token)
        assert not any(c.stages for c in (in0, in1, out0, out1, shared_sum, tail_sum))
        sh = shared_sum.total()
        g_sh1 = sh[0]
        g_sh2 = sh[1].reshape(96, 2, 384).transpose(2, 1, 0).reshape(384, 192)
        g_e1 = jnp.stack([in0.total(), in1.total()])
        g_e2 = jnp.stack([unfold(out0.total()), unfold(out1.total())])
        g_qkv = tl[:, :576]
        g_out = tl[:, 576:768]
        g_rt = lax.dynamic_slice_in_dim(tl[:, 768:776], 2 * expert, 2, 1)
    else:
        def flipped(grad):
            r, c = grad.shape
            return jnp.transpose(reduce_dense_t(grad))

        def reduce_dense_t(grad):
            r, c = grad.shape
            v = reduce_expert(grad.reshape(ne, r // ne, c))
            v = jnp.transpose(v.reshape(r // ne, nb, c // nb), (1, 0, 2))
            return reduce_batch(v)

        g_sh1 = reduce_dense(shared_grads[0])
        g_sh2 = flipped(shared_grads[1])
        g_e1 = jnp.stack([reduce_local(g[0][0]) for g in expert_grads])
        g_e2 = jnp.stack([
            jnp.transpose(reduce_batch(jnp.transpose(g[1][0].reshape(D, nb, FF // nb), (1, 0, 2))))
            for g in expert_grads
        ])
        g_qkv = reduce_dense(tail[0])
        g_out = reduce_dense(tail[1])
        g_rt = reduce_dense(tail[2][:, :EXPERTS])
    got = got.reshape(nb * ne * items, cols + width).astype(F32)
    grad_ada = jnp.dot(
        got[:, cols : cols + ada_rows].T, got[:, :cols], precision=lax.Precision.HIGHEST
    )
    return (
        result, grad_tokens, grad_ada, g_qkv, g_out, g_rt, g_sh1, g_sh2, g_e1, g_e2
    )


def solution(mesh):
    placed = (
        P(("batch", "expert"), None),
        P(("batch", "expert"), None),
        P(("batch", "expert")),
        P(("batch", "expert"), None),
        P(("batch", "expert"), None),
        P(),
        P(),
        P(),
        P(),
        P(),
        P(),
        P("expert", None, None),
        P("expert", None, None),
    )
    return jax.shard_map(
        per_device,
        mesh=mesh,
        in_specs=placed,
        out_specs=(
            P(("batch", "expert"), None),
            P(("batch", "expert"), None),
            P("batch", "expert"),
            P("batch", "expert"),
            P("batch", "expert"),
            P("batch", "expert"),
            P("batch", "expert"),
            P("batch", "expert"),
            P("expert", "batch", None),
            P("expert", "batch", None),
        ),
        check_vma=False,
    )
```

```python
import functools
import math

import jax
import jax.numpy as jnp
from jax import lax
from jax.experimental import pallas as pl
from jax.experimental.pallas import tpu as pltpu
from jax.sharding import PartitionSpec as P

D = 768
HEADS = 12
HEAD_DIM = 64
FF = 3072
EXPERTS = 8
SEQ = 256
CAP = 256
LANES = 128
PAIRS = HEADS // 2
H_MLP, G_SHARED, H_ATTN, HEADS_OUT = range(4)

GELU_C = 0.7978845608028654
GELU_A = 0.044715
EPSILON = 1e-06
MASKED = -1000000000.0
LOG2E = math.log2(math.e)
SCALE = HEAD_DIM ** (-0.5)

F32 = jnp.float32
BF16 = jnp.bfloat16
VMEM_LIMIT = 60 * 1024 * 1024
COST = 0.5


def dot_nn(a, b):
    return jnp.dot(a, b, preferred_element_type=F32)


def dot_nt(a, b):
    return lax.dot_general(a, b, (((1,), (1,)), ((), ())), preferred_element_type=F32)


def dot_tn(a, b):
    return lax.dot_general(a, b, (((0,), (0,)), ((), ())), preferred_element_type=F32)


def normalize(values):
    centre = values - jnp.mean(values, -1, keepdims=True)
    factor = lax.rsqrt(jnp.mean(centre * centre, -1, keepdims=True) + EPSILON)
    return (centre * factor, factor)


def norm_back(grad_norm, normed, factor):
    return factor * (
        grad_norm
        - jnp.mean(grad_norm, -1, keepdims=True)
        - normed * jnp.mean(grad_norm * normed, -1, keepdims=True)
    )


def half_masks():
    lane = lax.broadcasted_iota(jnp.int32, (1, LANES), 1)
    low = jnp.where(lane < HEAD_DIM, 1.0, 0.0).astype(BF16)
    return (low, (1.0 - low).astype(BF16))


def whole(shape):
    return pl.BlockSpec(shape, lambda *_: (0,) * len(shape))


def kind_of(which, t):
    return pl.BlockSpec((1, t, D), lambda *_: (which, 0, 0), pipeline_mode=pl.Buffered(1))


def once(shape):
    return pl.BlockSpec(shape, lambda *_: (0,) * len(shape), pipeline_mode=pl.Buffered(1))


ANY = pl.BlockSpec(memory_space=pl.ANY)


class Fetch:
    def __init__(self, pairs, sems):
        self.step = pl.program_id(0)
        self.copies = [
            pltpu.make_async_copy(src, dst, sems.at[i]) for i, (src, dst) in enumerate(pairs)
        ]

        @pl.when(self.step == 0)
        def _():
            for copy in self.copies:
                copy.start()

    def need(self, *which):
        @pl.when(self.step == 0)
        def _():
            for i in which:
                self.copies[i].wait()


def cost(flops, moved):
    return pl.CostEstimate(
        flops=int(COST * flops), bytes_accessed=int(COST * moved), transcendentals=0
    )


def params(**more):
    return pltpu.CompilerParams(vmem_limit_bytes=VMEM_LIMIT, **more)


def attn_forward_kernel(
    len_ref, tok_ref, cot_ref, mod_ref, wqkv_ref, wout_ref,
    qkv_ref, lse_ref, attn_ref, rows_ref,
):
    item = pl.program_id(0)
    mod = mod_ref[0]
    x = tok_ref[...].astype(F32)
    normed, _ = normalize(x)
    h = (normed * (1.0 + mod[1:2]) + mod[0:1]).astype(BF16)
    rows_ref[H_ATTN] = h
    qkv_ref[...] = dot_nn(h, wqkv_ref[...]).astype(BF16)
    key_live = lax.broadcasted_iota(jnp.int32, (1, SEQ), 1) < len_ref[item]
    masks = half_masks()
    lane = lax.broadcasted_iota(jnp.int32, (SEQ, LANES), 1)
    lse_all = jnp.zeros((SEQ, LANES), F32)
    for pair in range(PAIRS):
        at = LANES * pair
        q2 = qkv_ref[:, at : at + LANES]
        k2 = qkv_ref[:, D + at : D + at + LANES]
        v2 = qkv_ref[:, 2 * D + at : 2 * D + at + LANES]
        outs = []
        for half in range(2):
            s = dot_nt(q2 * masks[half], k2) * (SCALE * LOG2E)
            s = jnp.where(key_live, s, MASKED * LOG2E)
            peak = jnp.max(s, -1, keepdims=True)
            e = jnp.exp2(s - peak)
            total = jnp.sum(e, -1, keepdims=True)
            probs = (e * (1.0 / total)).astype(BF16)
            outs.append(dot_nn(probs, v2))
            lse = peak + jnp.log(total) * LOG2E
            lse_all = jnp.where(lane == 2 * pair + half, lse, lse_all)
        rows_ref[HEADS_OUT, :, at : at + LANES] = jnp.where(
            lane < HEAD_DIM, outs[0], outs[1]
        ).astype(BF16)
    lse_ref[...] = lse_all
    attn = dot_nn(rows_ref[HEADS_OUT], wout_ref[...])
    attn_ref[...] = attn
    x_mid = x + mod[2:3] * attn
    normed_mlp, _ = normalize(x_mid)
    rows_ref[H_MLP] = (normed_mlp * (1.0 + mod[4:5]) + mod[3:4]).astype(BF16)
    rows_ref[G_SHARED] = (mod[5:6] * cot_ref[...].astype(F32)).astype(BF16)


def attn_forward(lengths, tokens, cot, mod, wqkv, wout):
    t = tokens.shape[0]
    items = t // SEQ
    row = lambda w: pl.BlockSpec((SEQ, w), lambda i, _: (i, 0))
    return pl.pallas_call(
        attn_forward_kernel,
        name="attn_forward",
        grid_spec=pltpu.PrefetchScalarGridSpec(
            num_scalar_prefetch=1,
            grid=(items,),
            in_specs=[
                row(D), row(D), pl.BlockSpec((1, 6, D), lambda i, _: (i, 0, 0)),
                once((D, 3 * D)), once((D, D)),
            ],
            out_specs=[
                row(3 * D), row(LANES), row(D), pl.BlockSpec((4, SEQ, D), lambda i, _: (0, i, 0)),
            ],
        ),
        out_shape=[
            jax.ShapeDtypeStruct((t, 3 * D), BF16),
            jax.ShapeDtypeStruct((t, LANES), F32),
            jax.ShapeDtypeStruct((t, D), F32),
            jax.ShapeDtypeStruct((4, t, D), BF16),
        ],
        compiler_params=params(),
        cost_estimate=cost(int(8.1e9), int(24e6)),
    )(lengths, tokens, cot, mod, wqkv, wout)


def live_of(len_ref, items, shape, dim):
    tok = lax.broadcasted_iota(jnp.int32, shape, dim)
    limit = jnp.zeros(shape, jnp.int32)
    for i in range(items):
        limit = jnp.where(tok >= i * SEQ, i * SEQ + len_ref[i], limit)
    return tok < limit


def route_kernel(local, len_ref, h_ref, rw_ref, routes_ref, info_ref, line_ref, pos_ref):
    t = h_ref.shape[1]
    items = t // SEQ
    r0, r1 = routes_ref[0:1, :], routes_ref[1:2, :]
    expert = lax.broadcasted_iota(jnp.int32, (EXPERTS, t), 0)
    is0, is1 = expert == r0, expert == r1
    live = live_of(len_ref, items, (1, t), 1)
    hot = (is0 | is1) & live
    before = (
        lax.broadcasted_iota(jnp.int32, (t, t), 1) < lax.broadcasted_iota(jnp.int32, (t, t), 0)
    )
    tri = jnp.where(before, 1.0, 0.0).astype(BF16)
    count = dot_nt(jnp.where(hot, 1.0, 0.0).astype(BF16), tri)
    pos_ref[...] = jnp.where(hot, count, -1.0)
    pick = lambda where, v: jnp.sum(jnp.where(where, v, 0.0), 0, keepdims=True)
    p0, p1 = pick(is0, count), pick(is1, count)
    groups = EXPERTS // local
    block0 = (r0 % local) * groups + r0 // local
    block1 = (r1 % local) * groups + r1 // local
    slot0 = jnp.where(live & (p0 < CAP), block0.astype(F32) * CAP + p0, -1.0)
    slot1 = jnp.where(live & (p1 < CAP), block1.astype(F32) * CAP + p1, -1.0)
    logits = dot_nt(rw_ref[...], h_ref[0])
    l0, l1 = pick(is0, logits), pick(is1, logits)
    top = jnp.maximum(l0, l1)
    e0 = jnp.exp(l0 - top)
    e1 = jnp.exp(l1 - top)
    total = e0 + e1
    line = jnp.zeros((8, t), F32)
    for k, value in enumerate(
        (e0 / total, e1 / total, slot0, slot1, r0.astype(F32), r1.astype(F32))
    ):
        line = jnp.where(expert == k, value, line)
    line_ref[...] = line
    info_ref[:, 0:8] = line.T


def route(local, lengths, rows, rw_t, routes_t):
    t = rows.shape[1]
    return pl.pallas_call(
        functools.partial(route_kernel, local),
        name="route",
        grid=(1,),
        in_specs=[
            pl.BlockSpec(memory_space=pltpu.SMEM), kind_of(H_MLP, t), whole(rw_t.shape),
            whole(routes_t.shape),
        ],
        out_specs=[whole((t, LANES)), whole((8, t)), whole((EXPERTS, t))],
        out_shape=[
            jax.ShapeDtypeStruct((t, LANES), F32),
            jax.ShapeDtypeStruct((8, t), F32),
            jax.ShapeDtypeStruct((EXPERTS, t), F32),
        ],
        compiler_params=params(),
        cost_estimate=cost(int(1e9), int(3e6)),
    )(lengths, rows, rw_t, routes_t)


def dispatch_kernel(local, first, h_ref, cot_ref, mod_ref, line_ref, pos_ref, out_ref):
    t = h_ref.shape[1]
    items = t // SEQ
    expert = pl.program_id(0) * local + first
    pos = pos_ref[pl.ds(expert, 1), :]
    slot = lax.broadcasted_iota(jnp.int32, (CAP, t), 0).astype(F32)
    hot = jnp.where(slot == pos, 1.0, 0.0).astype(BF16)
    out_ref[0, 0] = dot_nn(hot, h_ref[0]).astype(BF16)
    name = expert.astype(F32)
    weight = jnp.where(
        line_ref[4:5] == name, line_ref[0:1], jnp.where(line_ref[5:6] == name, line_ref[1:2], 0.0)
    )
    high = weight.astype(BF16).astype(F32)
    middle = (weight - high).astype(BF16).astype(F32)
    item = (lax.broadcasted_iota(jnp.int32, (1, t), 1) // SEQ).astype(F32)
    lane = lax.broadcasted_iota(jnp.int32, (8, t), 0)
    table = jnp.zeros((8, t), F32)
    for k, value in enumerate((high, middle, weight - high - middle, item)):
        table = jnp.where(lane == k, value, table)
    values = dot_nt(hot, table.astype(BF16))
    weight_col = values[:, 0:1] + values[:, 1:2] + values[:, 2:3]
    item_col = values[:, 3:4]
    gate = jnp.broadcast_to(mod_ref[0, 5:6, :], (CAP, D))
    for i in range(1, items):
        gate = jnp.where(item_col == i, mod_ref[i, 5:6, :], gate)
    grad = gate * dot_nn(hot, cot_ref[...])
    out_ref[0, 1] = (weight_col * grad).astype(BF16)


def dispatch(first, local, rows, cot, mod, line, pos):
    t = rows.shape[1]
    groups = EXPERTS // local
    return pl.pallas_call(
        functools.partial(dispatch_kernel, local, first),
        name="dispatch",
        grid=(groups,),
        in_specs=[
            kind_of(H_MLP, t), once((t, D)), once(mod.shape), once((8, t)), once((EXPERTS, t)),
        ],
        out_specs=pl.BlockSpec((1, 2, CAP, D), lambda g: (g, 0, 0, 0)),
        out_shape=jax.ShapeDtypeStruct((groups, 2, CAP, D), BF16),
        compiler_params=params(),
        cost_estimate=cost(int(3.3e9), int(8e6)),
    )(rows, cot, mod, line, pos)


def gelu_pair(v):
    square = v * v
    gate = 0.5 * jnp.tanh(v * (GELU_C * GELU_A * square + GELU_C)) + 0.5
    act = v * gate
    slope = gate + act * (1.0 - gate) * (6.0 * GELU_C * GELU_A * square + 2.0 * GELU_C)
    return act, slope


def shared_main_kernel(halved, where_ref, x_ref, g_ref, w1_ref, w2_ref, *rest):
    y_ref, gx_ref, act_ref, *gpre_refs, gpre_ref = rest
    x, g = x_ref[0], g_ref[0]
    for f in range(4):
        cols = slice(f * (FF // 4), (f + 1) * (FF // 4))
        act, slope = gelu_pair(dot_nn(x, w1_ref[:, cols]))
        act_ref[:, cols] = act.astype(BF16)
        gpre_ref[:, cols] = (dot_nt(g, w2_ref[cols, :]) * slope).astype(BF16)
    y_ref[...] = dot_nn(act_ref[...], w2_ref[...])
    gx_ref[...] = dot_nt(gpre_ref[...], w1_ref[...])
    if halved:
        first = where_ref[0] == 0
        width = FF // 4
        for x_at in range(2):
            low = gpre_ref[:, 2 * x_at * width : (2 * x_at + 1) * width]
            high = gpre_ref[:, (2 * x_at + 1) * width : (2 * x_at + 2) * width]
            cols = slice(x_at * width, (x_at + 1) * width)
            gpre_refs[0][:, cols] = jnp.where(first, low, high)
            gpre_refs[1][:, cols] = jnp.where(first, high, low)


def shared_main(halved, where, rows, w1, w2):
    t = rows.shape[1]
    chunk = lambda w: pl.BlockSpec((SEQ, w), lambda s, m: (s, 0))
    kind = lambda k: pl.BlockSpec((1, SEQ, D), lambda s, m: (k, s, 0))
    widths = [FF // 2] * 2 if halved else [FF]
    return pl.pallas_call(
        functools.partial(shared_main_kernel, halved),
        name="shared_main",
        grid_spec=pltpu.PrefetchScalarGridSpec(
            num_scalar_prefetch=1,
            grid=(t // SEQ,),
            in_specs=[kind(H_MLP), kind(G_SHARED), once((D, FF)), once((FF, D))],
            out_specs=[chunk(D), chunk(D), chunk(FF)] + [chunk(w) for w in widths],
            scratch_shapes=[pltpu.VMEM((SEQ, FF), BF16)] if halved else [],
        ),
        out_shape=[jax.ShapeDtypeStruct((t, D), F32)] * 2
        + [jax.ShapeDtypeStruct((t, FF), BF16)]
        + [jax.ShapeDtypeStruct((t, w), BF16) for w in widths],
        compiler_params=params(),
        cost_estimate=cost(8 * t * D * FF, int(30e6)),
    )(where, rows, rows, w1, w2)


def store_out_grad(where_ref, part, keep_ref, send_ref):
    first = where_ref[0] == 0
    low, high = part[:, :384], part[:, 384:]
    mine = jnp.where(first, low, high)
    other = jnp.where(first, high, low)
    for k in range(8):
        cols = slice(k * 384, k * 384 + 384)
        keep_ref[0, 0, :, cols] = mine[k * 96 : k * 96 + 96]
        send_ref[0, 0, :, cols] = other[k * 96 : k * 96 + 96]


def expert_first_kernel(fast, where_ref, rows_ref, w1_ref, act_ref, slope_ref, *outs):
    x = rows_ref[:, 0].reshape(-1, D)
    g = rows_ref[:, 1].reshape(-1, D)
    act, slope = gelu_pair(dot_nn(x, w1_ref[0]))
    act = act.astype(BF16)
    act_ref[...] = act
    slope_ref[...] = slope
    part = dot_tn(g, act).astype(BF16)
    if fast:
        store_out_grad(where_ref, part, *outs)
    else:
        outs[0][...] = part


def expert_first(fast, where, rows, w1, which):
    count = rows.shape[0] * CAP
    tile = FF // 4 if fast else FF // 8
    tile_of = lambda s, m: ((s % 2) ^ m[2]) * 2 + ((s // 2) ^ m[1]) if fast else s
    col = pl.BlockSpec((count, tile), lambda s, m: (0, tile_of(s, m)))
    if fast:
        grads = [jax.ShapeDtypeStruct((2, 2, 96, FF), BF16)] * 2
        specs = [pl.BlockSpec((1, 1, 96, FF), lambda s, m: (s // 2, s % 2, 0, 0))] * 2
    else:
        grads = [jax.ShapeDtypeStruct((D, FF), BF16)]
        specs = [pl.BlockSpec((D, tile), lambda s, m: (0, s))]
    act, slope, *grads = pl.pallas_call(
        functools.partial(expert_first_kernel, fast),
        name="expert_first",
        grid_spec=pltpu.PrefetchScalarGridSpec(
            num_scalar_prefetch=1,
            grid=(FF // tile,),
            in_specs=[
                once(rows.shape), pl.BlockSpec((1, D, tile), lambda s, m: (which, 0, tile_of(s, m))),
            ],
            out_specs=[col, col] + specs,
        ),
        out_shape=[
            jax.ShapeDtypeStruct((count, FF), BF16), jax.ShapeDtypeStruct((count, FF), F32),
        ] + grads,
        compiler_params=params(),
        cost_estimate=cost(4 * count * D * FF, int(30e6)),
    )(where, rows, w1)
    return act, slope, grads


def expert_second_kernel(rows_ref, act_ref, slope_ref, w1_ref, w2_ref, out_ref, gpre_ref):
    g = rows_ref[0, 1]
    for f in range(4):
        cols = slice(f * (FF // 4), (f + 1) * (FF // 4))
        gpre_ref[:, cols] = (dot_nt(g, w2_ref[0, cols, :]) * slope_ref[:, cols]).astype(BF16)
    out_ref[0, 0] = dot_nn(act_ref[...], w2_ref[0]).astype(BF16)
    out_ref[0, 1] = dot_nt(gpre_ref[...], w1_ref[0]).astype(BF16)


def expert_second(rows, act, slope, w1, w2, which):
    count = rows.shape[0] * CAP
    chunk = lambda w: pl.BlockSpec((CAP, w), lambda s: (s, 0))
    pair = pl.BlockSpec((1, 2, CAP, D), lambda s: (s, 0, 0, 0))
    weight = lambda r, c: pl.BlockSpec(
        (1, r, c), lambda s: (which, 0, 0), pipeline_mode=pl.Buffered(1)
    )
    return pl.pallas_call(
        expert_second_kernel,
        name="expert_second",
        grid=(rows.shape[0],),
        in_specs=[pair, chunk(FF), chunk(FF), weight(D, FF), weight(FF, D)],
        out_specs=[pair, chunk(FF)],
        out_shape=[
            jax.ShapeDtypeStruct(rows.shape, BF16), jax.ShapeDtypeStruct((count, FF), BF16),
        ],
        compiler_params=params(),
        cost_estimate=cost(6 * count * D * FF, int(40e6)),
    )(rows, act, slope, w1, w2)


def weight_grad_kernel(fast, where_ref, a_ref, b_ref, *outs):
    part = dot_tn(a_ref[...].reshape(-1, D), b_ref[...]).astype(BF16)
    if not fast:
        outs[0][...] = part
        return
    first = where_ref[0] == 0
    keep_ref, send_ref = outs
    for z in range(4):
        low = part[192 * z : 192 * z + 96]
        high = part[192 * z + 96 : 192 * z + 192]
        at = (z % 2) ^ where_ref[1], (z // 2) ^ where_ref[2]
        keep_ref[at] = jnp.where(first, low, high)
        send_ref[at] = jnp.where(first, high, low)


def weight_grad(fast, where, a, kind, b):
    rows = b.shape[0]
    tile = FF // 4
    if a.ndim == 3:
        a_spec = kind_of(kind, rows)
    else:
        a_spec = pl.BlockSpec(
            (a.shape[0], 1, CAP, D), lambda s, m: (0, kind, 0, 0), pipeline_mode=pl.Buffered(1)
        )
    if fast:
        outs = [jax.ShapeDtypeStruct((2, 2, 96, FF), BF16)] * 2
        specs = [pl.BlockSpec((2, 2, 96, tile), lambda s, m: (0, 0, 0, s))] * 2
    else:
        outs = [jax.ShapeDtypeStruct((D, FF), BF16)]
        specs = [pl.BlockSpec((D, tile), lambda s, m: (0, s))]
    return pl.pallas_call(
        functools.partial(weight_grad_kernel, fast),
        name="weight_grad",
        grid_spec=pltpu.PrefetchScalarGridSpec(
            num_scalar_prefetch=1,
            grid=(FF // tile,),
            in_specs=[a_spec, pl.BlockSpec((rows, tile), lambda s, m: (0, s))],
            out_specs=specs,
        ),
        out_shape=outs,
        compiler_params=params(),
        cost_estimate=cost(2 * rows * D * FF, int(13e6)),
    )(where, a, b)


def batch_at(where_ref, b):
    z = b // 2
    return (b % 2) ^ where_ref[2], (z % 2) ^ where_ref[3], (z // 2) ^ where_ref[4]


def own_columns(where_ref, v, width):
    low = jnp.concatenate([v[:, :width], v[:, 2 * width : 3 * width]], 1)
    high = jnp.concatenate([v[:, width : 2 * width], v[:, 3 * width :]], 1)
    return jnp.where(where_ref[0] == 0, low, high)


def shared_grad_kernel(
    where_ref, mine_ref, peer_ref, gpre_ref, gpre_peer_ref, act_ref, act_peer_ref,
    keep_ref, send_ref, g_scr, part_scr,
):
    step = pl.program_id(0)
    side = step // 2
    rows = act_ref.shape[0]

    @pl.when(step == 0)
    def _():
        g_scr[:rows] = own_columns(where_ref, mine_ref[G_SHARED], D // 4)
        g_scr[rows:] = own_columns(where_ref, peer_ref[G_SHARED], D // 4)

    @pl.when(step % 2 == 0)
    def _():
        part = (
            dot_tn(mine_ref[H_MLP], gpre_ref[...]) + dot_tn(peer_ref[H_MLP], gpre_peer_ref[...])
        ).astype(BF16)
        for b in range(8):
            part_scr[batch_at(where_ref, b)] = part[b * 96 : b * 96 + 96]
        for s, ref in ((0, keep_ref), (1, send_ref)):
            @pl.when(side == s)
            def _():
                ref[:, :, :, 0] = part_scr[...]

    both = (dot_tn(g_scr[:rows], act_ref[...]) + dot_tn(g_scr[rows:], act_peer_ref[...])).astype(BF16)
    first = where_ref[1] == 0
    low, high = both[:192], both[192:]
    for ref, v in ((keep_ref, jnp.where(first, low, high)), (send_ref, jnp.where(first, high, low))):
        for h in range(2):
            for y in range(2):
                at = batch_at(where_ref, 2 * step + y)
                ref[(*at, 1, slice(None), slice(h * 384, h * 384 + 384))] = v[
                    h * 96 : h * 96 + 96, y * 384 : y * 384 + 384
                ]


def shared_grad(where, mine, peer, gpre, gpre_peer, act, act_peer):
    rows = act.shape[0]
    gpre_spec = pl.BlockSpec((rows, FF // 4), lambda s, m: (0, (s // 2) ^ m[1]))
    act_spec = pl.BlockSpec((rows, FF // 4), lambda s, m: (0, s))
    stack = pl.BlockSpec((2, rows, D), lambda s, m: (0, 0, 0), pipeline_mode=pl.Buffered(1))
    shape = (2, 2, 2, 2, 96, D)
    return pl.pallas_call(
        shared_grad_kernel,
        name="shared_grad",
        grid_spec=pltpu.PrefetchScalarGridSpec(
            num_scalar_prefetch=1,
            grid=(4,),
            in_specs=[stack, stack, gpre_spec, gpre_spec, act_spec, act_spec],
            out_specs=[once(shape)] * 2,
            scratch_shapes=[
                pltpu.VMEM((2 * rows, D // 2), BF16), pltpu.VMEM((2, 2, 2, 96, D), BF16),
            ],
        ),
        out_shape=[jax.ShapeDtypeStruct(shape, BF16)] * 2,
        compiler_params=params(),
        cost_estimate=cost(4 * rows * D * FF, int(25e6)),
    )(where, mine, peer, gpre, gpre_peer, act, act_peer)


def backward_kernel(
    local, fast, first_item, len_ref, where_ref, tok_ref, cot_ref, mod_ref, attn_ref, qkv_ref, lse_ref,
    sres_ref, gsh_ref, info_ref, wqkv_ref, wout_ref, rwt_ref, *rest,
):
    back = rest[:local]
    if fast:
        out_ref, gtok_ref, gmod_ref, own_ref, other_ref, gq_ref = rest[-6:]
    else:
        out_ref, gtok_ref, gmod_ref, own_ref, gq_ref = rest[-5:]
    item = pl.program_id(0) + first_item
    slots = EXPERTS * CAP
    each = slots // local

    def pick(hot, kind):
        value = None
        for j in range(local):
            rows = back[j][:, kind].reshape(each, D)
            term = dot_nn(hot[:, j * each : (j + 1) * each], rows)
            value = term if value is None else value + term
        return value

    mod = mod_ref[0]
    x = tok_ref[...].astype(F32)
    cot = cot_ref[...].astype(F32)
    attn = attn_ref[...]
    x_mid = x + mod[2:3] * attn
    normed_mlp, factor_mlp = normalize(x_mid)
    gw0, gw1 = info_ref[:, 0:1], info_ref[:, 1:2]
    slot = lax.broadcasted_iota(jnp.int32, (SEQ, slots), 1).astype(F32)
    hot0 = jnp.where(slot == info_ref[:, 2:3], 1.0, 0.0).astype(BF16)
    hot1 = jnp.where(slot == info_ref[:, 3:4], 1.0, 0.0).astype(BF16)
    row0 = pick(hot0, 0)
    row1 = pick(hot1, 0)
    mlp_out = sres_ref[...] + (gw0 * row0 + gw1 * row1)
    out_ref[...] = (x_mid + mod[5:6] * mlp_out).astype(BF16)
    gmod_ref[0, 5:6, :] = jnp.sum(cot * mlp_out, 0, keepdims=True)
    grad_mlp = mod[5:6] * cot
    gate0 = jnp.sum(grad_mlp * row0, -1, keepdims=True)
    gate1 = jnp.sum(grad_mlp * row1, -1, keepdims=True)
    weighted = gw0 * gate0 + gw1 * gate1
    sel0 = gw0 * (gate0 - weighted)
    sel1 = gw1 * (gate1 - weighted)
    high0 = sel0.astype(BF16).astype(F32)
    high1 = sel1.astype(BF16).astype(F32)
    lane = lax.broadcasted_iota(jnp.int32, (SEQ, LANES), 1)
    lane_f = lane.astype(F32)
    r0, r1 = info_ref[:, 4:5], info_ref[:, 5:6]
    g_logits = (
        jnp.where(lane_f == r0, high0, 0.0)
        + jnp.where(lane_f == r1, high1, 0.0)
        + jnp.where(lane_f == r0 + EXPERTS, sel0 - high0, 0.0)
        + jnp.where(lane_f == r1 + EXPERTS, sel1 - high1, 0.0)
    ).astype(BF16)
    grad_h = gsh_ref[...] + pick(hot0 + hot1, 1) + dot_nn(g_logits, rwt_ref[...])
    gmod_ref[0, 3:4, :] = jnp.sum(grad_h, 0, keepdims=True)
    gmod_ref[0, 4:5, :] = jnp.sum(grad_h * normed_mlp, 0, keepdims=True)
    grad_mid = cot + norm_back(grad_h * (1.0 + mod[4:5]), normed_mlp, factor_mlp)
    gmod_ref[0, 2:3, :] = jnp.sum(grad_mid * attn, 0, keepdims=True)
    g_attn = (mod[2:3] * grad_mid).astype(BF16)
    g_heads = dot_nt(g_attn, wout_ref[...]).astype(BF16)
    key_live = lax.broadcasted_iota(jnp.int32, (1, SEQ), 1) < len_ref[item]
    masks = half_masks()
    low_half = lane < HEAD_DIM
    for pair in range(PAIRS):
        at = LANES * pair
        q2 = qkv_ref[:, at : at + LANES]
        k2 = qkv_ref[:, D + at : D + at + LANES]
        v2 = qkv_ref[:, 2 * D + at : 2 * D + at + LANES]
        gh2 = g_heads[:, at : at + LANES]
        dq, dk, dv = [], [], []
        for half in range(2):
            head = 2 * pair + half
            s = dot_nt(q2 * masks[half], k2) * (SCALE * LOG2E)
            s = jnp.where(key_live, s, MASKED * LOG2E)
            probs = jnp.exp2(s - lse_ref[:, head : head + 1])
            g_probs = dot_nt(gh2 * masks[half], v2)
            spread = jnp.sum(probs * g_probs, -1, keepdims=True)
            g_scores = (probs * (g_probs - spread)).astype(BF16)
            dq.append(dot_nn(g_scores, k2))
            dk.append(dot_tn(g_scores, q2))
            dv.append(dot_tn(probs.astype(BF16), gh2))
        gq_ref[:, at : at + LANES] = (jnp.where(low_half, dq[0], dq[1]) * SCALE).astype(BF16)
        gq_ref[:, D + at : D + at + LANES] = (
            jnp.where(low_half, dk[0], dk[1]) * SCALE
        ).astype(BF16)
        gq_ref[:, 2 * D + at : 2 * D + at + LANES] = jnp.where(low_half, dv[0], dv[1]).astype(BF16)
    g_qkv = gq_ref[...]
    g_h = dot_nt(g_qkv, wqkv_ref[...])
    normed, factor = normalize(x)
    gmod_ref[0, 0:1, :] = jnp.sum(g_h, 0, keepdims=True)
    gmod_ref[0, 1:2, :] = jnp.sum(g_h * normed, 0, keepdims=True)
    gmod_ref[0, 6:8, :] = jnp.zeros((2, D), F32)
    gtok_ref[...] = grad_mid + norm_back(g_h * (1.0 + mod[1:2]), normed, factor)
    if fast:
        sides = [
            jnp.concatenate(
                [
                    g_qkv[:, 576 * c : 576 * c + 576],
                    g_qkv[:, 1152 + 576 * c : 1728 + 576 * c],
                    g_attn[:, 192 * c : 192 * c + 192],
                    g_attn[:, 384 + 192 * c : 576 + 192 * c],
                ], 1
            )
            for c in range(2)
        ]
        first = where_ref[0] == 0
        own_ref[:, : 2 * D] = jnp.where(first, sides[0], sides[1])
        own_ref[:, 2 * D :] = g_logits
        other_ref[:, : 2 * D] = jnp.where(first, sides[1], sides[0])
        other_ref[:, 2 * D :] = g_logits
    else:
        own_ref[:, : 3 * D] = g_qkv
        own_ref[:, 3 * D : 4 * D] = g_attn
        own_ref[:, 4 * D :] = g_logits


def backward(
    fast, where, first_item, count, so_far, lengths, tokens, cot, mod, attn, qkv, lse, sres, gsh,
    info, back, wqkv, wout, rwt,
):
    t = tokens.shape[0]
    row = lambda w: pl.BlockSpec((SEQ, w), lambda i, *_: (i + first_item, 0))
    new = lambda w: pl.BlockSpec((SEQ, w), lambda i, *_: (i, 0))
    local = len(back)
    item_block = lambda r: pl.BlockSpec((1, r, D), lambda i, *_: (i + first_item, 0, 0))
    known = 14 + local
    widths = [2 * D + LANES] * 2 if fast else [4 * D + LANES]
    outs = pl.pallas_call(
        functools.partial(backward_kernel, local, fast, first_item),
        name="backward",
        grid_spec=pltpu.PrefetchScalarGridSpec(
            num_scalar_prefetch=2,
            grid=(count,),
            in_specs=[
                row(D), row(D), item_block(6),
                row(D), row(3 * D), row(LANES), row(D), row(D), row(LANES),
                once((D, 3 * D)), once((D, D)), once((LANES, D)),
            ] + [once(b.shape) for b in back]
            + [pl.BlockSpec(memory_space=pl.ANY)] * len(so_far),
            out_specs=[row(D), row(D), item_block(8)] + [new(w) for w in widths],
            scratch_shapes=[
                pltpu.VMEM((SEQ, 3 * D), BF16),
            ],
        ),
        out_shape=[
            jax.ShapeDtypeStruct((t, D), BF16),
            jax.ShapeDtypeStruct((t, D), F32),
            jax.ShapeDtypeStruct((t // SEQ, 8, D), F32),
        ] + [jax.ShapeDtypeStruct((count * SEQ, w), BF16) for w in widths],
        input_output_aliases={known + i: i for i in range(len(so_far))},
        compiler_params=params(),
        cost_estimate=cost(int(5e9) * count, int(7e6) * count),
    )(
        lengths, where, tokens, cot, mod, attn, qkv, lse, sres, gsh, info, wqkv, wout, rwt,
        *back, *so_far,
    )
    return (outs[:3], *outs[3:])


def tail_grad_kernel(fast, many, where_ref, *refs):
    count = 3
    *refs, stack_ref, grad_ref, sems = refs
    stacks, grads, outs = refs[:many], refs[many:-count], refs[-count:]
    width = 3 * D // 2 if fast else 3 * D
    each = len(grads) // many
    t = stacks[0].shape[1]
    pairs = []
    for i, stack in enumerate(stacks):
        start = i * t
        pairs.append((stack.at[G_SHARED + 1 :], stack_ref.at[i, : 4 - G_SHARED - 1]))
        pairs.append((stack.at[H_MLP], stack_ref.at[i, 2]))
        for g in grads[i * each : (i + 1) * each]:
            pairs.append((g, grad_ref.at[pl.ds(start, g.shape[0])]))
            start += g.shape[0]
    fetch = Fetch(pairs, sems)
    d_qkv = d_out = d_router = None
    for i in range(many):
        fetch.need(*range((2 + each) * i, (2 + each) * (i + 1)))
        rows = slice(i * t, (i + 1) * t)
        terms = (
            dot_tn(stack_ref[i, 0], grad_ref[rows, :width]),
            dot_tn(stack_ref[i, 1], grad_ref[rows, width : width + width // 3]),
            dot_tn(stack_ref[i, 2], grad_ref[rows, width + width // 3 :]),
        )
        if i:
            terms = (d_qkv + terms[0], d_out + terms[1], d_router)
        d_qkv, d_out, d_router = terms
    d_qkv, d_out = d_qkv.astype(BF16), d_out.astype(BF16)
    d_router = (d_router + pltpu.roll(d_router, LANES - EXPERTS, 1)).astype(BF16)
    if not fast:
        outs[0][...], outs[1][...], outs[2][...] = d_qkv, d_out, d_router
        return
    outs[2][...] = d_router
    first = where_ref[1] == 0
    low, high = [
        jnp.concatenate(
            [d_qkv[:, 576 * x : 576 * x + 576], d_out[:, 192 * x : 192 * x + 192]], 1
        )
        for x in range(2)
    ]
    for ref, v in ((outs[0], jnp.where(first, low, high)), (outs[1], jnp.where(first, high, low))):
        for b in range(8):
            ref[batch_at(where_ref, b)] = v[b * 96 : b * 96 + 96]


def tail_grad(fast, where, stacks, grads):
    if fast:
        outs = [jax.ShapeDtypeStruct((2, 2, 2, 96, D), BF16)] * 2
        outs.append(jax.ShapeDtypeStruct((D, LANES), BF16))
    else:
        outs = [
            jax.ShapeDtypeStruct((D, 3 * D), BF16),
            jax.ShapeDtypeStruct((D, D), BF16),
            jax.ShapeDtypeStruct((D, LANES), BF16),
        ]
    t, wide = stacks[0].shape[1], grads[0].shape[1]
    many = len(stacks)
    return pl.pallas_call(
        functools.partial(tail_grad_kernel, fast, len(stacks)),
        name="tail_grad",
        grid_spec=pltpu.PrefetchScalarGridSpec(
            num_scalar_prefetch=1,
            grid=(1,),
            in_specs=[ANY] * (len(stacks) + len(grads)),
            out_specs=[once(o.shape) for o in outs],
            scratch_shapes=[
                pltpu.VMEM((many, 3, t, D), BF16),
                pltpu.VMEM((many * t, wide), BF16),
                pltpu.SemaphoreType.DMA((2 * many + len(grads),)),
            ],
        ),
        out_shape=outs,
        compiler_params=params(),
        cost_estimate=cost(int(5e9), int(20e6)),
    )(where, *stacks, *grads)


def after(value, *others):
    if not others:
        return value
    return lax.optimization_barrier((value,) + tuple(others))[0]


def group_sum(blocks, axis, groups):
    width = len(groups[0])
    if width == 1:
        return blocks[0].astype(F32)
    low = blocks.astype(BF16)
    if width == 2:
        place = jnp.zeros((), jnp.int32)
        index = lax.axis_index(axis)
        for g in groups:
            place = jnp.where(index == g[1], 1, place)
        sent = lax.dynamic_index_in_dim(low, 1 - place, 0, keepdims=False)
        kept = lax.dynamic_index_in_dim(low, place, 0, keepdims=False)
        return pair_sum(kept, sent, axis, groups)
    got = lax.all_to_all(low, axis, 0, 0, tiled=True, axis_index_groups=groups)
    return jnp.sum(got.astype(F32), 0)


def pair_sum(kept, sent, axis, groups):
    pairs = [(g[0], g[1]) for g in groups] + [(g[1], g[0]) for g in groups]
    got = lax.ppermute(sent, axis, pairs)
    return kept.astype(F32) + got.astype(F32)


def swap(value, axis, bit):
    size = lax.axis_size(axis)
    return lax.ppermute(value.astype(BF16), axis, [(i, i ^ bit) for i in range(size)])


class Chain:
    def __init__(self, keep, send, stages):
        self.terms, self.send, self.stages = [keep], send, list(stages)

    def total(self):
        value = self.terms[0].astype(F32)
        for term in self.terms[1:]:
            value = value + term.astype(F32)
        return value

    def step(self, send_after=(), take_after=()):
        axis, bit = self.stages.pop(0)
        got = swap(after(self.send, *send_after), axis, bit)
        self.got = after(got, *take_after)
        self.terms.append(self.got)
        if self.stages:
            terms = self.terms
            self.terms = [v[1] for v in terms]
            self.send = self.total().astype(BF16)
            self.terms = [v[0] for v in terms]
        else:
            self.send = None
        return self


def inner_groups(outer, inner):
    return [[o * inner + i for i in range(inner)] for o in range(outer)]


def outer_groups(outer, inner):
    return [[o * inner + i for o in range(outer)] for i in range(inner)]


def batch_split(size):
    inner = 2 if size <= 8 else 8
    return (size // inner, inner)


def reduce_batch(blocks):
    outer, inner = batch_split(lax.axis_size("batch"))
    v = jnp.moveaxis(blocks.reshape((outer, inner) + blocks.shape[1:]), 1, 0)
    v = group_sum(v, "batch", inner_groups(outer, inner))
    return group_sum(v, "batch", outer_groups(outer, inner))


def reduce_expert(blocks):
    outer, inner = lax.axis_size("expert") // 2, 2
    v = jnp.moveaxis(blocks.reshape((outer, inner) + blocks.shape[1:]), 1, 0)
    v = group_sum(v, "expert", inner_groups(outer, inner))
    return group_sum(v, "expert", outer_groups(outer, inner))


def reduce_dense(grad):
    nb, ne = lax.axis_size("batch"), lax.axis_size("expert")
    r, c = grad.shape
    v = jnp.transpose(grad.reshape(r, ne, c // ne), (1, 0, 2))
    v = reduce_expert(v)
    return reduce_batch(v.reshape(nb, r // nb, c // ne))


def reduce_local(grad):
    nb = lax.axis_size("batch")
    r, c = grad.shape
    return reduce_batch(grad.reshape(nb, r // nb, c))


def all_pairs(parts):
    nb, ne = parts.shape[:2]
    return lax.all_to_all(
        parts.reshape((nb * ne,) + parts.shape[2:]), ("batch", "expert"), 0, 0, tiled=True
    )


def per_device(
    tokens, condition, lengths, routes, cotangent, ada_weight, qkv_weight, out_weight,
    router_weight, shared_in, shared_out, expert_in, expert_out,
):
    nb, ne = lax.axis_size("batch"), lax.axis_size("expert")
    local = expert_in.shape[0]
    items = lengths.shape[0]
    t = tokens.shape[0]
    fast = nb == 8 and ne == 4 and local == 2
    batch, expert = lax.axis_index("batch"), lax.axis_index("expert")
    z_at = batch // 2
    where = jnp.stack([expert % 2, expert // 2, batch % 2, z_at % 2, z_at // 2]).astype(jnp.int32)
    y_at = jnp.stack([batch % 2, z_at % 2, z_at // 2]).astype(jnp.int32)

    act = jax.nn.silu(condition.astype(F32)).astype(BF16)
    mod = dot_nn(act, ada_weight).reshape(items, 6, D)
    rw_t = router_weight.T
    rwt_pad = jnp.pad(jnp.concatenate([rw_t, rw_t], 0), ((0, LANES - 2 * EXPERTS), (0, 0)))

    qkv, lse, attn, rows = attn_forward(lengths, tokens, cotangent, mod, qkv_weight, out_weight)
    if fast:
        peer_rows = swap(rows, "expert", 1)
    info, line, pos = route(local, lengths, rows, rw_t, routes.T)
    sent, received = [], []
    rows_now = rows
    for j in range(local):
        sent.append(dispatch(j, local, rows_now, cotangent, mod, line, pos))
        rows_now = after(rows, sent[j])
    sres, gsh, s_act, *s_gpre = shared_main(fast, where, rows_now, shared_in, shared_out)
    if fast:
        peer_act = swap(s_act, "expert", 1)
        peer_gpre = swap(s_gpre[1], "expert", 1)
    for j in range(local):
        part = after(sent[j], sres) if j else sent[j]
        received.append(lax.all_to_all(part, "expert", 0, 0, tiled=True))
    expert_stages = [("batch", 1), ("batch", 2), ("batch", 4)]
    dense_stages = [("expert", 2), ("batch", 1), ("batch", 2), ("batch", 4)]
    back, expert_grads, chains = [], [], []
    last = (sres,)
    for j in range(local):
        rows_in = after(received[j], *last)
        act_e, slope_e, d2 = expert_first(fast, y_at, rows_in, expert_in, j)
        waits = [d2[0], *back]
        if fast:
            chains.append(Chain(*d2, expert_stages))
            if j == 1:
                chains[0].step(take_after=d2[:1])
                waits.append(chains[0].send)
        rows_in = after(rows_in, *waits)
        y, gpre_e = expert_second(rows_in, act_e, slope_e, expert_in, expert_out, j)
        back.append(lax.all_to_all(y, "expert", 0, 0, tiled=True))
        d1 = weight_grad(fast, y_at, after(rows_in, y), 0, gpre_e)
        last = (d1[0],)
        if fast:
            chains.append(Chain(*d1, expert_stages))
        expert_grads.append((d1, d2))
    if fast:
        out0, in0, out1, in1 = chains
        now = last
        out0.step(take_after=now)
        in0.step(take_after=now)
        rows_now = after(rows, *last, out0.send, in0.send)
        shared_grads = shared_grad(where, rows_now, peer_rows, s_gpre[0], peer_gpre, s_act, peer_act)
        shared_sum = Chain(*shared_grads, dense_stages)
    else:
        rows_now = after(rows, *last)
        shared_grads = (
            weight_grad(fast, y_at, rows_now, H_MLP, s_gpre[0])[0],
            weight_grad(fast, y_at, rows_now, G_SHARED, s_act)[0],
        )
    pieces = [items // 2, items - items // 2]
    tok = after(tokens, shared_grads[0])
    outs, own, other = [], [], []
    done = 0
    for piece, per in enumerate(pieces):
        outs, first, *second = backward(
            fast, where, done, per, outs, lengths, tok, cotangent, mod, attn, qkv, lse,
            sres, gsh, info, back, qkv_weight, out_weight, rwt_pad,
        )
        done += per
        own.append(first)
        now = (outs[0],)
        tok = after(tokens, *now)
        if fast:
            other.append(swap(second[0], "expert", 1))
            if piece == 0:
                out0.step(take_after=now)
                in0.step(take_after=now)
                out1.step(take_after=now)
                tok = after(tok, out0.terms[-1], in0.send, out1.send)
            else:
                in1.step(take_after=now)
                in0.step(take_after=now)
                out1.step(take_after=now)
                shared_sum.step(take_after=now)
                where_now = after(where, in0.got, out1.got, in1.send, shared_sum.got)
    result, grad_tokens, grad_mod = outs
    stacks = [rows, peer_rows] if fast else [rows]
    if not fast:
        where_now = where
    tail = tail_grad(fast, where_now, stacks, own + other)

    cols, ada_rows = 6 * D // ne, D // nb
    width = ada_rows + -ada_rows % LANES
    each = ada_rows * EXPERTS // ne // items

    def exchange(*others):
        mod_parts = after(grad_mod, *others)[:, :6].reshape(items, ne, cols).astype(BF16)
        mod_parts = jnp.transpose(mod_parts, (1, 0, 2))
        act_parts = jnp.transpose(act.reshape(items, nb, ada_rows), (1, 0, 2))
        act_parts = jnp.pad(act_parts, ((0, 0), (0, 0), (0, -ada_rows % LANES)))
        pieces = [
            jnp.broadcast_to(mod_parts[None], (nb, ne, items, cols)),
            jnp.broadcast_to(act_parts[:, None], (nb, ne, items, width)),
        ]
        if fast:
            mine = after(tail[2], *others)[:, :EXPERTS].reshape(nb, ada_rows, ne, EXPERTS // ne)
            mine = jnp.transpose(mine, (0, 2, 1, 3)).reshape(nb, ne, items, each)
            pieces.append(jnp.pad(mine, ((0, 0), (0, 0), (0, 0), (0, -each % LANES))))
        parts = jnp.concatenate(pieces, -1)
        return all_pairs(parts)

    if not fast:
        got = exchange()

    if fast:
        def unfold(v):
            return v.reshape(96, 8, 384).transpose(2, 1, 0).reshape(384, D)

        tail_sum = Chain(*tail[:2], dense_stages)
        token = tail[0]
        for chain in (
            out1, in1, shared_sum, tail_sum, shared_sum, in1, tail_sum, tail_sum, shared_sum,
            tail_sum,
        ):
            chain.step(take_after=(token,))
            token = chain.send if chain.stages else chain.terms[-1]
            if chain is shared_sum and len(chain.stages) == 2:
                got = exchange(token)
            if chain is tail_sum and len(chain.stages) == 1:
                late = token
        tl = tail_sum.total()
        got = after(got, late)
        assert not any(c.stages for c in (in0, in1, out0, out1, shared_sum, tail_sum))
        sh = shared_sum.total()
        g_sh1 = sh[0]
        g_sh2 = sh[1].reshape(96, 2, 384).transpose(2, 1, 0).reshape(384, 192)
        g_e1 = jnp.stack([in0.total(), in1.total()])
        g_e2 = jnp.stack([unfold(out0.total()), unfold(out1.total())])
        g_qkv = tl[:, :576]
        g_out = tl[:, 576:768]
        rt = got[..., cols + width : cols + width + each].astype(F32)
        g_rt = jnp.sum(rt.reshape(nb * ne, ada_rows, EXPERTS // ne), 0)
    else:
        def flipped(grad):
            r, c = grad.shape
            return jnp.transpose(reduce_dense_t(grad))

        def reduce_dense_t(grad):
            r, c = grad.shape
            v = reduce_expert(grad.reshape(ne, r // ne, c))
            v = jnp.transpose(v.reshape(r // ne, nb, c // nb), (1, 0, 2))
            return reduce_batch(v)

        g_sh1 = reduce_dense(shared_grads[0])
        g_sh2 = flipped(shared_grads[1])
        g_e1 = jnp.stack([reduce_local(g[0][0]) for g in expert_grads])
        g_e2 = jnp.stack([
            jnp.transpose(reduce_batch(jnp.transpose(g[1][0].reshape(D, nb, FF // nb), (1, 0, 2))))
            for g in expert_grads
        ])
        g_qkv = reduce_dense(tail[0])
        g_out = reduce_dense(tail[1])
        g_rt = reduce_dense(tail[2][:, :EXPERTS])
    got = got.reshape(nb * ne * items, -1).astype(F32)
    grad_ada = jnp.dot(
        got[:, cols : cols + ada_rows].T, got[:, :cols], precision=lax.Precision.HIGHEST
    )
    return (
        result, grad_tokens, grad_ada, g_qkv, g_out, g_rt, g_sh1, g_sh2, g_e1, g_e2
    )


def solution(mesh):
    placed = (
        P(("batch", "expert"), None),
        P(("batch", "expert"), None),
        P(("batch", "expert")),
        P(("batch", "expert"), None),
        P(("batch", "expert"), None),
        P(),
        P(),
        P(),
        P(),
        P(),
        P(),
        P("expert", None, None),
        P("expert", None, None),
    )
    return jax.shard_map(
        per_device,
        mesh=mesh,
        in_specs=placed,
        out_specs=(
            P(("batch", "expert"), None),
            P(("batch", "expert"), None),
            P("batch", "expert"),
            P("batch", "expert"),
            P("batch", "expert"),
            P("batch", "expert"),
            P("batch", "expert"),
            P("batch", "expert"),
            P("expert", "batch", None),
            P("expert", "batch", None),
        ),
        check_vma=False,
    )
```

```python
import functools
import math

import jax
import jax.numpy as jnp
from jax import lax
from jax.experimental import pallas as pl
from jax.experimental.pallas import tpu as pltpu
from jax.sharding import PartitionSpec as P

D = 768
HEADS = 12
HEAD_DIM = 64
FF = 3072
EXPERTS = 8
SEQ = 256
CAP = 256
LANES = 128
PAIRS = HEADS // 2
H_MLP, G_SHARED, H_ATTN, HEADS_OUT = range(4)

GELU_C = 0.7978845608028654
GELU_A = 0.044715
EPSILON = 1e-06
MASKED = -1000000000.0
LOG2E = math.log2(math.e)
SCALE = HEAD_DIM ** (-0.5)

F32 = jnp.float32
BF16 = jnp.bfloat16
VMEM_LIMIT = 60 * 1024 * 1024
COST = 0.75


def dot_nn(a, b):
    return jnp.dot(a, b, preferred_element_type=F32)


def dot_nt(a, b):
    return lax.dot_general(a, b, (((1,), (1,)), ((), ())), preferred_element_type=F32)


def dot_tn(a, b):
    return lax.dot_general(a, b, (((0,), (0,)), ((), ())), preferred_element_type=F32)


def normalize(values):
    centre = values - jnp.mean(values, -1, keepdims=True)
    factor = lax.rsqrt(jnp.mean(centre * centre, -1, keepdims=True) + EPSILON)
    return (centre * factor, factor)


def norm_back(grad_norm, normed, factor):
    return factor * (
        grad_norm
        - jnp.mean(grad_norm, -1, keepdims=True)
        - normed * jnp.mean(grad_norm * normed, -1, keepdims=True)
    )


def half_masks():
    lane = lax.broadcasted_iota(jnp.int32, (1, LANES), 1)
    low = jnp.where(lane < HEAD_DIM, 1.0, 0.0).astype(BF16)
    return (low, (1.0 - low).astype(BF16))


def whole(shape):
    return pl.BlockSpec(shape, lambda *_: (0,) * len(shape))


def kind_of(which, t):
    return pl.BlockSpec((1, t, D), lambda *_: (which, 0, 0), pipeline_mode=pl.Buffered(1))


def once(shape):
    return pl.BlockSpec(shape, lambda *_: (0,) * len(shape), pipeline_mode=pl.Buffered(1))


ANY = pl.BlockSpec(memory_space=pl.ANY)


class Fetch:
    def __init__(self, pairs, sems):
        self.step = pl.program_id(0)
        self.copies = [
            pltpu.make_async_copy(src, dst, sems.at[i]) for i, (src, dst) in enumerate(pairs)
        ]

        @pl.when(self.step == 0)
        def _():
            for copy in self.copies:
                copy.start()

    def need(self, *which):
        @pl.when(self.step == 0)
        def _():
            for i in which:
                self.copies[i].wait()


def cost(flops, moved):
    return pl.CostEstimate(
        flops=int(COST * flops), bytes_accessed=int(COST * moved), transcendentals=0
    )


def params(**more):
    return pltpu.CompilerParams(vmem_limit_bytes=VMEM_LIMIT, **more)


def attn_forward_kernel(
    len_ref, tok_ref, cot_ref, mod_ref, wqkv_ref, wout_ref,
    qkv_ref, lse_ref, attn_ref, rows_ref,
):
    item = pl.program_id(0)
    mod = mod_ref[0]
    x = tok_ref[...].astype(F32)
    normed, _ = normalize(x)
    h = (normed * (1.0 + mod[1:2]) + mod[0:1]).astype(BF16)
    rows_ref[H_ATTN] = h
    qkv_ref[...] = dot_nn(h, wqkv_ref[...]).astype(BF16)
    key_live = lax.broadcasted_iota(jnp.int32, (1, SEQ), 1) < len_ref[item]
    masks = half_masks()
    lane = lax.broadcasted_iota(jnp.int32, (SEQ, LANES), 1)
    lse_all = jnp.zeros((SEQ, LANES), F32)
    for pair in range(PAIRS):
        at = LANES * pair
        q2 = qkv_ref[:, at : at + LANES]
        k2 = qkv_ref[:, D + at : D + at + LANES]
        v2 = qkv_ref[:, 2 * D + at : 2 * D + at + LANES]
        outs = []
        for half in range(2):
            s = dot_nt(q2 * masks[half], k2) * (SCALE * LOG2E)
            s = jnp.where(key_live, s, MASKED * LOG2E)
            peak = jnp.max(s, -1, keepdims=True)
            e = jnp.exp2(s - peak)
            total = jnp.sum(e, -1, keepdims=True)
            probs = (e * (1.0 / total)).astype(BF16)
            outs.append(dot_nn(probs, v2))
            lse = peak + jnp.log(total) * LOG2E
            lse_all = jnp.where(lane == 2 * pair + half, lse, lse_all)
        rows_ref[HEADS_OUT, :, at : at + LANES] = jnp.where(
            lane < HEAD_DIM, outs[0], outs[1]
        ).astype(BF16)
    lse_ref[...] = lse_all
    attn = dot_nn(rows_ref[HEADS_OUT], wout_ref[...])
    attn_ref[...] = attn
    x_mid = x + mod[2:3] * attn
    normed_mlp, _ = normalize(x_mid)
    rows_ref[H_MLP] = (normed_mlp * (1.0 + mod[4:5]) + mod[3:4]).astype(BF16)
    rows_ref[G_SHARED] = (mod[5:6] * cot_ref[...].astype(F32)).astype(BF16)


def attn_forward(lengths, tokens, cot, mod, wqkv, wout):
    t = tokens.shape[0]
    items = t // SEQ
    row = lambda w: pl.BlockSpec((SEQ, w), lambda i, _: (i, 0))
    return pl.pallas_call(
        attn_forward_kernel,
        name="attn_forward",
        grid_spec=pltpu.PrefetchScalarGridSpec(
            num_scalar_prefetch=1,
            grid=(items,),
            in_specs=[
                row(D), row(D), pl.BlockSpec((1, 6, D), lambda i, _: (i, 0, 0)),
                once((D, 3 * D)), once((D, D)),
            ],
            out_specs=[
                row(3 * D), row(LANES), row(D), pl.BlockSpec((4, SEQ, D), lambda i, _: (0, i, 0)),
            ],
        ),
        out_shape=[
            jax.ShapeDtypeStruct((t, 3 * D), BF16),
            jax.ShapeDtypeStruct((t, LANES), F32),
            jax.ShapeDtypeStruct((t, D), F32),
            jax.ShapeDtypeStruct((4, t, D), BF16),
        ],
        compiler_params=params(),
        cost_estimate=cost(int(8.1e9), int(24e6)),
    )(lengths, tokens, cot, mod, wqkv, wout)


def live_of(len_ref, items, shape, dim):
    tok = lax.broadcasted_iota(jnp.int32, shape, dim)
    limit = jnp.zeros(shape, jnp.int32)
    for i in range(items):
        limit = jnp.where(tok >= i * SEQ, i * SEQ + len_ref[i], limit)
    return tok < limit


def route_kernel(local, len_ref, h_ref, rw_ref, routes_ref, info_ref, line_ref, pos_ref):
    t = h_ref.shape[1]
    items = t // SEQ
    r0, r1 = routes_ref[0:1, :], routes_ref[1:2, :]
    expert = lax.broadcasted_iota(jnp.int32, (EXPERTS, t), 0)
    is0, is1 = expert == r0, expert == r1
    live = live_of(len_ref, items, (1, t), 1)
    hot = (is0 | is1) & live
    before = (
        lax.broadcasted_iota(jnp.int32, (t, t), 1) < lax.broadcasted_iota(jnp.int32, (t, t), 0)
    )
    tri = jnp.where(before, 1.0, 0.0).astype(BF16)
    count = dot_nt(jnp.where(hot, 1.0, 0.0).astype(BF16), tri)
    pos_ref[...] = jnp.where(hot, count, -1.0)
    pick = lambda where, v: jnp.sum(jnp.where(where, v, 0.0), 0, keepdims=True)
    p0, p1 = pick(is0, count), pick(is1, count)
    groups = EXPERTS // local
    block0 = (r0 % local) * groups + r0 // local
    block1 = (r1 % local) * groups + r1 // local
    slot0 = jnp.where(live & (p0 < CAP), block0.astype(F32) * CAP + p0, -1.0)
    slot1 = jnp.where(live & (p1 < CAP), block1.astype(F32) * CAP + p1, -1.0)
    logits = dot_nt(rw_ref[...], h_ref[0])
    l0, l1 = pick(is0, logits), pick(is1, logits)
    top = jnp.maximum(l0, l1)
    e0 = jnp.exp(l0 - top)
    e1 = jnp.exp(l1 - top)
    total = e0 + e1
    line = jnp.zeros((8, t), F32)
    for k, value in enumerate(
        (e0 / total, e1 / total, slot0, slot1, r0.astype(F32), r1.astype(F32))
    ):
        line = jnp.where(expert == k, value, line)
    line_ref[...] = line
    info_ref[:, 0:8] = line.T


def route(local, lengths, rows, rw_t, routes_t):
    t = rows.shape[1]
    return pl.pallas_call(
        functools.partial(route_kernel, local),
        name="route",
        grid=(1,),
        in_specs=[
            pl.BlockSpec(memory_space=pltpu.SMEM), kind_of(H_MLP, t), whole(rw_t.shape),
            whole(routes_t.shape),
        ],
        out_specs=[whole((t, LANES)), whole((8, t)), whole((EXPERTS, t))],
        out_shape=[
            jax.ShapeDtypeStruct((t, LANES), F32),
            jax.ShapeDtypeStruct((8, t), F32),
            jax.ShapeDtypeStruct((EXPERTS, t), F32),
        ],
        compiler_params=params(),
        cost_estimate=cost(int(1e9), int(3e6)),
    )(lengths, rows, rw_t, routes_t)


def dispatch_kernel(local, first, h_ref, cot_ref, mod_ref, line_ref, pos_ref, out_ref):
    t = h_ref.shape[1]
    items = t // SEQ
    expert = pl.program_id(0) * local + first
    pos = pos_ref[pl.ds(expert, 1), :]
    slot = lax.broadcasted_iota(jnp.int32, (CAP, t), 0).astype(F32)
    hot = jnp.where(slot == pos, 1.0, 0.0).astype(BF16)
    out_ref[0, 0] = dot_nn(hot, h_ref[0]).astype(BF16)
    name = expert.astype(F32)
    weight = jnp.where(
        line_ref[4:5] == name, line_ref[0:1], jnp.where(line_ref[5:6] == name, line_ref[1:2], 0.0)
    )
    high = weight.astype(BF16).astype(F32)
    middle = (weight - high).astype(BF16).astype(F32)
    item = (lax.broadcasted_iota(jnp.int32, (1, t), 1) // SEQ).astype(F32)
    lane = lax.broadcasted_iota(jnp.int32, (8, t), 0)
    table = jnp.zeros((8, t), F32)
    for k, value in enumerate((high, middle, weight - high - middle, item)):
        table = jnp.where(lane == k, value, table)
    values = dot_nt(hot, table.astype(BF16))
    weight_col = values[:, 0:1] + values[:, 1:2] + values[:, 2:3]
    item_col = values[:, 3:4]
    gate = jnp.broadcast_to(mod_ref[0, 5:6, :], (CAP, D))
    for i in range(1, items):
        gate = jnp.where(item_col == i, mod_ref[i, 5:6, :], gate)
    grad = gate * dot_nn(hot, cot_ref[...])
    out_ref[0, 1] = (weight_col * grad).astype(BF16)


def dispatch(first, local, rows, cot, mod, line, pos):
    t = rows.shape[1]
    groups = EXPERTS // local
    return pl.pallas_call(
        functools.partial(dispatch_kernel, local, first),
        name="dispatch",
        grid=(groups,),
        in_specs=[
            kind_of(H_MLP, t), once((t, D)), once(mod.shape), once((8, t)), once((EXPERTS, t)),
        ],
        out_specs=pl.BlockSpec((1, 2, CAP, D), lambda g: (g, 0, 0, 0)),
        out_shape=jax.ShapeDtypeStruct((groups, 2, CAP, D), BF16),
        compiler_params=params(),
        cost_estimate=cost(int(3.3e9), int(8e6)),
    )(rows, cot, mod, line, pos)


def gelu_pair(v):
    square = v * v
    gate = 0.5 * jnp.tanh(v * (GELU_C * GELU_A * square + GELU_C)) + 0.5
    act = v * gate
    slope = gate + act * (1.0 - gate) * (6.0 * GELU_C * GELU_A * square + 2.0 * GELU_C)
    return act, slope


def shared_main_kernel(halved, where_ref, x_ref, g_ref, w1_ref, w2_ref, *rest):
    y_ref, gx_ref, act_ref, *gpre_refs, gpre_ref = rest
    x, g = x_ref[0], g_ref[0]
    for f in range(4):
        cols = slice(f * (FF // 4), (f + 1) * (FF // 4))
        act, slope = gelu_pair(dot_nn(x, w1_ref[:, cols]))
        act_ref[:, cols] = act.astype(BF16)
        gpre_ref[:, cols] = (dot_nt(g, w2_ref[cols, :]) * slope).astype(BF16)
    y_ref[...] = dot_nn(act_ref[...], w2_ref[...])
    gx_ref[...] = dot_nt(gpre_ref[...], w1_ref[...])
    if halved:
        first = where_ref[0] == 0
        width = FF // 4
        for x_at in range(2):
            low = gpre_ref[:, 2 * x_at * width : (2 * x_at + 1) * width]
            high = gpre_ref[:, (2 * x_at + 1) * width : (2 * x_at + 2) * width]
            cols = slice(x_at * width, (x_at + 1) * width)
            gpre_refs[0][:, cols] = jnp.where(first, low, high)
            gpre_refs[1][:, cols] = jnp.where(first, high, low)


def shared_main(halved, where, rows, w1, w2):
    t = rows.shape[1]
    chunk = lambda w: pl.BlockSpec((SEQ, w), lambda s, m: (s, 0))
    kind = lambda k: pl.BlockSpec((1, SEQ, D), lambda s, m: (k, s, 0))
    widths = [FF // 2] * 2 if halved else [FF]
    return pl.pallas_call(
        functools.partial(shared_main_kernel, halved),
        name="shared_main",
        grid_spec=pltpu.PrefetchScalarGridSpec(
            num_scalar_prefetch=1,
            grid=(t // SEQ,),
            in_specs=[kind(H_MLP), kind(G_SHARED), once((D, FF)), once((FF, D))],
            out_specs=[chunk(D), chunk(D), chunk(FF)] + [chunk(w) for w in widths],
            scratch_shapes=[pltpu.VMEM((SEQ, FF), BF16)] if halved else [],
        ),
        out_shape=[jax.ShapeDtypeStruct((t, D), F32)] * 2
        + [jax.ShapeDtypeStruct((t, FF), BF16)]
        + [jax.ShapeDtypeStruct((t, w), BF16) for w in widths],
        compiler_params=params(),
        cost_estimate=cost(8 * t * D * FF, int(30e6)),
    )(where, rows, rows, w1, w2)


def store_out_grad(where_ref, part, keep_ref, send_ref):
    first = where_ref[0] == 0
    low, high = part[:, :384], part[:, 384:]
    mine = jnp.where(first, low, high)
    other = jnp.where(first, high, low)
    for k in range(8):
        cols = slice(k * 384, k * 384 + 384)
        keep_ref[0, 0, :, cols] = mine[k * 96 : k * 96 + 96]
        send_ref[0, 0, :, cols] = other[k * 96 : k * 96 + 96]


def expert_first_kernel(fast, where_ref, rows_ref, w1_ref, act_ref, slope_ref, *outs):
    x = rows_ref[:, 0].reshape(-1, D)
    g = rows_ref[:, 1].reshape(-1, D)
    act, slope = gelu_pair(dot_nn(x, w1_ref[0]))
    act = act.astype(BF16)
    act_ref[...] = act
    slope_ref[...] = slope
    part = dot_tn(g, act).astype(BF16)
    if fast:
        store_out_grad(where_ref, part, *outs)
    else:
        outs[0][...] = part


def expert_first(fast, where, rows, w1, which):
    count = rows.shape[0] * CAP
    tile = FF // 4 if fast else FF // 8
    tile_of = lambda s, m: ((s % 2) ^ m[2]) * 2 + ((s // 2) ^ m[1]) if fast else s
    col = pl.BlockSpec((count, tile), lambda s, m: (0, tile_of(s, m)))
    if fast:
        grads = [jax.ShapeDtypeStruct((2, 2, 96, FF), BF16)] * 2
        specs = [pl.BlockSpec((1, 1, 96, FF), lambda s, m: (s // 2, s % 2, 0, 0))] * 2
    else:
        grads = [jax.ShapeDtypeStruct((D, FF), BF16)]
        specs = [pl.BlockSpec((D, tile), lambda s, m: (0, s))]
    act, slope, *grads = pl.pallas_call(
        functools.partial(expert_first_kernel, fast),
        name="expert_first",
        grid_spec=pltpu.PrefetchScalarGridSpec(
            num_scalar_prefetch=1,
            grid=(FF // tile,),
            in_specs=[
                once(rows.shape), pl.BlockSpec((1, D, tile), lambda s, m: (which, 0, tile_of(s, m))),
            ],
            out_specs=[col, col] + specs,
        ),
        out_shape=[
            jax.ShapeDtypeStruct((count, FF), BF16), jax.ShapeDtypeStruct((count, FF), F32),
        ] + grads,
        compiler_params=params(),
        cost_estimate=cost(4 * count * D * FF, int(30e6)),
    )(where, rows, w1)
    return act, slope, grads


def expert_second_kernel(rows_ref, act_ref, slope_ref, w1_ref, w2_ref, out_ref, gpre_ref):
    g = rows_ref[0, 1]
    for f in range(4):
        cols = slice(f * (FF // 4), (f + 1) * (FF // 4))
        gpre_ref[:, cols] = (dot_nt(g, w2_ref[0, cols, :]) * slope_ref[:, cols]).astype(BF16)
    out_ref[0, 0] = dot_nn(act_ref[...], w2_ref[0]).astype(BF16)
    out_ref[0, 1] = dot_nt(gpre_ref[...], w1_ref[0]).astype(BF16)


def expert_second(rows, act, slope, w1, w2, which):
    count = rows.shape[0] * CAP
    chunk = lambda w: pl.BlockSpec((CAP, w), lambda s: (s, 0))
    pair = pl.BlockSpec((1, 2, CAP, D), lambda s: (s, 0, 0, 0))
    weight = lambda r, c: pl.BlockSpec(
        (1, r, c), lambda s: (which, 0, 0), pipeline_mode=pl.Buffered(1)
    )
    return pl.pallas_call(
        expert_second_kernel,
        name="expert_second",
        grid=(rows.shape[0],),
        in_specs=[pair, chunk(FF), chunk(FF), weight(D, FF), weight(FF, D)],
        out_specs=[pair, chunk(FF)],
        out_shape=[
            jax.ShapeDtypeStruct(rows.shape, BF16), jax.ShapeDtypeStruct((count, FF), BF16),
        ],
        compiler_params=params(),
        cost_estimate=cost(6 * count * D * FF, int(40e6)),
    )(rows, act, slope, w1, w2)


def weight_grad_kernel(fast, where_ref, a_ref, b_ref, *outs):
    part = dot_tn(a_ref[...].reshape(-1, D), b_ref[...]).astype(BF16)
    if not fast:
        outs[0][...] = part
        return
    first = where_ref[0] == 0
    keep_ref, send_ref = outs
    for z in range(4):
        low = part[192 * z : 192 * z + 96]
        high = part[192 * z + 96 : 192 * z + 192]
        at = (z % 2) ^ where_ref[1], (z // 2) ^ where_ref[2]
        keep_ref[at] = jnp.where(first, low, high)
        send_ref[at] = jnp.where(first, high, low)


def weight_grad(fast, where, a, kind, b):
    rows = b.shape[0]
    tile = FF // 4
    if a.ndim == 3:
        a_spec = kind_of(kind, rows)
    else:
        a_spec = pl.BlockSpec(
            (a.shape[0], 1, CAP, D), lambda s, m: (0, kind, 0, 0), pipeline_mode=pl.Buffered(1)
        )
    if fast:
        outs = [jax.ShapeDtypeStruct((2, 2, 96, FF), BF16)] * 2
        specs = [pl.BlockSpec((2, 2, 96, tile), lambda s, m: (0, 0, 0, s))] * 2
    else:
        outs = [jax.ShapeDtypeStruct((D, FF), BF16)]
        specs = [pl.BlockSpec((D, tile), lambda s, m: (0, s))]
    return pl.pallas_call(
        functools.partial(weight_grad_kernel, fast),
        name="weight_grad",
        grid_spec=pltpu.PrefetchScalarGridSpec(
            num_scalar_prefetch=1,
            grid=(FF // tile,),
            in_specs=[a_spec, pl.BlockSpec((rows, tile), lambda s, m: (0, s))],
            out_specs=specs,
        ),
        out_shape=outs,
        compiler_params=params(),
        cost_estimate=cost(2 * rows * D * FF, int(13e6)),
    )(where, a, b)


def batch_at(where_ref, b):
    z = b // 2
    return (b % 2) ^ where_ref[2], (z % 2) ^ where_ref[3], (z // 2) ^ where_ref[4]


def own_columns(where_ref, v, width):
    low = jnp.concatenate([v[:, :width], v[:, 2 * width : 3 * width]], 1)
    high = jnp.concatenate([v[:, width : 2 * width], v[:, 3 * width :]], 1)
    return jnp.where(where_ref[0] == 0, low, high)


def shared_grad_kernel(
    where_ref, mine_ref, peer_ref, gpre_ref, gpre_peer_ref, act_ref, act_peer_ref,
    keep_ref, send_ref, g_scr, part_scr,
):
    step = pl.program_id(0)
    side = step // 2
    rows = act_ref.shape[0]

    @pl.when(step == 0)
    def _():
        g_scr[:rows] = own_columns(where_ref, mine_ref[G_SHARED], D // 4)
        g_scr[rows:] = own_columns(where_ref, peer_ref[G_SHARED], D // 4)

    @pl.when(step % 2 == 0)
    def _():
        part = (
            dot_tn(mine_ref[H_MLP], gpre_ref[...]) + dot_tn(peer_ref[H_MLP], gpre_peer_ref[...])
        ).astype(BF16)
        for b in range(8):
            part_scr[batch_at(where_ref, b)] = part[b * 96 : b * 96 + 96]
        for s, ref in ((0, keep_ref), (1, send_ref)):
            @pl.when(side == s)
            def _():
                ref[:, :, :, 0] = part_scr[...]

    both = (dot_tn(g_scr[:rows], act_ref[...]) + dot_tn(g_scr[rows:], act_peer_ref[...])).astype(BF16)
    first = where_ref[1] == 0
    low, high = both[:192], both[192:]
    for ref, v in ((keep_ref, jnp.where(first, low, high)), (send_ref, jnp.where(first, high, low))):
        for h in range(2):
            for y in range(2):
                at = batch_at(where_ref, 2 * step + y)
                ref[(*at, 1, slice(None), slice(h * 384, h * 384 + 384))] = v[
                    h * 96 : h * 96 + 96, y * 384 : y * 384 + 384
                ]


def shared_grad(where, mine, peer, gpre, gpre_peer, act, act_peer):
    rows = act.shape[0]
    gpre_spec = pl.BlockSpec((rows, FF // 4), lambda s, m: (0, (s // 2) ^ m[1]))
    act_spec = pl.BlockSpec((rows, FF // 4), lambda s, m: (0, s))
    stack = pl.BlockSpec((2, rows, D), lambda s, m: (0, 0, 0), pipeline_mode=pl.Buffered(1))
    shape = (2, 2, 2, 2, 96, D)
    return pl.pallas_call(
        shared_grad_kernel,
        name="shared_grad",
        grid_spec=pltpu.PrefetchScalarGridSpec(
            num_scalar_prefetch=1,
            grid=(4,),
            in_specs=[stack, stack, gpre_spec, gpre_spec, act_spec, act_spec],
            out_specs=[once(shape)] * 2,
            scratch_shapes=[
                pltpu.VMEM((2 * rows, D // 2), BF16), pltpu.VMEM((2, 2, 2, 96, D), BF16),
            ],
        ),
        out_shape=[jax.ShapeDtypeStruct(shape, BF16)] * 2,
        compiler_params=params(),
        cost_estimate=cost(4 * rows * D * FF, int(25e6)),
    )(where, mine, peer, gpre, gpre_peer, act, act_peer)


def backward_kernel(
    local, fast, first_item, len_ref, where_ref, tok_ref, cot_ref, mod_ref, attn_ref, qkv_ref, lse_ref,
    sres_ref, gsh_ref, info_ref, wqkv_ref, wout_ref, rwt_ref, *rest,
):
    back = rest[:local]
    if fast:
        out_ref, gtok_ref, gmod_ref, own_ref, other_ref, gq_ref = rest[-6:]
    else:
        out_ref, gtok_ref, gmod_ref, own_ref, gq_ref = rest[-5:]
    item = pl.program_id(0) + first_item
    slots = EXPERTS * CAP
    each = slots // local

    def pick(hot, kind):
        value = None
        for j in range(local):
            rows = back[j][:, kind].reshape(each, D)
            term = dot_nn(hot[:, j * each : (j + 1) * each], rows)
            value = term if value is None else value + term
        return value

    mod = mod_ref[0]
    x = tok_ref[...].astype(F32)
    cot = cot_ref[...].astype(F32)
    attn = attn_ref[...]
    x_mid = x + mod[2:3] * attn
    normed_mlp, factor_mlp = normalize(x_mid)
    gw0, gw1 = info_ref[:, 0:1], info_ref[:, 1:2]
    slot = lax.broadcasted_iota(jnp.int32, (SEQ, slots), 1).astype(F32)
    hot0 = jnp.where(slot == info_ref[:, 2:3], 1.0, 0.0).astype(BF16)
    hot1 = jnp.where(slot == info_ref[:, 3:4], 1.0, 0.0).astype(BF16)
    row0 = pick(hot0, 0)
    row1 = pick(hot1, 0)
    mlp_out = sres_ref[...] + (gw0 * row0 + gw1 * row1)
    out_ref[...] = (x_mid + mod[5:6] * mlp_out).astype(BF16)
    gmod_ref[0, 5:6, :] = jnp.sum(cot * mlp_out, 0, keepdims=True)
    grad_mlp = mod[5:6] * cot
    gate0 = jnp.sum(grad_mlp * row0, -1, keepdims=True)
    gate1 = jnp.sum(grad_mlp * row1, -1, keepdims=True)
    weighted = gw0 * gate0 + gw1 * gate1
    sel0 = gw0 * (gate0 - weighted)
    sel1 = gw1 * (gate1 - weighted)
    high0 = sel0.astype(BF16).astype(F32)
    high1 = sel1.astype(BF16).astype(F32)
    lane = lax.broadcasted_iota(jnp.int32, (SEQ, LANES), 1)
    lane_f = lane.astype(F32)
    r0, r1 = info_ref[:, 4:5], info_ref[:, 5:6]
    g_logits = (
        jnp.where(lane_f == r0, high0, 0.0)
        + jnp.where(lane_f == r1, high1, 0.0)
        + jnp.where(lane_f == r0 + EXPERTS, sel0 - high0, 0.0)
        + jnp.where(lane_f == r1 + EXPERTS, sel1 - high1, 0.0)
    ).astype(BF16)
    grad_h = gsh_ref[...] + pick(hot0 + hot1, 1) + dot_nn(g_logits, rwt_ref[...])
    gmod_ref[0, 3:4, :] = jnp.sum(grad_h, 0, keepdims=True)
    gmod_ref[0, 4:5, :] = jnp.sum(grad_h * normed_mlp, 0, keepdims=True)
    grad_mid = cot + norm_back(grad_h * (1.0 + mod[4:5]), normed_mlp, factor_mlp)
    gmod_ref[0, 2:3, :] = jnp.sum(grad_mid * attn, 0, keepdims=True)
    g_attn = (mod[2:3] * grad_mid).astype(BF16)
    g_heads = dot_nt(g_attn, wout_ref[...]).astype(BF16)
    key_live = lax.broadcasted_iota(jnp.int32, (1, SEQ), 1) < len_ref[item]
    masks = half_masks()
    low_half = lane < HEAD_DIM
    for pair in range(PAIRS):
        at = LANES * pair
        q2 = qkv_ref[:, at : at + LANES]
        k2 = qkv_ref[:, D + at : D + at + LANES]
        v2 = qkv_ref[:, 2 * D + at : 2 * D + at + LANES]
        gh2 = g_heads[:, at : at + LANES]
        dq, dk, dv = [], [], []
        for half in range(2):
            head = 2 * pair + half
            s = dot_nt(q2 * masks[half], k2) * (SCALE * LOG2E)
            s = jnp.where(key_live, s, MASKED * LOG2E)
            probs = jnp.exp2(s - lse_ref[:, head : head + 1])
            g_probs = dot_nt(gh2 * masks[half], v2)
            spread = jnp.sum(probs * g_probs, -1, keepdims=True)
            g_scores = (probs * (g_probs - spread)).astype(BF16)
            dq.append(dot_nn(g_scores, k2))
            dk.append(dot_tn(g_scores, q2))
            dv.append(dot_tn(probs.astype(BF16), gh2))
        gq_ref[:, at : at + LANES] = (jnp.where(low_half, dq[0], dq[1]) * SCALE).astype(BF16)
        gq_ref[:, D + at : D + at + LANES] = (
            jnp.where(low_half, dk[0], dk[1]) * SCALE
        ).astype(BF16)
        gq_ref[:, 2 * D + at : 2 * D + at + LANES] = jnp.where(low_half, dv[0], dv[1]).astype(BF16)
    g_qkv = gq_ref[...]
    g_h = dot_nt(g_qkv, wqkv_ref[...])
    normed, factor = normalize(x)
    gmod_ref[0, 0:1, :] = jnp.sum(g_h, 0, keepdims=True)
    gmod_ref[0, 1:2, :] = jnp.sum(g_h * normed, 0, keepdims=True)
    gmod_ref[0, 6:8, :] = jnp.zeros((2, D), F32)
    gtok_ref[...] = grad_mid + norm_back(g_h * (1.0 + mod[1:2]), normed, factor)
    if fast:
        sides = [
            jnp.concatenate(
                [
                    g_qkv[:, 576 * c : 576 * c + 576],
                    g_qkv[:, 1152 + 576 * c : 1728 + 576 * c],
                    g_attn[:, 192 * c : 192 * c + 192],
                    g_attn[:, 384 + 192 * c : 576 + 192 * c],
                ], 1
            )
            for c in range(2)
        ]
        first = where_ref[0] == 0
        own_ref[:, : 2 * D] = jnp.where(first, sides[0], sides[1])
        own_ref[:, 2 * D :] = g_logits
        other_ref[:, : 2 * D] = jnp.where(first, sides[1], sides[0])
        other_ref[:, 2 * D :] = g_logits
    else:
        own_ref[:, : 3 * D] = g_qkv
        own_ref[:, 3 * D : 4 * D] = g_attn
        own_ref[:, 4 * D :] = g_logits


def backward(
    fast, where, first_item, count, so_far, lengths, tokens, cot, mod, attn, qkv, lse, sres, gsh,
    info, back, wqkv, wout, rwt,
):
    t = tokens.shape[0]
    row = lambda w: pl.BlockSpec((SEQ, w), lambda i, *_: (i + first_item, 0))
    new = lambda w: pl.BlockSpec((SEQ, w), lambda i, *_: (i, 0))
    local = len(back)
    item_block = lambda r: pl.BlockSpec((1, r, D), lambda i, *_: (i + first_item, 0, 0))
    known = 14 + local
    widths = [2 * D + LANES] * 2 if fast else [4 * D + LANES]
    outs = pl.pallas_call(
        functools.partial(backward_kernel, local, fast, first_item),
        name="backward",
        grid_spec=pltpu.PrefetchScalarGridSpec(
            num_scalar_prefetch=2,
            grid=(count,),
            in_specs=[
                row(D), row(D), item_block(6),
                row(D), row(3 * D), row(LANES), row(D), row(D), row(LANES),
                once((D, 3 * D)), once((D, D)), once((LANES, D)),
            ] + [once(b.shape) for b in back]
            + [pl.BlockSpec(memory_space=pl.ANY)] * len(so_far),
            out_specs=[row(D), row(D), item_block(8)] + [new(w) for w in widths],
            scratch_shapes=[
                pltpu.VMEM((SEQ, 3 * D), BF16),
            ],
        ),
        out_shape=[
            jax.ShapeDtypeStruct((t, D), BF16),
            jax.ShapeDtypeStruct((t, D), F32),
            jax.ShapeDtypeStruct((t // SEQ, 8, D), F32),
        ] + [jax.ShapeDtypeStruct((count * SEQ, w), BF16) for w in widths],
        input_output_aliases={known + i: i for i in range(len(so_far))},
        compiler_params=params(),
        cost_estimate=cost(int(5e9) * count, int(7e6) * count),
    )(
        lengths, where, tokens, cot, mod, attn, qkv, lse, sres, gsh, info, wqkv, wout, rwt,
        *back, *so_far,
    )
    return (outs[:3], *outs[3:])


def tail_grad_kernel(fast, many, where_ref, *refs):
    count = 3
    *refs, stack_ref, grad_ref, sems = refs
    stacks, grads, outs = refs[:many], refs[many:-count], refs[-count:]
    width = 3 * D // 2 if fast else 3 * D
    each = len(grads) // many
    t = stacks[0].shape[1]
    pairs = []
    for i, stack in enumerate(stacks):
        start = i * t
        pairs.append((stack.at[G_SHARED + 1 :], stack_ref.at[i, : 4 - G_SHARED - 1]))
        pairs.append((stack.at[H_MLP], stack_ref.at[i, 2]))
        for g in grads[i * each : (i + 1) * each]:
            pairs.append((g, grad_ref.at[pl.ds(start, g.shape[0])]))
            start += g.shape[0]
    fetch = Fetch(pairs, sems)
    d_qkv = d_out = d_router = None
    for i in range(many):
        fetch.need(*range((2 + each) * i, (2 + each) * (i + 1)))
        rows = slice(i * t, (i + 1) * t)
        terms = (
            dot_tn(stack_ref[i, 0], grad_ref[rows, :width]),
            dot_tn(stack_ref[i, 1], grad_ref[rows, width : width + width // 3]),
            dot_tn(stack_ref[i, 2], grad_ref[rows, width + width // 3 :]),
        )
        if i:
            terms = (d_qkv + terms[0], d_out + terms[1], d_router)
        d_qkv, d_out, d_router = terms
    d_qkv, d_out = d_qkv.astype(BF16), d_out.astype(BF16)
    d_router = (d_router + pltpu.roll(d_router, LANES - EXPERTS, 1)).astype(BF16)
    if not fast:
        outs[0][...], outs[1][...], outs[2][...] = d_qkv, d_out, d_router
        return
    outs[2][...] = d_router
    first = where_ref[1] == 0
    low, high = [
        jnp.concatenate(
            [d_qkv[:, 576 * x : 576 * x + 576], d_out[:, 192 * x : 192 * x + 192]], 1
        )
        for x in range(2)
    ]
    for ref, v in ((outs[0], jnp.where(first, low, high)), (outs[1], jnp.where(first, high, low))):
        for b in range(8):
            ref[batch_at(where_ref, b)] = v[b * 96 : b * 96 + 96]


def tail_grad(fast, where, stacks, grads):
    if fast:
        outs = [jax.ShapeDtypeStruct((2, 2, 2, 96, D), BF16)] * 2
        outs.append(jax.ShapeDtypeStruct((D, LANES), BF16))
    else:
        outs = [
            jax.ShapeDtypeStruct((D, 3 * D), BF16),
            jax.ShapeDtypeStruct((D, D), BF16),
            jax.ShapeDtypeStruct((D, LANES), BF16),
        ]
    t, wide = stacks[0].shape[1], grads[0].shape[1]
    many = len(stacks)
    return pl.pallas_call(
        functools.partial(tail_grad_kernel, fast, len(stacks)),
        name="tail_grad",
        grid_spec=pltpu.PrefetchScalarGridSpec(
            num_scalar_prefetch=1,
            grid=(1,),
            in_specs=[ANY] * (len(stacks) + len(grads)),
            out_specs=[once(o.shape) for o in outs],
            scratch_shapes=[
                pltpu.VMEM((many, 3, t, D), BF16),
                pltpu.VMEM((many * t, wide), BF16),
                pltpu.SemaphoreType.DMA((2 * many + len(grads),)),
            ],
        ),
        out_shape=outs,
        compiler_params=params(),
        cost_estimate=cost(int(5e9), int(20e6)),
    )(where, *stacks, *grads)


def after(value, *others):
    if not others:
        return value
    return lax.optimization_barrier((value,) + tuple(others))[0]


def group_sum(blocks, axis, groups):
    width = len(groups[0])
    if width == 1:
        return blocks[0].astype(F32)
    low = blocks.astype(BF16)
    if width == 2:
        place = jnp.zeros((), jnp.int32)
        index = lax.axis_index(axis)
        for g in groups:
            place = jnp.where(index == g[1], 1, place)
        sent = lax.dynamic_index_in_dim(low, 1 - place, 0, keepdims=False)
        kept = lax.dynamic_index_in_dim(low, place, 0, keepdims=False)
        return pair_sum(kept, sent, axis, groups)
    got = lax.all_to_all(low, axis, 0, 0, tiled=True, axis_index_groups=groups)
    return jnp.sum(got.astype(F32), 0)


def pair_sum(kept, sent, axis, groups):
    pairs = [(g[0], g[1]) for g in groups] + [(g[1], g[0]) for g in groups]
    got = lax.ppermute(sent, axis, pairs)
    return kept.astype(F32) + got.astype(F32)


def swap(value, axis, bit):
    size = lax.axis_size(axis)
    return lax.ppermute(value.astype(BF16), axis, [(i, i ^ bit) for i in range(size)])


class Chain:
    def __init__(self, keep, send, stages):
        self.terms, self.send, self.stages = [keep], send, list(stages)

    def total(self):
        value = self.terms[0].astype(F32)
        for term in self.terms[1:]:
            value = value + term.astype(F32)
        return value

    def step(self, send_after=(), take_after=()):
        axis, bit = self.stages.pop(0)
        got = swap(after(self.send, *send_after), axis, bit)
        self.got = after(got, *take_after)
        self.terms.append(self.got)
        if self.stages:
            terms = self.terms
            self.terms = [v[1] for v in terms]
            self.send = self.total().astype(BF16)
            self.terms = [v[0] for v in terms]
        else:
            self.send = None
        return self


def inner_groups(outer, inner):
    return [[o * inner + i for i in range(inner)] for o in range(outer)]


def outer_groups(outer, inner):
    return [[o * inner + i for o in range(outer)] for i in range(inner)]


def batch_split(size):
    inner = 2 if size <= 8 else 8
    return (size // inner, inner)


def reduce_batch(blocks):
    outer, inner = batch_split(lax.axis_size("batch"))
    v = jnp.moveaxis(blocks.reshape((outer, inner) + blocks.shape[1:]), 1, 0)
    v = group_sum(v, "batch", inner_groups(outer, inner))
    return group_sum(v, "batch", outer_groups(outer, inner))


def reduce_expert(blocks):
    outer, inner = lax.axis_size("expert") // 2, 2
    v = jnp.moveaxis(blocks.reshape((outer, inner) + blocks.shape[1:]), 1, 0)
    v = group_sum(v, "expert", inner_groups(outer, inner))
    return group_sum(v, "expert", outer_groups(outer, inner))


def reduce_dense(grad):
    nb, ne = lax.axis_size("batch"), lax.axis_size("expert")
    r, c = grad.shape
    v = jnp.transpose(grad.reshape(r, ne, c // ne), (1, 0, 2))
    v = reduce_expert(v)
    return reduce_batch(v.reshape(nb, r // nb, c // ne))


def reduce_local(grad):
    nb = lax.axis_size("batch")
    r, c = grad.shape
    return reduce_batch(grad.reshape(nb, r // nb, c))


def all_pairs(parts):
    nb, ne = parts.shape[:2]
    return lax.all_to_all(
        parts.reshape((nb * ne,) + parts.shape[2:]), ("batch", "expert"), 0, 0, tiled=True
    )


def per_device(
    tokens, condition, lengths, routes, cotangent, ada_weight, qkv_weight, out_weight,
    router_weight, shared_in, shared_out, expert_in, expert_out,
):
    nb, ne = lax.axis_size("batch"), lax.axis_size("expert")
    local = expert_in.shape[0]
    items = lengths.shape[0]
    t = tokens.shape[0]
    fast = nb == 8 and ne == 4 and local == 2
    batch, expert = lax.axis_index("batch"), lax.axis_index("expert")
    z_at = batch // 2
    where = jnp.stack([expert % 2, expert // 2, batch % 2, z_at % 2, z_at // 2]).astype(jnp.int32)
    y_at = jnp.stack([batch % 2, z_at % 2, z_at // 2]).astype(jnp.int32)

    act = jax.nn.silu(condition.astype(F32)).astype(BF16)
    mod = dot_nn(act, ada_weight).reshape(items, 6, D)
    rw_t = router_weight.T
    rwt_pad = jnp.pad(jnp.concatenate([rw_t, rw_t], 0), ((0, LANES - 2 * EXPERTS), (0, 0)))

    qkv, lse, attn, rows = attn_forward(lengths, tokens, cotangent, mod, qkv_weight, out_weight)
    if fast:
        peer_rows = swap(rows, "expert", 1)
    info, line, pos = route(local, lengths, rows, rw_t, routes.T)
    sent, received = [], []
    rows_now = rows
    for j in range(local):
        sent.append(dispatch(j, local, rows_now, cotangent, mod, line, pos))
        rows_now = after(rows, sent[j])
    sres, gsh, s_act, *s_gpre = shared_main(fast, where, rows_now, shared_in, shared_out)
    if fast:
        peer_act = swap(s_act, "expert", 1)
        peer_gpre = swap(s_gpre[1], "expert", 1)
    for j in range(local):
        part = after(sent[j], sres) if j else sent[j]
        received.append(lax.all_to_all(part, "expert", 0, 0, tiled=True))
    expert_stages = [("batch", 1), ("batch", 2), ("batch", 4)]
    dense_stages = [("expert", 2), ("batch", 1), ("batch", 2), ("batch", 4)]
    back, expert_grads, chains = [], [], []
    last = (sres,)
    for j in range(local):
        rows_in = after(received[j], *last)
        act_e, slope_e, d2 = expert_first(fast, y_at, rows_in, expert_in, j)
        waits = [d2[0], *back]
        if fast:
            chains.append(Chain(*d2, expert_stages))
            if j == 1:
                chains[0].step(take_after=d2[:1])
                waits.append(chains[0].send)
        rows_in = after(rows_in, *waits)
        y, gpre_e = expert_second(rows_in, act_e, slope_e, expert_in, expert_out, j)
        back.append(lax.all_to_all(y, "expert", 0, 0, tiled=True))
        d1 = weight_grad(fast, y_at, after(rows_in, y), 0, gpre_e)
        last = (d1[0],)
        if fast:
            chains.append(Chain(*d1, expert_stages))
        expert_grads.append((d1, d2))
    if fast:
        out0, in0, out1, in1 = chains
        now = last
        out0.step(take_after=now)
        in0.step(take_after=now)
        rows_now = after(rows, *last, out0.send, in0.send)
        shared_grads = shared_grad(where, rows_now, peer_rows, s_gpre[0], peer_gpre, s_act, peer_act)
        shared_sum = Chain(*shared_grads, dense_stages)
    else:
        rows_now = after(rows, *last)
        shared_grads = (
            weight_grad(fast, y_at, rows_now, H_MLP, s_gpre[0])[0],
            weight_grad(fast, y_at, rows_now, G_SHARED, s_act)[0],
        )
    pieces = [items // 2, items - items // 2]
    tok = after(tokens, shared_grads[0])
    outs, own, other = [], [], []
    done = 0
    for piece, per in enumerate(pieces):
        outs, first, *second = backward(
            fast, where, done, per, outs, lengths, tok, cotangent, mod, attn, qkv, lse,
            sres, gsh, info, back, qkv_weight, out_weight, rwt_pad,
        )
        done += per
        own.append(first)
        now = (outs[0],)
        tok = after(tokens, *now)
        if fast:
            other.append(swap(second[0], "expert", 1))
            if piece == 0:
                out0.step(take_after=now)
                in0.step(take_after=now)
                out1.step(take_after=now)
                tok = after(tok, out0.terms[-1], in0.send, out1.send)
            else:
                in1.step(take_after=now)
                in0.step(take_after=now)
                out1.step(take_after=now)
                shared_sum.step(take_after=now)
                where_now = after(where, in0.got, out1.got, in1.send, shared_sum.got)
    result, grad_tokens, grad_mod = outs
    stacks = [rows, peer_rows] if fast else [rows]
    if not fast:
        where_now = where
    tail = tail_grad(fast, where_now, stacks, own + other)

    cols, ada_rows = 6 * D // ne, D // nb
    width = ada_rows + -ada_rows % LANES
    each = ada_rows * EXPERTS // ne // items

    def exchange(*others):
        mod_parts = after(grad_mod, *others)[:, :6].reshape(items, ne, cols).astype(BF16)
        mod_parts = jnp.transpose(mod_parts, (1, 0, 2))
        act_parts = jnp.transpose(act.reshape(items, nb, ada_rows), (1, 0, 2))
        act_parts = jnp.pad(act_parts, ((0, 0), (0, 0), (0, -ada_rows % LANES)))
        pieces = [
            jnp.broadcast_to(mod_parts[None], (nb, ne, items, cols)),
            jnp.broadcast_to(act_parts[:, None], (nb, ne, items, width)),
        ]
        if fast:
            mine = after(tail[2], *others)[:, :EXPERTS].reshape(nb, ada_rows, ne, EXPERTS // ne)
            mine = jnp.transpose(mine, (0, 2, 1, 3)).reshape(nb, ne, items, each)
            pieces.append(jnp.pad(mine, ((0, 0), (0, 0), (0, 0), (0, -each % LANES))))
        parts = jnp.concatenate(pieces, -1)
        return all_pairs(parts)

    if not fast:
        got = exchange()

    if fast:
        def unfold(v):
            return v.reshape(96, 8, 384).transpose(2, 1, 0).reshape(384, D)

        tail_sum = Chain(*tail[:2], dense_stages)
        token = tail[0]
        for chain in (
            out1, in1, shared_sum, tail_sum, shared_sum, in1, tail_sum, tail_sum, shared_sum,
            tail_sum,
        ):
            chain.step(take_after=(token,))
            token = chain.send if chain.stages else chain.terms[-1]
            if chain is shared_sum and len(chain.stages) == 2:
                got = exchange(token)
            if chain is tail_sum and len(chain.stages) == 1:
                late = token
        tl = tail_sum.total()
        got = after(got, late)
        assert not any(c.stages for c in (in0, in1, out0, out1, shared_sum, tail_sum))
        sh = shared_sum.total()
        g_sh1 = sh[0]
        g_sh2 = sh[1].reshape(96, 2, 384).transpose(2, 1, 0).reshape(384, 192)
        g_e1 = jnp.stack([in0.total(), in1.total()])
        g_e2 = jnp.stack([unfold(out0.total()), unfold(out1.total())])
        g_qkv = tl[:, :576]
        g_out = tl[:, 576:768]
        rt = got[..., cols + width : cols + width + each].astype(F32)
        g_rt = jnp.sum(rt.reshape(nb * ne, ada_rows, EXPERTS // ne), 0)
    else:
        def flipped(grad):
            r, c = grad.shape
            return jnp.transpose(reduce_dense_t(grad))

        def reduce_dense_t(grad):
            r, c = grad.shape
            v = reduce_expert(grad.reshape(ne, r // ne, c))
            v = jnp.transpose(v.reshape(r // ne, nb, c // nb), (1, 0, 2))
            return reduce_batch(v)

        g_sh1 = reduce_dense(shared_grads[0])
        g_sh2 = flipped(shared_grads[1])
        g_e1 = jnp.stack([reduce_local(g[0][0]) for g in expert_grads])
        g_e2 = jnp.stack([
            jnp.transpose(reduce_batch(jnp.transpose(g[1][0].reshape(D, nb, FF // nb), (1, 0, 2))))
            for g in expert_grads
        ])
        g_qkv = reduce_dense(tail[0])
        g_out = reduce_dense(tail[1])
        g_rt = reduce_dense(tail[2][:, :EXPERTS])
    got = got.reshape(nb * ne * items, -1).astype(F32)
    grad_ada = jnp.dot(
        got[:, cols : cols + ada_rows].T, got[:, :cols], precision=lax.Precision.HIGHEST
    )
    return (
        result, grad_tokens, grad_ada, g_qkv, g_out, g_rt, g_sh1, g_sh2, g_e1, g_e2
    )


def solution(mesh):
    placed = (
        P(("batch", "expert"), None),
        P(("batch", "expert"), None),
        P(("batch", "expert")),
        P(("batch", "expert"), None),
        P(("batch", "expert"), None),
        P(),
        P(),
        P(),
        P(),
        P(),
        P(),
        P("expert", None, None),
        P("expert", None, None),
    )
    return jax.shard_map(
        per_device,
        mesh=mesh,
        in_specs=placed,
        out_specs=(
            P(("batch", "expert"), None),
            P(("batch", "expert"), None),
            P("batch", "expert"),
            P("batch", "expert"),
            P("batch", "expert"),
            P("batch", "expert"),
            P("batch", "expert"),
            P("batch", "expert"),
            P("expert", "batch", None),
            P("expert", "batch", None),
        ),
        check_vma=False,
    )
```
